128 devices in a mesh: ctx: 4 (over y), head: 32 (over x, z, core).
Axes of the slice: x: 4, y: 4, z: 4, core: 2. Of those that a mesh axis runs over, the one named last changes fastest.
Arguments:
- queries: bfloat16 [16384, 4096], P('ctx', 'head'), may hold values from -6 to 6
- key_heads: bfloat16 [16384, 4096], P('ctx', 'head'), may hold values from -8 to 8
- value_heads: bfloat16 [16384, 4096], P('ctx', 'head'), may hold values from -120 to 120
- out_gain: bfloat16 [4096], P('head'), may hold values from 0.099609375 to 1.8984375
- out_weight: bfloat16 [4096, 2048], P('head'), may hold values from -0.09375 to 0.09375
- residual: bfloat16 [16384, 2048], P(('ctx', 'head')), may hold values from -36 to 36
- norm_gain: bfloat16 [2048], replicated, may hold values from 0.099609375 to 1.8984375
- routes: int32 [16384, 8], P(('ctx', 'head')), may hold values from 0 to 127, all different within a row; in each aligned block of 128 rows (0 to 127, 128 to 255, ...) at most 10 rows name the same one
- route_weights: float32 [16384, 8], P(('ctx', 'head')), may hold values from 0.02 to 0.4
- cotangent: bfloat16 [16384, 2048], P(('ctx', 'head')), may hold values from -6 to 6
- w_gate: bfloat16 [128, 2048, 768], P(('ctx', 'head')), may hold values from -0.125 to 0.125
- w_up: bfloat16 [128, 2048, 768], P(('ctx', 'head')), may hold values from -0.125 to 0.125
- w_down: bfloat16 [128, 768, 2048], P(('ctx', 'head')), may hold values from -0.21875 to 0.21875
Outputs:
- hidden_out: bfloat16 [16384, 2048], P(('ctx', 'head'))
- grad_gate: bfloat16 [128, 2048, 768], P(('ctx', 'head'))
- grad_up: bfloat16 [128, 2048, 768], P(('ctx', 'head'))
- grad_down: bfloat16 [128, 768, 2048], P(('ctx', 'head'))
The draws below stay inside these ranges and needn't reach their ends.
Inputs may be any that keep to these rules, and one draw needn't show every extreme that they name: `routes`: each row names 8 different experts. Within each aligned block of 128 rows no expert is named by more than 10 rows; in some blocks an expert is named by exactly 10 rows.
All inputs are finite; a program needn't handle non-finite values.
Results may differ from the reference program's by a relative error of at most 0.025.
Values may be sent and summed in bfloat16 or wider, within the bound.
No kernel may reach another device: no remote copies, remote signals or barrier semaphores. Data moves between devices by JAX's collectives and lax.ppermute only.
A program may use at most 192 MiB of HBM per device.

```python
import math
import jax
import jax.numpy as jnp
import numpy as np
from jax import lax

D = 2048
FF = 768
HEADS = 32
HD = 128
EXPERTS = 128
TOPK = 8
TOK_DEV = 128
CAP = 10
TOKENS = 16384
N_CTX = 4
N_HEAD = 32


def draw_key_heads(key, part):
    entry_key, jitter_key, slope_key, base_key = jax.random.split(key, 4)
    fraction = jnp.arange(TOKENS).astype(jnp.float32) / TOKENS - 0.5
    jitter = jax.random.uniform(jitter_key, (TOKENS, 1), jnp.float32, -0.75, 0.75)
    slope = jax.random.uniform(slope_key, (HEADS,), jnp.float32, -5.0, 5.0)
    base = jax.random.uniform(base_key, (HEADS,), jnp.float32, -1.0, 0.5)
    offset_heads = base[None, :] + slope[None, :] * fraction[:, None]
    offset = jnp.repeat(offset_heads, HD, axis=1)
    entries = jnp.clip(jax.random.normal(entry_key, (TOKENS, HEADS * HD), jnp.float32), -4.0, 4.0)
    return jnp.clip(entries + offset + jitter, -8.0, 8.0).astype(jnp.bfloat16)


def draw_value_heads(key, part):
    columns = jnp.arange(HEADS * HD) // HD
    position = columns.astype(jnp.float32) / (HEADS - 1)
    entries = jnp.clip(jax.random.normal(key, (TOKENS, HEADS * HD), jnp.float32), -4.0, 4.0)
    column_scale = 10.0 ** position
    return (entries * column_scale[None, :]).astype(jnp.bfloat16)


def draw_residual(key, part):
    row_key, column_key, entry_key = jax.random.split(key, 3)
    row_scale = jnp.exp(jax.random.uniform(row_key, (TOKENS, 1), jnp.float32, math.log(0.3), math.log(3.0)))
    column_scale = jnp.exp(jax.random.uniform(column_key, (1, D), jnp.float32, math.log(0.3), math.log(3.0)))
    entries = jnp.clip(jax.random.normal(entry_key, (TOKENS, D), jnp.float32), -4.0, 4.0)
    return jnp.clip(entries * row_scale * column_scale, -36.0, 36.0).astype(jnp.bfloat16)


def level_of(key, dims, cuts, smallest, top_value):
    def one(dim, parts):
        heights = jax.random.uniform(jax.random.fold_in(jax.random.fold_in(key, 6), dim), (parts,), jnp.float32, smallest / len(cuts), top_value / len(cuts))
        return jnp.repeat(jnp.exp(heights), dims[dim] // parts).reshape((-1,) + (1,) * (len(dims) - dim - 1))

    loudness = one(*cuts[0])
    for cut in cuts[1:]:
        loudness = loudness * one(*cut)
    return loudness


def assign_block(rng, own, number, rows, count, top, most, skew):
    order = jax.random.permutation(rng, count)
    heavy_load, usual = load_shares(count, rows * top, most, skew, True), load_shares(count, rows * top, most, skew, False)
    places = jnp.arange(count)

    def named(lengths, rotation):
        used = int((lengths > 0).sum())
        fixed = max(1, used // 4)
        passed = fixed + (places - fixed + rotation * (used - fixed)) % max(1, count - fixed)
        return jnp.zeros((count,), jnp.int32).at[order[jnp.where(places < fixed, places, passed)]].set(jnp.asarray(lengths, jnp.int32))

    lengths = jnp.where(number % 4 == 0, named(heavy_load, number // 4), named(usual, number - number // 4 - 1))
    mixed = jax.random.permutation(jax.random.fold_in(own, 3), count)
    giver, sink = mixed[0:count // 2 * 2:2], mixed[1:count // 2 * 2:2]
    slack = jnp.minimum(lengths[giver] - 1, most - lengths[sink]) // 2
    slack = jnp.where((giver == order[0]) | (sink == order[0]) | (lengths[sink] == 0), 0, jnp.maximum(slack, 0))
    passed = jax.random.randint(jax.random.fold_in(own, 4), (count // 2,), 0, 1 << 20) % (slack + 1)
    lengths = lengths.at[giver].add(-passed).at[sink].add(passed)
    items = jnp.searchsorted(jnp.cumsum(lengths), jnp.arange(rows * top), side="right").astype(jnp.int32)
    grid = items.reshape(top, rows).T
    grid = grid[jax.random.permutation(jax.random.fold_in(own, 1), rows)]
    rotation = jax.random.randint(jax.random.fold_in(own, 2), (rows, 1), 0, top)
    return jnp.take_along_axis(grid, (jnp.arange(top)[None, :] + rotation) % top, axis=1)


def load_shares(number_of, total, most, lean, full):
    portions = [(1 << 20) // math.isqrt(grade ** lean) + 1 for grade in range(1, number_of + 1)]
    largest = most if full else min(most, max(-(-total // number_of), total * portions[0] // sum(portions)))
    least = 1 if total - largest >= number_of - 1 else 0
    counts, rest = [largest] + [least] * (number_of - 1), total - largest - least * (number_of - 1)
    while rest > 0:
        free = [i for i in range(1, number_of) if counts[i] < largest] or [i for i in range(1, number_of) if counts[i] < most]
        whole, remaining = sum([portions[i] for i in free]), rest
        for i in free:
            more = min(most - counts[i], max(1, remaining * portions[i] // whole), rest)
            counts[i] = counts[i] + more
            rest = rest - more
    return np.array(counts)


def scatter_about(stream_key, dims, scale, bound, shards=(), held_as=jnp.bfloat16):
    values = scale * jax.random.normal(stream_key, dims, jnp.float32)
    if shards:
        values = values * level_of(stream_key, dims, shards, -0.22, 0.18)
    return jnp.clip(values, -bound, bound).astype(held_as)


def setup_inputs(seed: int = 0) -> dict:
    arg_keys = jax.random.split(jax.random.key(seed), 14)
    queries = scatter_about(arg_keys[0], (TOKENS, HEADS * HD), 1.0, 6.0, ((0, 4), (1, 32)))
    key_heads = draw_key_heads(jax.random.fold_in(arg_keys[13], 71), 0)
    value_heads = draw_value_heads(jax.random.fold_in(arg_keys[13], 71), 0)
    out_gain = jnp.clip(1.0 + 0.18 * jax.random.normal(arg_keys[3], (HEADS * HD,), jnp.float32), 0.099609375, 1.8984375).astype(jnp.bfloat16)
    out_weight = scatter_about(arg_keys[4], (HEADS * HD, D), (HEADS * HD) ** -0.5, 0.09375, ((0, 32),))
    residual = draw_residual(jax.random.fold_in(arg_keys[13], 71), 0)
    norm_gain = jnp.clip(1.0 + 0.18 * jax.random.normal(arg_keys[6], (D,), jnp.float32), 0.099609375, 1.8984375).astype(jnp.bfloat16)
    routes_keys = jax.random.split(jax.random.fold_in(arg_keys[7], 1), TOKENS // TOK_DEV)
    routes_turns = jax.random.permutation(jax.random.fold_in(arg_keys[7], 3), TOKENS // TOK_DEV)
    routes = jax.vmap(lambda own, number: assign_block(jax.random.fold_in(arg_keys[7], 2), own, number, TOK_DEV, EXPERTS, TOPK, CAP, 2))(routes_keys, routes_turns).reshape((TOKENS, TOPK))
    route_weights = jnp.clip(0.02 + 0.38 * jax.random.uniform(arg_keys[8], (TOKENS, TOPK), jnp.float32) ** level_of(arg_keys[8], (TOKENS, TOPK), ((0, 128),), -0.2, 0.2), 0.02, 0.4)
    cotangent = scatter_about(arg_keys[9], (TOKENS, D), 1.0, 6.0, ((0, 128),))
    w_gate = scatter_about(arg_keys[10], (EXPERTS, D, FF), D ** -0.5, 0.125, ((0, 128),))
    w_up = scatter_about(arg_keys[11], (EXPERTS, D, FF), D ** -0.5, 0.125, ((0, 128),))
    w_down = scatter_about(arg_keys[12], (EXPERTS, FF, D), FF ** -0.5, 0.21875, ((0, 128),))
    return {"queries": queries, "key_heads": key_heads, "value_heads": value_heads, "out_gain": out_gain, "out_weight": out_weight, "residual": residual, "norm_gain": norm_gain, "routes": routes, "route_weights": route_weights, "cotangent": cotangent, "w_gate": w_gate, "w_up": w_up, "w_down": w_down}


epsilon = 1e-06
highest = lax.Precision.HIGHEST

def round_half(values):
    return lax.optimization_barrier(values.astype(jnp.bfloat16)).astype(jnp.float32)

def feature_map(values):
    widened = values.astype(jnp.float32)
    return round_half(jnp.where(widened > 0, widened + 1.0, jnp.exp(jnp.minimum(widened, 0.0))))

def rms_norm(values, gain):
    widened = values.astype(jnp.float32)
    inverse = lax.rsqrt(lax.optimization_barrier(jnp.mean(widened * widened, axis=-1, keepdims=True)) + epsilon)
    return (widened * inverse * gain.astype(jnp.float32)).astype(jnp.bfloat16)

def attend_blocks(query_raw, key_feat, value_wide, state_sum, key_sum, block_size):
    length = query_raw.shape[0]
    heads_here = key_feat.shape[1]
    head_size = key_feat.shape[2]
    causal_mask = jnp.tril(jnp.ones((block_size, block_size), jnp.bool_))

    def into_blocks(array_in):
        return array_in.reshape(length // block_size, block_size, heads_here, head_size)

    def one_block(carry, inputs):
        running_state, running_keys = carry
        query_block, key_block, value_block = inputs
        query_block = feature_map(query_block)
        scores = jnp.einsum('bhi,chi->hbc', query_block, key_block, precision=highest)
        scores = jnp.where(causal_mask[None], scores, 0.0)
        numerator = jnp.einsum('hbc,chj->bhj', scores, value_block, precision=highest)
        numerator = numerator + jnp.einsum('bhi,hij->bhj', query_block, running_state, precision=highest)
        denominator = jnp.einsum('hbc->bh', scores) + jnp.einsum('bhi,hi->bh', query_block, running_keys, precision=highest)
        result = (numerator / denominator[:, :, None]).astype(jnp.bfloat16)
        running_state = running_state + jnp.einsum('bhi,bhj->hij', key_block, value_block, precision=highest)
        running_keys = running_keys + lax.optimization_barrier(jnp.sum(key_block, axis=0))
        return ((running_state, running_keys), result)
    carry_out, outputs = lax.scan(one_block, (state_sum, key_sum), (into_blocks(query_raw), into_blocks(key_feat), into_blocks(value_wide)))
    return outputs.reshape(length, heads_here * head_size)

def expert_grads(rows_in, scaled, gate_mat, up_mat, down_mat):
    gate_pre = jnp.dot(rows_in, gate_mat, preferred_element_type=jnp.float32)
    up_pre = jnp.dot(rows_in, up_mat, preferred_element_type=jnp.float32)
    sigmoid_gate = jax.nn.sigmoid(gate_pre)
    active = gate_pre * sigmoid_gate
    hidden_units = (active * up_pre).astype(jnp.bfloat16)
    grad_down = lax.dot_general(hidden_units, scaled, (((0,), (0,)), ((), ())), preferred_element_type=jnp.float32).astype(jnp.bfloat16)
    grad_hidden = lax.dot_general(scaled, down_mat, (((1,), (1,)), ((), ())), preferred_element_type=jnp.float32)
    silu_slope = sigmoid_gate * (1.0 + gate_pre * (1.0 - sigmoid_gate))
    grad_pre_gate = (grad_hidden * up_pre * silu_slope).astype(jnp.bfloat16)
    grad_pre_up = (grad_hidden * active).astype(jnp.bfloat16)
    grad_gate = lax.dot_general(rows_in, grad_pre_gate, (((0,), (0,)), ((), ())), preferred_element_type=jnp.float32).astype(jnp.bfloat16)
    grad_up = lax.dot_general(rows_in, grad_pre_up, (((0,), (0,)), ((), ())), preferred_element_type=jnp.float32).astype(jnp.bfloat16)
    return (grad_gate, grad_up, grad_down)

def reference(queries, key_heads, value_heads, out_gain, out_weight, residual, norm_gain, routes, route_weights, cotangent, w_gate, w_up, w_down):
    block_size = min(512, TOKENS // N_CTX)
    key_feat = feature_map(key_heads.reshape(TOKENS, HEADS, HD))
    value_wide = value_heads.reshape(TOKENS, HEADS, HD).astype(jnp.float32)
    attention = attend_blocks(queries.reshape(TOKENS, HEADS, HD), key_feat, value_wide, jnp.zeros((HEADS, HD, HD), jnp.float32), jnp.zeros((HEADS, HD), jnp.float32), block_size)
    att_wide = attention.astype(jnp.float32)
    inv_rms = lax.rsqrt(lax.optimization_barrier(jnp.sum(att_wide * att_wide, axis=1)) / (HEADS * HD) + epsilon)
    normed = (att_wide * inv_rms[:, None] * out_gain.astype(jnp.float32)).astype(jnp.bfloat16)
    group_width = HEADS * HD // N_HEAD

    def add_group(group_index, running):
        start = (group_index * group_width).astype(jnp.int32)
        columns = lax.dynamic_slice_in_dim(normed, start, group_width, 1)
        weight_rows = lax.dynamic_slice_in_dim(out_weight, start, group_width, 0)
        return running + round_half(jnp.dot(columns, weight_rows, preferred_element_type=jnp.float32))
    projected = lax.fori_loop(0, N_HEAD, add_group, jnp.zeros((TOKENS, D), jnp.float32))
    hidden_out = (residual.astype(jnp.float32) + projected).astype(jnp.bfloat16)
    moe_in = rms_norm(hidden_out, norm_gain)
    blocks = TOKENS // TOK_DEV
    per_block = TOK_DEV * TOPK
    total_assign = blocks * per_block
    flat_routes = routes.reshape(blocks, per_block).astype(jnp.int32)
    onehot = (flat_routes[:, :, None] == jnp.arange(EXPERTS, dtype=jnp.int32)[None, None, :]).astype(jnp.int32)
    rank_in_block = lax.optimization_barrier(jnp.sum(jnp.cumsum(onehot, axis=1) * onehot, axis=2)) - 1
    position = jnp.arange(blocks, dtype=jnp.int32)[:, None] * CAP + rank_in_block
    slot_table = jnp.full((EXPERTS, blocks * CAP), total_assign, jnp.int32)
    slot_table = slot_table.at[flat_routes, position].set(jnp.arange(total_assign, dtype=jnp.int32).reshape(blocks, per_block))
    flat_weights = route_weights.reshape(total_assign)

    def per_expert(inputs):
        slot_list, gate_mat, up_mat, down_mat = inputs
        is_filled = slot_list < total_assign
        safe_index = jnp.minimum(slot_list, total_assign - 1)
        token_index = safe_index // TOPK
        rows_in = jnp.where(is_filled[:, None], moe_in[token_index], jnp.zeros((), jnp.bfloat16)).astype(jnp.bfloat16)
        weighted = flat_weights[safe_index][:, None] * cotangent[token_index].astype(jnp.float32)
        scaled = jnp.where(is_filled[:, None], weighted, 0.0).astype(jnp.bfloat16)
        return expert_grads(rows_in, scaled, gate_mat, up_mat, down_mat)
    grad_gate, grad_up, grad_down = lax.map(per_expert, (slot_table, w_gate, w_up, w_down))
    return (hidden_out, grad_gate, grad_up, grad_down)
```

```python
import jax
import jax.numpy as jnp
from jax import lax
from jax.experimental import pallas as pl
from jax.experimental.pallas import tpu as pltpu
from jax.sharding import Mesh, PartitionSpec as P

HD = 128
HEADS = 32
EXPERTS = 128
TOPK = 8
MAIN = 8
TAIL = 2
QUART = 4
EPS = 1e-06
BF = jnp.bfloat16
F32 = jnp.float32
ALL = ("ctx", "chip", "core")


def phi(values):
    wide = values.astype(F32)
    return jnp.where(wide > 0, wide + 1.0, jnp.exp(jnp.minimum(wide, 0.0))).astype(BF)


def dot(a, b, ca=1, cb=0):
    return lax.dot_general(a, b, (((ca,), (cb,)), ((), ())), preferred_element_type=F32)


def params(**kw):
    return pltpu.CompilerParams(vmem_limit_bytes=56 * 1024 * 1024, **kw)


def state_kernel(k_ref, v_ref, o_ref, acc):
    i = pl.program_id(0)

    @pl.when(i == 0)
    def _():
        acc[...] = jnp.zeros_like(acc)

    kf = phi(k_ref[...])
    v = v_ref[...]
    acc[...] += dot(kf, jnp.concatenate([v, jnp.ones_like(v)], axis=1), 0, 0)

    @pl.when(i == pl.num_programs(0) - 1)
    def _():
        for c in range(o_ref.shape[0]):
            o_ref[c] = acc[...].astype(BF)


def span_states(keys, values, n_ctx):
    length = keys.shape[0]
    block = min(1024, length)
    return pl.pallas_call(
        state_kernel,
        grid=(length // block,),
        in_specs=[pl.BlockSpec((block, HD), lambda i: (i, 0))] * 2,
        out_specs=pl.BlockSpec((n_ctx, HD, 2 * HD), lambda i: (0, 0, 0)),
        out_shape=jax.ShapeDtypeStruct((n_ctx, HD, 2 * HD), BF),
        scratch_shapes=[pltpu.VMEM((HD, 2 * HD), F32)],
        compiler_params=params(),
    )(keys, values)


CHUNK = 256


def attend_kernel(at_ref, q_ref, k_ref, v_ref, s_ref, o_ref, state):
    @pl.when(pl.program_id(0) == 0)
    def _():
        total = jnp.zeros(state.shape, F32)
        for c in range(s_ref.shape[0]):
            total = total + jnp.where(c < at_ref[0], s_ref[c].astype(F32), 0.0)
        state[...] = total

    rows = lax.broadcasted_iota(jnp.int32, (CHUNK, CHUNK), 0)
    cols = lax.broadcasted_iota(jnp.int32, (CHUNK, CHUNK), 1)
    run = state[...]
    for n in range(q_ref.shape[0] // CHUNK):
        part = pl.ds(n * CHUNK, CHUNK)
        qf = phi(q_ref[part, :])
        kf = phi(k_ref[part, :])
        v = v_ref[part, :]
        v1 = jnp.concatenate([v, jnp.ones_like(v)], axis=1)
        scores = jnp.where(rows >= cols, dot(qf, kf, 1, 1), 0.0).astype(BF)
        both = dot(scores, v1) + dot(qf, run.astype(BF))
        o_ref[part, :] = (both[:, :HD] / both[:, HD:]).astype(BF)
        run = run + dot(kf, v1, 0, 0)
    state[...] = run


def attend(at, queries, keys, values, states):
    length = queries.shape[0]
    block = min(1024, length)
    tok = pl.BlockSpec((block, HD), lambda i, at: (i, 0))
    return pl.pallas_call(
        attend_kernel,
        grid_spec=pltpu.PrefetchScalarGridSpec(
            num_scalar_prefetch=1,
            grid=(length // block,),
            in_specs=[tok, tok, tok, pl.BlockSpec(states.shape, lambda i, at: (0, 0, 0))],
            out_specs=tok,
            scratch_shapes=[pltpu.VMEM((HD, 2 * HD), F32)],
        ),
        out_shape=jax.ShapeDtypeStruct(queries.shape, BF),
        compiler_params=params(),
    )(at, queries, keys, values, states)


def ranks(routes_t, expand):
    tokens = routes_t.shape[1]
    experts = lax.broadcasted_iota(jnp.int32, (EXPERTS, tokens), 0)
    named = jnp.zeros((EXPERTS, tokens), F32)
    for k in range(TOPK):
        named = named + jnp.where(routes_t[k : k + 1, :] == experts, 1.0, 0.0)
    earlier = lax.broadcasted_iota(jnp.int32, (tokens, tokens), 0)
    later = lax.broadcasted_iota(jnp.int32, (tokens, tokens), 1)
    before = jnp.where(earlier < later, 1.0, 0.0).astype(BF)
    rank = jnp.where(named > 0.0, dot(named.astype(BF), before), -1.0)
    return dot(expand, rank.astype(BF))


def expander():
    row = lax.broadcasted_iota(jnp.int32, (EXPERTS * MAIN, EXPERTS), 0) // MAIN
    col = lax.broadcasted_iota(jnp.int32, (EXPERTS * MAIN, EXPERTS), 1)
    return jnp.where(row == col, 1.0, 0.0).astype(BF)


def picks(rank8):
    row = lax.broadcasted_iota(jnp.int32, rank8.shape, 0)
    main = rank8 == (row % MAIN).astype(F32)
    tail = rank8 == (MAIN + row % TAIL).astype(F32)
    return main, tail, (row % MAIN) // TAIL


def tail_rows(tail, quarter, table):
    width = table.shape[1] // QUART
    total = None
    for q in range(QUART):
        pick = jnp.where(tail & (quarter == q), 1.0, 0.0).astype(BF)
        piece = dot(pick, table[:, q * width : (q + 1) * width])
        total = piece if total is None else total + piece
    return total


BLOCKS = 4


def pack_cot_kernel(routes_ref, weights_ref, cot_ref, main_ref, tail_ref, rank_s, weight_s):
    step = pl.program_id(0)

    @pl.when(step == 0)
    def _():
        expand = expander()
        routes_t = routes_ref[...]
        rank_s[...] = ranks(routes_t, expand)
        experts = lax.broadcasted_iota(jnp.int32, (EXPERTS, routes_t.shape[1]), 0)
        weight = jnp.zeros(experts.shape, F32)
        for k in range(TOPK):
            weight = weight + jnp.where(
                routes_t[k : k + 1, :] == experts, weights_ref[k : k + 1, :], 0.0
            )
        total = jnp.zeros(rank_s.shape, F32)
        for _ in range(3):
            piece = weight.astype(BF)
            total = total + dot(expand, piece)
            weight = weight - piece.astype(F32)
        weight_s[...] = total

    size = EXPERTS * MAIN // BLOCKS
    part = pl.ds(step * size, size)
    weight8 = weight_s[part, :]
    main, tail, quarter = picks(rank_s[part, :])
    table = cot_ref[...]
    scale = jnp.sum(jnp.where(main, weight8, 0.0), axis=1, keepdims=True)
    main_ref[...] = (dot(jnp.where(main, 1.0, 0.0).astype(BF), table) * scale).astype(BF)
    scale = jnp.sum(jnp.where(tail, weight8, 0.0), axis=1, keepdims=True)
    tail_ref[...] = (tail_rows(tail, quarter, table) * scale).astype(BF)


def packed_shapes(width):
    rows = EXPERTS * MAIN
    size = rows // BLOCKS
    specs = [
        pl.BlockSpec((size, width), lambda i: (i, 0)),
        pl.BlockSpec((size, width // QUART), lambda i: (i, 0)),
    ]
    shapes = [
        jax.ShapeDtypeStruct((rows, width), BF),
        jax.ShapeDtypeStruct((rows, width // QUART), BF),
    ]
    return specs, shapes


def whole(array):
    return pl.BlockSpec(array.shape, lambda *_: (0,) * array.ndim)


def pack_cot(routes_t, weights_t, cotangent):
    tokens, width = cotangent.shape
    specs, shapes = packed_shapes(width)
    return pl.pallas_call(
        pack_cot_kernel,
        grid=(BLOCKS,),
        in_specs=[whole(routes_t), whole(weights_t), whole(cotangent)],
        out_specs=specs,
        out_shape=shapes,
        scratch_shapes=[pltpu.VMEM((EXPERTS * MAIN, tokens), F32)] * 2,
        compiler_params=params(),
    )(routes_t, weights_t, cotangent)


def project_kernel(core_ref, x_ref, w_ref, mine_ref, ss_ref, theirs_ref, own_s, other_s):
    step = pl.program_id(0)
    tokens = mine_ref.shape[0]
    width = mine_ref.shape[1]
    total = pl.num_programs(0) * width

    @pl.when(step == 0)
    def _():
        core = core_ref[0]
        for at, keep in ((core, own_s), (1 - core, other_s)):
            square = jnp.zeros((tokens, HD), F32)
            for s in range(x_ref.shape[0]):
                piece = x_ref[s, pl.ds(pl.multiple_of(at * tokens, tokens), tokens), :]
                keep[:, s * HD : (s + 1) * HD] = piece
                wide = piece.astype(F32)
                square = square + wide * wide
            summed = jnp.broadcast_to(jnp.sum(square, axis=1, keepdims=True), (tokens, HD))
            if keep is own_s:
                ss_ref[...] = summed
            else:
                high = summed.astype(BF)
                theirs_ref[:, total : total + HD] = high
                theirs_ref[:, total + HD :] = (summed - high.astype(F32)).astype(BF)

    w = w_ref[...]
    mine_ref[...] = dot(own_s[...], w)
    theirs_ref[:, pl.ds(pl.multiple_of(step * width, width), width)] = dot(other_s[...], w).astype(BF)


def project(core, x, weight):
    sources, chip_tokens, _ = x.shape
    tokens = chip_tokens // 2
    depth, width = weight.shape
    block = 512
    return pl.pallas_call(
        project_kernel,
        grid_spec=pltpu.PrefetchScalarGridSpec(
            num_scalar_prefetch=1,
            grid=(width // block,),
            in_specs=[
                pl.BlockSpec(x.shape, lambda i, c: (0, 0, 0)),
                pl.BlockSpec((depth, block), lambda i, c: (0, i)),
            ],
            out_specs=[
                pl.BlockSpec((tokens, block), lambda i, c: (0, i)),
                pl.BlockSpec((tokens, HD), lambda i, c: (0, 0)),
                pl.BlockSpec((tokens, width + 2 * HD), lambda i, c: (0, 0)),
            ],
            scratch_shapes=[pltpu.VMEM((tokens, depth), BF)] * 2,
        ),
        out_shape=[
            jax.ShapeDtypeStruct((tokens, width), F32),
            jax.ShapeDtypeStruct((tokens, HD), F32),
            jax.ShapeDtypeStruct((tokens, width + 2 * HD), BF),
        ],
        compiler_params=params(),
    )(core, x, weight)


def norm_pack_kernel(
    mine_ref, ss_ref, got_ref, residual_ref, gain_ref, routes_ref,
    hidden_ref, main_ref, tail_ref, rank_s, table_s,
):
    step = pl.program_id(0)

    @pl.when(step == 0)
    def _():
        width = mine_ref.shape[1]
        squares = (
            ss_ref[...]
            + got_ref[:, width : width + HD].astype(F32)
            + got_ref[:, width + HD :].astype(F32)
        )[:, :1]
        inverse = lax.rsqrt(squares / (HEADS * HD) + EPS)
        projected = (mine_ref[...] + got_ref[:, :width].astype(F32)) * inverse
        hidden = (residual_ref[...].astype(F32) + projected).astype(BF)
        hidden_ref[...] = hidden
        wide = hidden.astype(F32)
        scale = lax.rsqrt(jnp.mean(wide * wide, axis=1, keepdims=True) + EPS)
        table_s[...] = (wide * scale * gain_ref[...].astype(F32)).astype(BF)
        rank_s[...] = ranks(routes_ref[...], expander())

    size = EXPERTS * MAIN // BLOCKS
    main, tail, quarter = picks(rank_s[pl.ds(step * size, size), :])
    table = table_s[...]
    main_ref[...] = dot(jnp.where(main, 1.0, 0.0).astype(BF), table).astype(BF)
    tail_ref[...] = tail_rows(tail, quarter, table).astype(BF)


def norm_pack(mine, squares, got, residual, gain, routes_t):
    tokens, width = residual.shape
    specs, shapes = packed_shapes(width)
    args = (mine, squares, got, residual, gain, routes_t)
    return pl.pallas_call(
        norm_pack_kernel,
        grid=(BLOCKS,),
        in_specs=[whole(a) for a in args],
        out_specs=[pl.BlockSpec((tokens, width), lambda i: (0, 0))] + specs,
        out_shape=[jax.ShapeDtypeStruct((tokens, width), BF)] + shapes,
        scratch_shapes=[
            pltpu.VMEM((EXPERTS * MAIN, tokens), F32),
            pltpu.VMEM((tokens, width), BF),
        ],
        compiler_params=params(),
    )(*args)


def untail(tail):
    sources, rows, width = tail.shape
    split = tail.reshape(sources, QUART, TAIL, width).transpose(0, 2, 1, 3)
    return split.reshape(sources * TAIL, QUART * width)


def expert_grads(rows_in, scaled, gate_mat, up_mat, down_mat):
    gate_pre = dot(rows_in, gate_mat)
    up_pre = dot(rows_in, up_mat)
    sigmoid_gate = jax.nn.sigmoid(gate_pre)
    active = gate_pre * sigmoid_gate
    hidden_units = (active * up_pre).astype(BF)
    grad_down = dot(hidden_units, scaled, 0, 0).astype(BF)
    grad_hidden = dot(scaled, down_mat, 1, 1)
    silu_slope = sigmoid_gate * (1.0 + gate_pre * (1.0 - sigmoid_gate))
    grad_pre_gate = (grad_hidden * up_pre * silu_slope).astype(BF)
    grad_pre_up = (grad_hidden * active).astype(BF)
    grad_gate = dot(rows_in, grad_pre_gate, 0, 0).astype(BF)
    grad_up = dot(rows_in, grad_pre_up, 0, 0).astype(BF)
    return (grad_gate, grad_up, grad_down)


def exchange(array, axes):
    return lax.all_to_all(array, axes, split_axis=0, concat_axis=0, tiled=True)


def on_device(
    queries, key_heads, value_heads, out_gain, out_weight, residual, norm_gain,
    routes, route_weights, cotangent, w_gate, w_up, w_down,
):
    n_ctx = lax.axis_size("ctx")
    n_chip = lax.axis_size("chip")
    width = residual.shape[1]
    at = lax.axis_index("ctx").astype(jnp.int32).reshape(1)
    core = lax.axis_index("core").astype(jnp.int32).reshape(1)

    scaled_weight = (out_weight.astype(F32) * out_gain.astype(F32)[:, None]).astype(BF)
    weight = lax.all_gather(scaled_weight, "chip", axis=0, tiled=True)

    states = exchange(span_states(key_heads, value_heads, n_ctx), "ctx")
    routes_t = routes.T
    cot_main, cot_tail = pack_cot(routes_t, route_weights.T, cotangent)
    attention = attend(at, queries, key_heads, value_heads, states)
    by_chip = exchange(attention.reshape(n_chip, -1, HD), "chip")
    cot_main = exchange(cot_main.reshape(EXPERTS, MAIN, width), ALL)
    cot_tail = exchange(cot_tail.reshape(EXPERTS, MAIN, width // QUART), ALL)

    mine, squares, theirs = project(core, by_chip, weight)
    got = lax.ppermute(theirs, "core", [(0, 1), (1, 0)])
    hidden_out, moe_main, moe_tail = norm_pack(
        mine, squares, got, residual, norm_gain[None], routes_t
    )
    moe_main = exchange(moe_main.reshape(EXPERTS, MAIN, width), ALL)
    moe_tail = exchange(moe_tail.reshape(EXPERTS, MAIN, width // QUART), ALL)

    rows_in = jnp.concatenate([moe_main.reshape(-1, width), untail(moe_tail)], axis=0)
    scaled = jnp.concatenate([cot_main.reshape(-1, width), untail(cot_tail)], axis=0)
    grads = expert_grads(rows_in, scaled, w_gate[0], w_up[0], w_down[0])
    return (hidden_out,) + tuple(g[None] for g in grads)


def solution(mesh):
    n_ctx, n_head = mesh.devices.shape
    fine = Mesh(mesh.devices.reshape(n_ctx, n_head // 2, 2), ALL)
    head = ("chip", "core")
    in_specs = (
        P("ctx", head), P("ctx", head), P("ctx", head), P(head), P(head, None),
        P(ALL, None), P(), P(ALL, None), P(ALL, None), P(ALL, None),
        P(ALL, None, None), P(ALL, None, None), P(ALL, None, None),
    )
    out_specs = (P(ALL, None), P(ALL, None, None), P(ALL, None, None), P(ALL, None, None))
    return jax.shard_map(
        on_device, mesh=fine, in_specs=in_specs, out_specs=out_specs, check_vma=False
    )
```

```python
import jax
import jax.numpy as jnp
from jax import lax
from jax.experimental import pallas as pl
from jax.experimental.pallas import tpu as pltpu
from jax.sharding import Mesh, PartitionSpec as P

HD = 128
HEADS = 32
EXPERTS = 128
TOPK = 8
MAIN = 8
TAIL = 2
QUART = 4
EPS = 1e-06
BF = jnp.bfloat16
F32 = jnp.float32
ALL = ("ctx", "chip", "core")


def phi(values):
    wide = values.astype(F32)
    return jnp.where(wide > 0, wide + 1.0, jnp.exp(jnp.minimum(wide, 0.0))).astype(BF)


def dot(a, b, ca=1, cb=0):
    return lax.dot_general(a, b, (((ca,), (cb,)), ((), ())), preferred_element_type=F32)


def params(**kw):
    return pltpu.CompilerParams(vmem_limit_bytes=56 * 1024 * 1024, **kw)


def state_kernel(k_ref, v_ref, o_ref, acc):
    i = pl.program_id(0)

    @pl.when(i == 0)
    def _():
        acc[...] = jnp.zeros_like(acc)

    kf = phi(k_ref[...])
    v = v_ref[...]
    acc[...] += dot(kf, jnp.concatenate([v, jnp.ones_like(v)], axis=1), 0, 0)

    @pl.when(i == pl.num_programs(0) - 1)
    def _():
        for c in range(o_ref.shape[0]):
            o_ref[c] = acc[...].astype(BF)


def span_states(keys, values, n_ctx):
    length = keys.shape[0]
    block = min(1024, length)
    return pl.pallas_call(
        state_kernel,
        grid=(length // block,),
        in_specs=[pl.BlockSpec((block, HD), lambda i: (i, 0))] * 2,
        out_specs=pl.BlockSpec((n_ctx, HD, 2 * HD), lambda i: (0, 0, 0)),
        out_shape=jax.ShapeDtypeStruct((n_ctx, HD, 2 * HD), BF),
        scratch_shapes=[pltpu.VMEM((HD, 2 * HD), F32)],
        compiler_params=params(),
    )(keys, values)


CHUNK = 256
EXTRA = 16


def attend_kernel(at_ref, q_ref, k_ref, v_ref, s_ref, g_ref, o_ref, state):
    @pl.when(pl.program_id(0) == 0)
    def _():
        total = jnp.zeros(state.shape, F32)
        for c in range(s_ref.shape[0]):
            total = total + jnp.where(c < at_ref[0], s_ref[c].astype(F32), 0.0)
        state[...] = total

    rows = lax.broadcasted_iota(jnp.int32, (CHUNK, CHUNK), 0)
    cols = lax.broadcasted_iota(jnp.int32, (CHUNK, CHUNK), 1)
    run = state[...]
    per_chip = o_ref.shape[1] - EXTRA
    for c in range(o_ref.shape[0]):
        o_ref[c, per_chip:, :] = jnp.broadcast_to(g_ref[...], (EXTRA, HD))
    for n in range(q_ref.shape[0] // CHUNK):
        part = pl.ds(n * CHUNK, CHUNK)
        qf = phi(q_ref[part, :])
        kf = phi(k_ref[part, :])
        v = v_ref[part, :]
        v1 = jnp.concatenate([v, jnp.ones_like(v)], axis=1)
        scores = jnp.where(rows >= cols, dot(qf, kf, 1, 1), 0.0).astype(BF)
        both = dot(scores, v1) + dot(qf, run.astype(BF))
        o_ref[n, :per_chip, :] = (both[:, :HD] / both[:, HD:]).astype(BF)
        run = run + dot(kf, v1, 0, 0)
    state[...] = run


def attend(at, queries, keys, values, states, gain):
    length = queries.shape[0]
    block = min(1024, length)
    each = block // CHUNK
    tok = pl.BlockSpec((block, HD), lambda i, at: (i, 0))
    return pl.pallas_call(
        attend_kernel,
        grid_spec=pltpu.PrefetchScalarGridSpec(
            num_scalar_prefetch=1,
            grid=(length // block,),
            in_specs=[tok, tok, tok, whole(states), whole(gain)],
            out_specs=pl.BlockSpec((each, CHUNK + EXTRA, HD), lambda i, at: (i, 0, 0)),
            scratch_shapes=[pltpu.VMEM((HD, 2 * HD), F32)],
        ),
        out_shape=jax.ShapeDtypeStruct((length // CHUNK, CHUNK + EXTRA, HD), BF),
        compiler_params=params(),
    )(at, queries, keys, values, states, gain)


def ranks(routes_t, expand):
    tokens = routes_t.shape[1]
    experts = lax.broadcasted_iota(jnp.int32, (EXPERTS, tokens), 0)
    named = jnp.zeros((EXPERTS, tokens), F32)
    for k in range(TOPK):
        named = named + jnp.where(routes_t[k : k + 1, :] == experts, 1.0, 0.0)
    earlier = lax.broadcasted_iota(jnp.int32, (tokens, tokens), 0)
    later = lax.broadcasted_iota(jnp.int32, (tokens, tokens), 1)
    before = jnp.where(earlier < later, 1.0, 0.0).astype(BF)
    rank = jnp.where(named > 0.0, dot(named.astype(BF), before), -1.0)
    return dot(expand, rank.astype(BF))


def expander():
    row = lax.broadcasted_iota(jnp.int32, (EXPERTS * MAIN, EXPERTS), 0) // MAIN
    col = lax.broadcasted_iota(jnp.int32, (EXPERTS * MAIN, EXPERTS), 1)
    return jnp.where(row == col, 1.0, 0.0).astype(BF)


def picks(rank8):
    row = lax.broadcasted_iota(jnp.int32, rank8.shape, 0)
    main = rank8 == (row % MAIN).astype(F32)
    tail = rank8 == (MAIN + row % TAIL).astype(F32)
    return main, tail, (row % MAIN) // TAIL


def tail_rows(tail, quarter, table):
    width = table.shape[1] // QUART
    total = None
    for q in range(QUART):
        pick = jnp.where(tail & (quarter == q), 1.0, 0.0).astype(BF)
        piece = dot(pick, table[:, q * width : (q + 1) * width])
        total = piece if total is None else total + piece
    return total


BLOCKS = 4


def pack_cot_kernel(routes_ref, weights_ref, cot_ref, out_ref, rank_s, weight_s):
    step = pl.program_id(0)

    @pl.when(step == 0)
    def _():
        expand = expander()
        routes_t = routes_ref[...]
        rank_s[...] = ranks(routes_t, expand)
        experts = lax.broadcasted_iota(jnp.int32, (EXPERTS, routes_t.shape[1]), 0)
        weight = jnp.zeros(experts.shape, F32)
        for k in range(TOPK):
            weight = weight + jnp.where(
                routes_t[k : k + 1, :] == experts, weights_ref[k : k + 1, :], 0.0
            )
        total = jnp.zeros(rank_s.shape, F32)
        for _ in range(3):
            piece = weight.astype(BF)
            total = total + dot(expand, piece)
            weight = weight - piece.astype(F32)
        weight_s[...] = total

    size = EXPERTS * MAIN // BLOCKS
    part = pl.ds(step * size, size)
    weight8 = weight_s[part, :]
    main, tail, quarter = picks(rank_s[part, :])
    table = cot_ref[...]
    scale = jnp.sum(jnp.where(main, weight8, 0.0), axis=1, keepdims=True)
    width = table.shape[1]
    out_ref[:, :width] = (dot(jnp.where(main, 1.0, 0.0).astype(BF), table) * scale).astype(BF)
    scale = jnp.sum(jnp.where(tail, weight8, 0.0), axis=1, keepdims=True)
    out_ref[:, width:] = (tail_rows(tail, quarter, table) * scale).astype(BF)


def packed(width):
    rows = EXPERTS * MAIN
    wide = width + width // QUART
    spec = pl.BlockSpec((rows // BLOCKS, wide), lambda i: (i, 0))
    return spec, jax.ShapeDtypeStruct((rows, wide), BF)


def whole(array):
    return pl.BlockSpec(array.shape, lambda *_: (0,) * array.ndim)


def pack_cot(routes_t, weights_t, cotangent):
    tokens, width = cotangent.shape
    spec, shape = packed(width)
    return pl.pallas_call(
        pack_cot_kernel,
        grid=(BLOCKS,),
        in_specs=[whole(routes_t), whole(weights_t), whole(cotangent)],
        out_specs=spec,
        out_shape=shape,
        scratch_shapes=[pltpu.VMEM((EXPERTS * MAIN, tokens), F32)] * 2,
        compiler_params=params(),
    )(routes_t, weights_t, cotangent)


def project_kernel(core_ref, x_ref, w_ref, mine_ref, ss_ref, theirs_ref, own_s, other_s):
    step = pl.program_id(0)
    tokens = mine_ref.shape[0]
    width = mine_ref.shape[1]
    total = pl.num_programs(0) * width

    @pl.when(step == 0)
    def _():
        core = core_ref[0]
        for at, keep in ((core, own_s), (1 - core, other_s)):
            square = jnp.zeros((tokens, HD), F32)
            for s in range(x_ref.shape[0]):
                piece = x_ref[s, pl.ds(pl.multiple_of(at * tokens, tokens), tokens), :]
                wide = piece.astype(F32)
                gain = x_ref[s, 2 * tokens : 2 * tokens + 1, :].astype(F32)
                keep[:, s * HD : (s + 1) * HD] = (wide * gain).astype(BF)
                square = square + wide * wide
            summed = jnp.broadcast_to(jnp.sum(square, axis=1, keepdims=True), (tokens, HD))
            if keep is own_s:
                ss_ref[...] = summed
            else:
                high = summed.astype(BF)
                theirs_ref[:, total : total + HD] = high
                theirs_ref[:, total + HD :] = (summed - high.astype(F32)).astype(BF)

    w = w_ref[...]
    mine_ref[...] = dot(own_s[...], w)
    theirs_ref[:, pl.ds(pl.multiple_of(step * width, width), width)] = dot(other_s[...], w).astype(BF)


def project(core, x, weight):
    tokens = (x.shape[1] - EXTRA) // 2
    depth = x.shape[0] * HD
    block = weight.shape[1]
    blocks = weight.shape[0] // depth
    width = blocks * block
    return pl.pallas_call(
        project_kernel,
        grid_spec=pltpu.PrefetchScalarGridSpec(
            num_scalar_prefetch=1,
            grid=(blocks,),
            in_specs=[
                pl.BlockSpec(x.shape, lambda i, c: (0, 0, 0)),
                pl.BlockSpec((depth, block), lambda i, c: (i, 0)),
            ],
            out_specs=[
                pl.BlockSpec((tokens, block), lambda i, c: (0, i)),
                pl.BlockSpec((tokens, HD), lambda i, c: (0, 0)),
                pl.BlockSpec((tokens, width + 2 * HD), lambda i, c: (0, 0)),
            ],
            scratch_shapes=[pltpu.VMEM((tokens, depth), BF)] * 2,
        ),
        out_shape=[
            jax.ShapeDtypeStruct((tokens, width), F32),
            jax.ShapeDtypeStruct((tokens, HD), F32),
            jax.ShapeDtypeStruct((tokens, width + 2 * HD), BF),
        ],
        compiler_params=params(),
    )(core, x, weight)


def norm_pack_kernel(
    mine_ref, ss_ref, got_ref, residual_ref, gain_ref, routes_ref,
    hidden_ref, out_ref, rank_s, table_s,
):
    step = pl.program_id(0)

    @pl.when(step == 0)
    def _():
        width = mine_ref.shape[1]
        squares = (
            ss_ref[...]
            + got_ref[:, width : width + HD].astype(F32)
            + got_ref[:, width + HD :].astype(F32)
        )[:, :1]
        inverse = lax.rsqrt(squares / (HEADS * HD) + EPS)
        projected = (mine_ref[...] + got_ref[:, :width].astype(F32)) * inverse
        hidden = (residual_ref[...].astype(F32) + projected).astype(BF)
        hidden_ref[...] = hidden
        wide = hidden.astype(F32)
        scale = lax.rsqrt(jnp.mean(wide * wide, axis=1, keepdims=True) + EPS)
        table_s[...] = (wide * scale * gain_ref[...].astype(F32)).astype(BF)
        rank_s[...] = ranks(routes_ref[...], expander())

    size = EXPERTS * MAIN // BLOCKS
    main, tail, quarter = picks(rank_s[pl.ds(step * size, size), :])
    table = table_s[...]
    width = table.shape[1]
    out_ref[:, :width] = dot(jnp.where(main, 1.0, 0.0).astype(BF), table).astype(BF)
    out_ref[:, width:] = tail_rows(tail, quarter, table).astype(BF)


def norm_pack(mine, squares, got, residual, gain, routes_t):
    tokens, width = residual.shape
    spec, shape = packed(width)
    args = (mine, squares, got, residual, gain, routes_t)
    return pl.pallas_call(
        norm_pack_kernel,
        grid=(BLOCKS,),
        in_specs=[whole(a) for a in args],
        out_specs=[pl.BlockSpec((tokens, width), lambda i: (0, 0)), spec],
        out_shape=[jax.ShapeDtypeStruct((tokens, width), BF), shape],
        scratch_shapes=[
            pltpu.VMEM((EXPERTS * MAIN, tokens), F32),
            pltpu.VMEM((tokens, width), BF),
        ],
        compiler_params=params(),
    )(*args)


def untail(tail):
    sources, rows, width = tail.shape
    split = tail.reshape(sources, QUART, TAIL, width).transpose(0, 2, 1, 3)
    return split.reshape(sources * TAIL, QUART * width)


def expert_grads(rows_in, scaled, gate_mat, up_mat, down_mat):
    gate_pre = dot(rows_in, gate_mat)
    up_pre = dot(rows_in, up_mat)
    sigmoid_gate = jax.nn.sigmoid(gate_pre)
    active = gate_pre * sigmoid_gate
    hidden_units = (active * up_pre).astype(BF)
    grad_down = dot(hidden_units, scaled, 0, 0).astype(BF)
    grad_hidden = dot(scaled, down_mat, 1, 1)
    silu_slope = sigmoid_gate * (1.0 + gate_pre * (1.0 - sigmoid_gate))
    grad_pre_gate = (grad_hidden * up_pre * silu_slope).astype(BF)
    grad_pre_up = (grad_hidden * active).astype(BF)
    grad_gate = dot(rows_in, grad_pre_gate, 0, 0).astype(BF)
    grad_up = dot(rows_in, grad_pre_up, 0, 0).astype(BF)
    return (grad_gate, grad_up, grad_down)


def exchange(array, axes):
    return lax.all_to_all(array, axes, split_axis=0, concat_axis=0, tiled=True)


def on_device(
    queries, key_heads, value_heads, out_gain, out_weight, residual, norm_gain,
    routes, route_weights, cotangent, w_gate, w_up, w_down,
):
    n_ctx = lax.axis_size("ctx")
    width = residual.shape[1]
    at = lax.axis_index("ctx").astype(jnp.int32).reshape(1)
    core = lax.axis_index("core").astype(jnp.int32).reshape(1)

    strip = width // n_ctx
    weight = lax.dynamic_slice_in_dim(out_weight, at[0] * strip, strip, 1)
    weight = lax.all_gather(weight, ("ctx", "chip"), axis=0, tiled=True)
    states = exchange(span_states(key_heads, value_heads, n_ctx), "ctx")
    routes_t = routes.T
    cot = pack_cot(routes_t, route_weights.T, cotangent)
    attention = attend(at, queries, key_heads, value_heads, states, out_gain[None])
    by_chip = exchange(attention, "chip")
    cot, by_chip = lax.optimization_barrier((cot, by_chip))
    cot = exchange(cot.reshape(EXPERTS, MAIN, -1), ALL)

    mine, squares, theirs = project(core, by_chip, weight)
    got = lax.ppermute(theirs, "core", [(0, 1), (1, 0)])
    hidden_out, moe = norm_pack(mine, squares, got, residual, norm_gain[None], routes_t)
    moe = exchange(moe.reshape(EXPERTS, MAIN, -1), ALL)

    def rows(both):
        main = both[:, :, :width].reshape(-1, width)
        return jnp.concatenate([main, untail(both[:, :, width:])], axis=0)

    grads = expert_grads(rows(moe), rows(cot), w_gate[0], w_up[0], w_down[0])
    return (hidden_out,) + tuple(g[None] for g in grads)


def solution(mesh):
    n_ctx, n_head = mesh.devices.shape
    fine = Mesh(mesh.devices.reshape(n_ctx, n_head // 2, 2), ALL)
    head = ("chip", "core")
    in_specs = (
        P("ctx", head), P("ctx", head), P("ctx", head), P(head), P(head, None),
        P(ALL, None), P(), P(ALL, None), P(ALL, None), P(ALL, None),
        P(ALL, None, None), P(ALL, None, None), P(ALL, None, None),
    )
    out_specs = (P(ALL, None), P(ALL, None, None), P(ALL, None, None), P(ALL, None, None))
    return jax.shard_map(
        on_device, mesh=fine, in_specs=in_specs, out_specs=out_specs, check_vma=False
    )
```

```python
import jax
import jax.numpy as jnp
from jax import lax
from jax.experimental import pallas as pl
from jax.experimental.pallas import tpu as pltpu
from jax.sharding import Mesh, PartitionSpec as P


HD = 128
HEADS = 32
EXPERTS = 128
TOPK = 8
MAIN = 8
TAIL = 2
QUART = 4
EPS = 1e-06
BF = jnp.bfloat16
F32 = jnp.float32
CHIP = ("x", "z")
ALL = ("ctx",) + CHIP + ("core",)
NEAR = (0, -1, 1, 2)


def phi(values):
    wide = values.astype(F32)
    return jnp.where(wide > 0, wide + 1.0, jnp.exp(jnp.minimum(wide, 0.0))).astype(BF)


def dot(a, b, ca=1, cb=0):
    return lax.dot_general(a, b, (((ca,), (cb,)), ((), ())), preferred_element_type=F32)


def params(**kw):
    return pltpu.CompilerParams(vmem_limit_bytes=56 * 1024 * 1024, **kw)


def state_kernel(k_ref, v_ref, o_ref, acc):
    i = pl.program_id(0)

    @pl.when(i == 0)
    def _():
        acc[...] = jnp.zeros_like(acc)

    kf = phi(k_ref[...])
    v = v_ref[...]
    acc[...] += dot(kf, jnp.concatenate([v, jnp.ones_like(v)], axis=1), 0, 0)

    @pl.when(i == pl.num_programs(0) - 1)
    def _():
        for c in range(o_ref.shape[0]):
            o_ref[c] = acc[...].astype(BF)


def span_states(keys, values, n_ctx):
    length = keys.shape[0]
    block = min(1024, length)
    return pl.pallas_call(
        state_kernel,
        grid=(length // block,),
        in_specs=[pl.BlockSpec((block, HD), lambda i: (i, 0))] * 2,
        out_specs=pl.BlockSpec((n_ctx, HD, 2 * HD), lambda i: (0, 0, 0)),
        out_shape=jax.ShapeDtypeStruct((n_ctx, HD, 2 * HD), BF),
        scratch_shapes=[pltpu.VMEM((HD, 2 * HD), F32)],
        compiler_params=params(),
    )(keys, values)


CHUNK = 256
EXTRA = 16


def attend_kernel(at_ref, q_ref, k_ref, v_ref, s_ref, g_ref, o_ref, state):
    @pl.when(pl.program_id(0) == 0)
    def _():
        total = jnp.zeros(state.shape, F32)
        for c in range(s_ref.shape[0]):
            total = total + jnp.where(c < at_ref[0], s_ref[c].astype(F32), 0.0)
        state[...] = total

    rows = lax.broadcasted_iota(jnp.int32, (CHUNK, CHUNK), 0)
    cols = lax.broadcasted_iota(jnp.int32, (CHUNK, CHUNK), 1)
    run = state[...]
    per_chip = o_ref.shape[1] - EXTRA
    for c in range(o_ref.shape[0]):
        o_ref[c, per_chip:, :] = jnp.broadcast_to(g_ref[...], (EXTRA, HD))
    for n in range(q_ref.shape[0] // CHUNK):
        part = pl.ds(n * CHUNK, CHUNK)
        qf = phi(q_ref[part, :])
        kf = phi(k_ref[part, :])
        v = v_ref[part, :]
        v1 = jnp.concatenate([v, jnp.ones_like(v)], axis=1)
        scores = jnp.where(rows >= cols, dot(qf, kf, 1, 1), 0.0).astype(BF)
        both = dot(scores, v1) + dot(qf, run.astype(BF))
        o_ref[n, :per_chip, :] = (both[:, :HD] / both[:, HD:]).astype(BF)
        run = run + dot(kf, v1, 0, 0)
    state[...] = run


def attend(at, queries, keys, values, states, gain):
    length = queries.shape[0]
    block = min(1024, length)
    each = block // CHUNK
    tok = pl.BlockSpec((block, HD), lambda i, at: (i, 0))
    return pl.pallas_call(
        attend_kernel,
        grid_spec=pltpu.PrefetchScalarGridSpec(
            num_scalar_prefetch=1,
            grid=(length // block,),
            in_specs=[tok, tok, tok, whole(states), whole(gain)],
            out_specs=pl.BlockSpec((each, CHUNK + EXTRA, HD), lambda i, at: (i, 0, 0)),
            scratch_shapes=[pltpu.VMEM((HD, 2 * HD), F32)],
        ),
        out_shape=jax.ShapeDtypeStruct((length // CHUNK, CHUNK + EXTRA, HD), BF),
        compiler_params=params(),
    )(at, queries, keys, values, states, gain)


def ranks(routes_t, expand):
    tokens = routes_t.shape[1]
    experts = lax.broadcasted_iota(jnp.int32, (EXPERTS, tokens), 0)
    named = jnp.zeros((EXPERTS, tokens), F32)
    for k in range(TOPK):
        named = named + jnp.where(routes_t[k : k + 1, :] == experts, 1.0, 0.0)
    earlier = lax.broadcasted_iota(jnp.int32, (tokens, tokens), 0)
    later = lax.broadcasted_iota(jnp.int32, (tokens, tokens), 1)
    before = jnp.where(earlier < later, 1.0, 0.0).astype(BF)
    rank = jnp.where(named > 0.0, dot(named.astype(BF), before), -1.0)
    return dot(expand, rank.astype(BF))


def expander():
    row = lax.broadcasted_iota(jnp.int32, (EXPERTS * MAIN, EXPERTS), 0) // MAIN
    col = lax.broadcasted_iota(jnp.int32, (EXPERTS * MAIN, EXPERTS), 1)
    return jnp.where(row == col, 1.0, 0.0).astype(BF)


def picks(rank8):
    row = lax.broadcasted_iota(jnp.int32, rank8.shape, 0)
    main = rank8 == (row % MAIN).astype(F32)
    tail = rank8 == (MAIN + row % TAIL).astype(F32)
    return main, tail, (row % MAIN) // TAIL


def tail_rows(tail, quarter, table):
    width = table.shape[1] // QUART
    total = None
    for q in range(QUART):
        pick = jnp.where(tail & (quarter == q), 1.0, 0.0).astype(BF)
        piece = dot(pick, table[:, q * width : (q + 1) * width])
        total = piece if total is None else total + piece
    return total


BLOCKS = 4


def pack_cot_kernel(routes_ref, weights_ref, cot_ref, out_ref, rank_s, weight_s):
    step = pl.program_id(0)

    @pl.when(step == 0)
    def _():
        expand = expander()
        routes_t = routes_ref[...]
        rank_s[...] = ranks(routes_t, expand)
        experts = lax.broadcasted_iota(jnp.int32, (EXPERTS, routes_t.shape[1]), 0)
        weight = jnp.zeros(experts.shape, F32)
        for k in range(TOPK):
            weight = weight + jnp.where(
                routes_t[k : k + 1, :] == experts, weights_ref[k : k + 1, :], 0.0
            )
        total = jnp.zeros(rank_s.shape, F32)
        for _ in range(3):
            piece = weight.astype(BF)
            total = total + dot(expand, piece)
            weight = weight - piece.astype(F32)
        weight_s[...] = total

    size = EXPERTS * MAIN // BLOCKS
    part = pl.ds(step * size, size)
    weight8 = weight_s[part, :]
    main, tail, quarter = picks(rank_s[part, :])
    table = cot_ref[...]
    scale = jnp.sum(jnp.where(main, weight8, 0.0), axis=1, keepdims=True)
    width = table.shape[1]
    out_ref[:, :width] = (dot(jnp.where(main, 1.0, 0.0).astype(BF), table) * scale).astype(BF)
    scale = jnp.sum(jnp.where(tail, weight8, 0.0), axis=1, keepdims=True)
    out_ref[:, width:] = (tail_rows(tail, quarter, table) * scale).astype(BF)


def packed(width):
    rows = EXPERTS * MAIN
    wide = width + width // QUART
    spec = pl.BlockSpec((rows // BLOCKS, wide), lambda i: (i, 0))
    return spec, jax.ShapeDtypeStruct((rows, wide), BF)


def whole(array):
    return pl.BlockSpec(array.shape, lambda *_: (0,) * array.ndim)


def pack_cot(routes_t, weights_t, cotangent):
    tokens, width = cotangent.shape
    spec, shape = packed(width)
    return pl.pallas_call(
        pack_cot_kernel,
        grid=(BLOCKS,),
        in_specs=[whole(routes_t), whole(weights_t), whole(cotangent)],
        out_specs=spec,
        out_shape=shape,
        scratch_shapes=[pltpu.VMEM((EXPERTS * MAIN, tokens), F32)] * 2,
        compiler_params=params(),
    )(routes_t, weights_t, cotangent)


def project_kernel(place_ref, x_ref, *refs):
    pieces, (mine_ref, ss_ref, theirs_ref, keep_a, keep_b) = refs[:-5], refs[-5:]
    tokens, total = mine_ref.shape
    core = place_ref[0]
    for half in range(2):
        at = pl.multiple_of((core if half == 0 else 1 - core) * tokens, tokens)
        rows = slice(half * tokens, (half + 1) * tokens)
        square = jnp.zeros((tokens, HD), F32)
        for s in range(x_ref.shape[0]):
            chip = place_ref[1 + s]
            wide = x_ref[chip, pl.ds(at, tokens), :].astype(F32)
            gain = x_ref[chip, pl.ds(2 * tokens, 8), :].astype(F32)[:1]
            square = square + wide * wide
            piece = (wide * gain).astype(BF)
            other = s % 4 * 4 + s // 4
            keep_a[rows, s * HD : (s + 1) * HD] = piece
            keep_b[rows, other * HD : (other + 1) * HD] = piece
        summed = jnp.broadcast_to(jnp.sum(square, axis=1, keepdims=True), (tokens, HD))
        if half == 0:
            ss_ref[...] = summed
        else:
            high = summed.astype(BF)
            theirs_ref[:, total : total + HD] = high
            theirs_ref[:, total + HD :] = (summed - high.astype(F32)).astype(BF)

    side = total // 2
    for n, keep in enumerate((keep_a, keep_b)):
        own, left, right, far_left, far_right = pieces[5 * n : 5 * n + 5]
        depth = own.shape[0]
        for j, far in enumerate((far_left, far_right)):
            width = far.shape[1]
            cols = slice(j * width, (j + 1) * width)
            both = dot(keep[:, 3 * depth :], far[...])
            for g, piece in enumerate((own, left, right)):
                both = both + dot(keep[:, g * depth : (g + 1) * depth], piece[:, cols])
            to = slice(n * side + j * width, n * side + (j + 1) * width)
            mine_ref[:, to] = both[:tokens]
            theirs_ref[:, to] = both[tokens:].astype(BF)


def project(place, x, pieces, width):
    tokens = (x.shape[1] - EXTRA) // 2
    depth = x.shape[0] * HD
    args = (x,) + tuple(pieces)
    return pl.pallas_call(
        project_kernel,
        grid_spec=pltpu.PrefetchScalarGridSpec(
            num_scalar_prefetch=1,
            grid=(1,),
            in_specs=[whole(a) for a in args],
            out_specs=[
                pl.BlockSpec((tokens, width), lambda i, c: (0, 0)),
                pl.BlockSpec((tokens, HD), lambda i, c: (0, 0)),
                pl.BlockSpec((tokens, width + 2 * HD), lambda i, c: (0, 0)),
            ],
            scratch_shapes=[pltpu.VMEM((2 * tokens, depth), BF)] * 2,
        ),
        out_shape=[
            jax.ShapeDtypeStruct((tokens, width), F32),
            jax.ShapeDtypeStruct((tokens, HD), F32),
            jax.ShapeDtypeStruct((tokens, width + 2 * HD), BF),
        ],
        compiler_params=params(),
    )(place, *args)


def norm_pack_kernel(
    mine_ref, ss_ref, got_ref, residual_ref, gain_ref, routes_ref,
    hidden_ref, out_ref, rank_s, table_s,
):
    step = pl.program_id(0)

    @pl.when(step == 0)
    def _():
        width = mine_ref.shape[1]
        squares = (
            ss_ref[...]
            + got_ref[:, width : width + HD].astype(F32)
            + got_ref[:, width + HD :].astype(F32)
        )[:, :1]
        inverse = lax.rsqrt(squares / (HEADS * HD) + EPS)
        projected = (mine_ref[...] + got_ref[:, :width].astype(F32)) * inverse
        hidden = (residual_ref[...].astype(F32) + projected).astype(BF)
        hidden_ref[...] = hidden
        wide = hidden.astype(F32)
        scale = lax.rsqrt(jnp.mean(wide * wide, axis=1, keepdims=True) + EPS)
        table_s[...] = (wide * scale * gain_ref[...].astype(F32)).astype(BF)
        rank_s[...] = ranks(routes_ref[...], expander())

    size = EXPERTS * MAIN // BLOCKS
    main, tail, quarter = picks(rank_s[pl.ds(step * size, size), :])
    table = table_s[...]
    width = table.shape[1]
    out_ref[:, :width] = dot(jnp.where(main, 1.0, 0.0).astype(BF), table).astype(BF)
    out_ref[:, width:] = tail_rows(tail, quarter, table).astype(BF)


def norm_pack(mine, squares, got, residual, gain, routes_t):
    tokens, width = residual.shape
    spec, shape = packed(width)
    args = (mine, squares, got, residual, gain, routes_t)
    return pl.pallas_call(
        norm_pack_kernel,
        grid=(BLOCKS,),
        in_specs=[whole(a) for a in args],
        out_specs=[pl.BlockSpec((tokens, width), lambda i: (0, 0)), spec],
        out_shape=[jax.ShapeDtypeStruct((tokens, width), BF), shape],
        scratch_shapes=[
            pltpu.VMEM((EXPERTS * MAIN, tokens), F32),
            pltpu.VMEM((tokens, width), BF),
        ],
        compiler_params=params(),
    )(*args)


ROWS = 256


def untail(tail, keep):
    sources = tail.shape[0] // MAIN
    to = lax.broadcasted_iota(jnp.int32, (sources * TAIL, tail.shape[0]), 0)
    of = lax.broadcasted_iota(jnp.int32, (sources * TAIL, tail.shape[0]), 1)
    width = tail.shape[1]
    for q in range(QUART):
        pick = of == to // TAIL * MAIN + q * TAIL + to % TAIL
        piece = dot(jnp.where(pick, 1.0, 0.0).astype(BF), tail)
        keep(slice(q * width, (q + 1) * width), piece.astype(BF))


def hidden_kernel(rows_ref, tail_ref, down_ref, out_ref, scaled_ref):
    step = pl.program_id(0)
    last = pl.num_programs(0) - 1

    @pl.when(step < last)
    def _():
        out_ref[...] = dot(rows_ref[...], down_ref[...], 1, 1)

    @pl.when(step == last)
    def _():
        def keep(cols, piece):
            scaled_ref[:, cols] = piece

        untail(tail_ref[...], keep)
        out_ref[...] = dot(scaled_ref[...], down_ref[...], 1, 1)


def hidden_grad(cot, down):
    rows = cot.shape[0]
    units, width = down.shape
    blocks = rows // ROWS
    tails = rows // MAIN * TAIL
    return pl.pallas_call(
        hidden_kernel,
        grid=(blocks + 1,),
        in_specs=[
            pl.BlockSpec((ROWS, width), lambda i: (jnp.minimum(i, blocks - 1), 0)),
            pl.BlockSpec((rows, width // QUART), lambda i: (0, QUART)),
            whole(down),
        ],
        out_specs=[
            pl.BlockSpec((ROWS, units), lambda i: (i, 0)),
            pl.BlockSpec((tails, width), lambda i: (0, 0)),
        ],
        out_shape=[
            jax.ShapeDtypeStruct((rows + tails, units), F32),
            jax.ShapeDtypeStruct((tails, width), BF),
        ],
        compiler_params=params(),
    )(cot, cot, down)


def grads_kernel(
    x_ref, tail_ref, back_ref, gate_ref, up_ref, scaled_ref, scaled_tail_ref,
    grad_gate_ref, grad_up_ref, grad_down_ref, x_s, hidden_s, pre_s,
):
    step = pl.program_id(0)
    total, _ = x_s.shape
    units = gate_ref.shape[1]
    blocks = total // ROWS
    part = pl.ds(pl.multiple_of(step * ROWS, ROWS), ROWS)

    @pl.when(step < blocks - 1)
    def _():
        x_s[part, :] = x_ref[...]

    @pl.when(step == blocks - 1)
    def _():
        def keep(cols, piece):
            x_s[total - ROWS :, cols] = piece

        untail(tail_ref[...], keep)

    @pl.when(step < blocks)
    def _():
        x = x_s[part, :]
        piece = 256
        for c in range(units // piece):
            cols = slice(c * piece, (c + 1) * piece)
            gate = dot(x, gate_ref[:, cols])
            up = dot(x, up_ref[:, cols])
            back = back_ref[:, cols]
            sig = jax.nn.sigmoid(gate)
            active = gate * sig
            hidden_s[cols, part] = jnp.transpose(active * up).astype(BF)
            slope = sig * (1.0 + gate * (1.0 - sig))
            pre_s[part, cols] = (back * up * slope).astype(BF)
            pre_s[part, units + c * piece : units + (c + 1) * piece] = (back * active).astype(BF)

    @pl.when(step >= blocks)
    def _():
        block = grad_gate_ref.shape[0]
        x = x_s[:, pl.ds(pl.multiple_of((step - blocks) * block, block), block)]
        both = dot(x, pre_s[...], 0, 0)
        grad_gate_ref[...] = both[:, :units].astype(BF)
        grad_up_ref[...] = both[:, units:].astype(BF)
        main = scaled_ref.shape[0]
        down = dot(hidden_s[:, :main], scaled_ref[...])
        down = down + dot(hidden_s[:, main:], scaled_tail_ref[...])
        grad_down_ref[...] = down.astype(BF)


def expert_grads(moe, cot, scaled_tail, back, gate, up):
    main = moe.shape[0]
    width, units = gate.shape
    total = back.shape[0]
    blocks = total // ROWS
    block = 256
    at_rows = lambda i: (jnp.minimum(i, blocks - 2), 0)
    at_cols = lambda i: (0, jnp.maximum(i - blocks, 0))
    at_out = lambda i: (jnp.maximum(i - blocks, 0), 0)
    return pl.pallas_call(
        grads_kernel,
        grid=(blocks + width // block,),
        in_specs=[
            pl.BlockSpec((ROWS, width), at_rows),
            pl.BlockSpec((main, width // QUART), lambda i: (0, QUART)),
            pl.BlockSpec((ROWS, units), lambda i: (jnp.minimum(i, blocks - 1), 0)),
            whole(gate),
            whole(up),
            pl.BlockSpec((main, block), at_cols),
            pl.BlockSpec((total - main, block), at_cols),
        ],
        out_specs=[
            pl.BlockSpec((block, units), at_out),
            pl.BlockSpec((block, units), at_out),
            pl.BlockSpec((units, block), at_cols),
        ],
        out_shape=[
            jax.ShapeDtypeStruct((width, units), BF),
            jax.ShapeDtypeStruct((width, units), BF),
            jax.ShapeDtypeStruct((units, width), BF),
        ],
        scratch_shapes=[
            pltpu.VMEM((total, width), BF),
            pltpu.VMEM((units, total), BF),
            pltpu.VMEM((total, 2 * units), BF),
        ],
        compiler_params=params(),
    )(moe, moe, back, gate, up, cot, scaled_tail)


def shift(array, axis, by):
    size = lax.axis_size(axis)
    return lax.ppermute(array, axis, [(i, (i + by) % size) for i in range(size)])


def around(array, axis):
    left = shift(array, axis, 1)
    right = shift(array, axis, -1)
    half = array.shape[1] // 2
    far_left = shift(left[:, :half], axis, 1)
    far_right = shift(right[:, half:], axis, -1)
    return array, left, right, far_left, far_right


def joined(parts):
    own, left, right, far_left, far_right = parts
    far = jnp.concatenate([far_left, far_right], axis=1)
    return jnp.concatenate([own, left, right, far], axis=0)


def spread_weight(weight):
    half = weight.shape[1] // 2
    first = joined(around(weight[:, :half], "z"))
    second = joined(around(weight[:, half:], "x"))
    return around(first, "x") + around(second, "z")


def exchange(array, axes):
    return lax.all_to_all(array, axes, split_axis=0, concat_axis=0, tiled=True)


def on_device(
    queries, key_heads, value_heads, out_gain, out_weight, residual, norm_gain,
    routes, route_weights, cotangent, w_gate, w_up, w_down,
):
    n_ctx = lax.axis_size("ctx")
    width = residual.shape[1]
    at = lax.axis_index("ctx").astype(jnp.int32).reshape(1)
    n_x, n_z = lax.axis_size("x"), lax.axis_size("z")
    near = jnp.array(NEAR, jnp.int32)
    at_x = (lax.axis_index("x") + near) % n_x
    at_z = (lax.axis_index("z") + near) % n_z
    order = (at_x[:, None] * n_z + at_z[None, :]).reshape(-1)
    place = jnp.concatenate([lax.axis_index("core").reshape(1), order]).astype(jnp.int32)

    pieces = spread_weight(out_weight)
    states = span_states(key_heads, value_heads, n_ctx)
    states = exchange(states, "ctx")
    attention = attend(at, queries, key_heads, value_heads, states, out_gain[None])
    by_chip = exchange(attention, CHIP)
    routes_t = routes.T
    cot = pack_cot(routes_t, route_weights.T, cotangent)
    cot, by_chip = lax.optimization_barrier((cot, by_chip))
    cot = exchange(cot.reshape(EXPERTS, MAIN, -1), ALL)

    mine, squares, theirs = project(place, by_chip, pieces, width)
    got = lax.ppermute(theirs, "core", [(0, 1), (1, 0)])
    hidden_out, moe = norm_pack(mine, squares, got, residual, norm_gain[None], routes_t)
    moe = exchange(moe.reshape(EXPERTS, MAIN, -1), ALL)

    moe = moe.reshape(EXPERTS * MAIN, -1)
    cot = cot.reshape(EXPERTS * MAIN, -1)
    back, scaled_tail = hidden_grad(cot, w_down[0])
    grads = expert_grads(moe, cot, scaled_tail, back, w_gate[0], w_up[0])
    return (hidden_out,) + tuple(g[None] for g in grads)


def solution(mesh):
    n_ctx, n_head = mesh.devices.shape
    side = 4
    fine = Mesh(mesh.devices.reshape(n_ctx, side, n_head // (2 * side), 2), ALL)
    head = CHIP + ("core",)
    in_specs = (
        P("ctx", head), P("ctx", head), P("ctx", head), P(head), P(head, None),
        P(ALL, None), P(), P(ALL, None), P(ALL, None), P(ALL, None),
        P(ALL, None, None), P(ALL, None, None), P(ALL, None, None),
    )
    out_specs = (P(ALL, None), P(ALL, None, None), P(ALL, None, None), P(ALL, None, None))

    return jax.shard_map(
        on_device, mesh=fine, in_specs=in_specs, out_specs=out_specs, check_vma=False
    )
```

```python
import jax
import jax.numpy as jnp
from jax import lax
from jax.experimental import pallas as pl
from jax.experimental.pallas import tpu as pltpu
from jax.sharding import Mesh, PartitionSpec as P


HD = 128
HEADS = 32
EXPERTS = 128
TOPK = 8
MAIN = 8
TAIL = 2
QUART = 4
EPS = 1e-06
BF = jnp.bfloat16
F32 = jnp.float32
CHIP = ("x", "z")
ALL = ("ctx",) + CHIP + ("core",)
NEAR = (0, -1, 1, 2)


def phi(values):
    wide = values.astype(F32)
    return jnp.where(wide > 0, wide + 1.0, jnp.exp(jnp.minimum(wide, 0.0))).astype(BF)


def dot(a, b, ca=1, cb=0):
    return lax.dot_general(a, b, (((ca,), (cb,)), ((), ())), preferred_element_type=F32)


def params(**kw):
    return pltpu.CompilerParams(vmem_limit_bytes=56 * 1024 * 1024, **kw)


def state_kernel(k_ref, v_ref, o_ref, acc):
    i = pl.program_id(0)

    @pl.when(i == 0)
    def _():
        acc[...] = jnp.zeros_like(acc)

    kf = phi(k_ref[...])
    v = v_ref[...]
    acc[...] += dot(kf, jnp.concatenate([v, jnp.ones_like(v)], axis=1), 0, 0)

    @pl.when(i == pl.num_programs(0) - 1)
    def _():
        for c in range(o_ref.shape[0]):
            o_ref[c] = acc[...].astype(BF)


def span_states(keys, values, n_ctx):
    length = keys.shape[0]
    block = min(1024, length)
    return pl.pallas_call(
        state_kernel,
        grid=(length // block,),
        in_specs=[pl.BlockSpec((block, HD), lambda i: (i, 0))] * 2,
        out_specs=pl.BlockSpec((n_ctx, HD, 2 * HD), lambda i: (0, 0, 0)),
        out_shape=jax.ShapeDtypeStruct((n_ctx, HD, 2 * HD), BF),
        scratch_shapes=[pltpu.VMEM((HD, 2 * HD), F32)],
        compiler_params=params(),
    )(keys, values)


CHUNK = 256
EXTRA = 16


def attend_kernel(at_ref, q_ref, k_ref, v_ref, s_ref, g_ref, o_ref, state):
    @pl.when(pl.program_id(0) == 0)
    def _():
        total = jnp.zeros(state.shape, F32)
        for c in range(s_ref.shape[0]):
            total = total + jnp.where(c < at_ref[0], s_ref[c].astype(F32), 0.0)
        state[...] = total

    rows = lax.broadcasted_iota(jnp.int32, (CHUNK, CHUNK), 0)
    cols = lax.broadcasted_iota(jnp.int32, (CHUNK, CHUNK), 1)
    run = state[...]
    per_chip = o_ref.shape[1] - EXTRA
    for c in range(o_ref.shape[0]):
        o_ref[c, per_chip:, :] = jnp.broadcast_to(g_ref[...], (EXTRA, HD))
    for n in range(q_ref.shape[0] // CHUNK):
        part = pl.ds(n * CHUNK, CHUNK)
        qf = phi(q_ref[part, :])
        kf = phi(k_ref[part, :])
        v = v_ref[part, :]
        v1 = jnp.concatenate([v, jnp.ones_like(v)], axis=1)
        scores = jnp.where(rows >= cols, dot(qf, kf, 1, 1), 0.0).astype(BF)
        both = dot(scores, v1) + dot(qf, run.astype(BF))
        o_ref[n, :per_chip, :] = (both[:, :HD] / both[:, HD:]).astype(BF)
        run = run + dot(kf, v1, 0, 0)
    state[...] = run


def attend(at, queries, keys, values, states, gain):
    length = queries.shape[0]
    block = min(1024, length)
    each = block // CHUNK
    tok = pl.BlockSpec((block, HD), lambda i, at: (i, 0))
    return pl.pallas_call(
        attend_kernel,
        grid_spec=pltpu.PrefetchScalarGridSpec(
            num_scalar_prefetch=1,
            grid=(length // block,),
            in_specs=[tok, tok, tok, whole(states), whole(gain)],
            out_specs=pl.BlockSpec((each, CHUNK + EXTRA, HD), lambda i, at: (i, 0, 0)),
            scratch_shapes=[pltpu.VMEM((HD, 2 * HD), F32)],
        ),
        out_shape=jax.ShapeDtypeStruct((length // CHUNK, CHUNK + EXTRA, HD), BF),
        compiler_params=params(),
    )(at, queries, keys, values, states, gain)


def ranks(routes_t, expand):
    tokens = routes_t.shape[1]
    experts = lax.broadcasted_iota(jnp.int32, (EXPERTS, tokens), 0)
    named = jnp.zeros((EXPERTS, tokens), F32)
    for k in range(TOPK):
        named = named + jnp.where(routes_t[k : k + 1, :] == experts, 1.0, 0.0)
    earlier = lax.broadcasted_iota(jnp.int32, (tokens, tokens), 0)
    later = lax.broadcasted_iota(jnp.int32, (tokens, tokens), 1)
    before = jnp.where(earlier < later, 1.0, 0.0).astype(BF)
    rank = jnp.where(named > 0.0, dot(named.astype(BF), before), -1.0)
    return dot(expand, rank.astype(BF))


def expander():
    row = lax.broadcasted_iota(jnp.int32, (EXPERTS * MAIN, EXPERTS), 0) // MAIN
    col = lax.broadcasted_iota(jnp.int32, (EXPERTS * MAIN, EXPERTS), 1)
    return jnp.where(row == col, 1.0, 0.0).astype(BF)


def picks(rank8):
    row = lax.broadcasted_iota(jnp.int32, rank8.shape, 0)
    main = rank8 == (row % MAIN).astype(F32)
    tail = rank8 == (MAIN + row % TAIL).astype(F32)
    return main, tail, (row % MAIN) // TAIL


def tail_rows(tail, quarter, table):
    width = table.shape[1] // QUART
    total = None
    for q in range(QUART):
        pick = jnp.where(tail & (quarter == q), 1.0, 0.0).astype(BF)
        piece = dot(pick, table[:, q * width : (q + 1) * width])
        total = piece if total is None else total + piece
    return total


BLOCKS = 4


def pack_cot_kernel(routes_ref, weights_ref, cot_ref, out_ref, rank_s, weight_s):
    step = pl.program_id(0)

    @pl.when(step == 0)
    def _():
        expand = expander()
        routes_t = routes_ref[...]
        rank_s[...] = ranks(routes_t, expand)
        experts = lax.broadcasted_iota(jnp.int32, (EXPERTS, routes_t.shape[1]), 0)
        weight = jnp.zeros(experts.shape, F32)
        for k in range(TOPK):
            weight = weight + jnp.where(
                routes_t[k : k + 1, :] == experts, weights_ref[k : k + 1, :], 0.0
            )
        total = jnp.zeros(rank_s.shape, F32)
        for _ in range(3):
            piece = weight.astype(BF)
            total = total + dot(expand, piece)
            weight = weight - piece.astype(F32)
        weight_s[...] = total

    size = EXPERTS * MAIN // BLOCKS
    part = pl.ds(step * size, size)
    weight8 = weight_s[part, :]
    main, tail, quarter = picks(rank_s[part, :])
    table = cot_ref[...]
    scale = jnp.sum(jnp.where(main, weight8, 0.0), axis=1, keepdims=True)
    width = table.shape[1]
    out_ref[:, :width] = (dot(jnp.where(main, 1.0, 0.0).astype(BF), table) * scale).astype(BF)
    scale = jnp.sum(jnp.where(tail, weight8, 0.0), axis=1, keepdims=True)
    out_ref[:, width:] = (tail_rows(tail, quarter, table) * scale).astype(BF)


def packed(width):
    rows = EXPERTS * MAIN
    wide = width + width // QUART
    spec = pl.BlockSpec((rows // BLOCKS, wide), lambda i: (i, 0))
    return spec, jax.ShapeDtypeStruct((rows, wide), BF)


def whole(array):
    return pl.BlockSpec(array.shape, lambda *_: (0,) * array.ndim)


def pack_cot(routes_t, weights_t, cotangent):
    tokens, width = cotangent.shape
    spec, shape = packed(width)
    return pl.pallas_call(
        pack_cot_kernel,
        grid=(BLOCKS,),
        in_specs=[whole(routes_t), whole(weights_t), whole(cotangent)],
        out_specs=spec,
        out_shape=shape,
        scratch_shapes=[pltpu.VMEM((EXPERTS * MAIN, tokens), F32)] * 2,
        compiler_params=params(),
    )(routes_t, weights_t, cotangent)


def project_kernel(place_ref, x_ref, *refs):
    pieces, (mine_ref, ss_ref, theirs_ref, keep_a, keep_b) = refs[:-5], refs[-5:]
    tokens, total = mine_ref.shape
    core = place_ref[0]
    for half in range(2):
        at = pl.multiple_of((core if half == 0 else 1 - core) * tokens, tokens)
        rows = slice(half * tokens, (half + 1) * tokens)
        square = jnp.zeros((tokens, HD), F32)
        for s in range(x_ref.shape[0]):
            chip = place_ref[1 + s]
            wide = x_ref[chip, pl.ds(at, tokens), :].astype(F32)
            gain = x_ref[chip, pl.ds(2 * tokens, 8), :].astype(F32)[:1]
            square = square + wide * wide
            piece = (wide * gain).astype(BF)
            other = s % 4 * 4 + s // 4
            keep_a[rows, s * HD : (s + 1) * HD] = piece
            keep_b[rows, other * HD : (other + 1) * HD] = piece
        summed = jnp.broadcast_to(jnp.sum(square, axis=1, keepdims=True), (tokens, HD))
        if half == 0:
            ss_ref[...] = summed
        else:
            high = summed.astype(BF)
            theirs_ref[:, total : total + HD] = high
            theirs_ref[:, total + HD :] = (summed - high.astype(F32)).astype(BF)

    depth, side = pieces[0].shape
    for n in range(total // side):
        keep = keep_a if 2 * n < total // side else keep_b
        both = jnp.zeros((2 * tokens, side), F32)
        for g in range(4):
            both = both + dot(keep[:, g * depth : (g + 1) * depth], pieces[4 * n + g][...])
        to = slice(n * side, (n + 1) * side)
        mine_ref[:, to] = both[:tokens]
        theirs_ref[:, to] = both[tokens:].astype(BF)


def project(place, x, pieces, width):
    tokens = (x.shape[1] - EXTRA) // 2
    depth = x.shape[0] * HD
    args = (x,) + tuple(pieces)
    return pl.pallas_call(
        project_kernel,
        grid_spec=pltpu.PrefetchScalarGridSpec(
            num_scalar_prefetch=1,
            grid=(1,),
            in_specs=[whole(a) for a in args],
            out_specs=[
                pl.BlockSpec((tokens, width), lambda i, c: (0, 0)),
                pl.BlockSpec((tokens, HD), lambda i, c: (0, 0)),
                pl.BlockSpec((tokens, width + 2 * HD), lambda i, c: (0, 0)),
            ],
            scratch_shapes=[pltpu.VMEM((2 * tokens, depth), BF)] * 2,
        ),
        out_shape=[
            jax.ShapeDtypeStruct((tokens, width), F32),
            jax.ShapeDtypeStruct((tokens, HD), F32),
            jax.ShapeDtypeStruct((tokens, width + 2 * HD), BF),
        ],
        compiler_params=params(),
    )(place, *args)


def norm_pack_kernel(
    mine_ref, ss_ref, got_ref, residual_ref, gain_ref, routes_ref,
    hidden_ref, out_ref, rank_s, table_s,
):
    step = pl.program_id(0)

    @pl.when(step == 0)
    def _():
        width = mine_ref.shape[1]
        squares = (
            ss_ref[...]
            + got_ref[:, width : width + HD].astype(F32)
            + got_ref[:, width + HD :].astype(F32)
        )[:, :1]
        inverse = lax.rsqrt(squares / (HEADS * HD) + EPS)
        projected = (mine_ref[...] + got_ref[:, :width].astype(F32)) * inverse
        hidden = (residual_ref[...].astype(F32) + projected).astype(BF)
        hidden_ref[...] = hidden
        wide = hidden.astype(F32)
        scale = lax.rsqrt(jnp.mean(wide * wide, axis=1, keepdims=True) + EPS)
        table_s[...] = (wide * scale * gain_ref[...].astype(F32)).astype(BF)
        rank_s[...] = ranks(routes_ref[...], expander())

    size = EXPERTS * MAIN // BLOCKS
    main, tail, quarter = picks(rank_s[pl.ds(step * size, size), :])
    table = table_s[...]
    width = table.shape[1]
    out_ref[:, :width] = dot(jnp.where(main, 1.0, 0.0).astype(BF), table).astype(BF)
    out_ref[:, width:] = tail_rows(tail, quarter, table).astype(BF)


def norm_pack(mine, squares, got, residual, gain, routes_t):
    tokens, width = residual.shape
    spec, shape = packed(width)
    args = (mine, squares, got, residual, gain, routes_t)
    return pl.pallas_call(
        norm_pack_kernel,
        grid=(BLOCKS,),
        in_specs=[whole(a) for a in args],
        out_specs=[pl.BlockSpec((tokens, width), lambda i: (0, 0)), spec],
        out_shape=[jax.ShapeDtypeStruct((tokens, width), BF), shape],
        scratch_shapes=[
            pltpu.VMEM((EXPERTS * MAIN, tokens), F32),
            pltpu.VMEM((tokens, width), BF),
        ],
        compiler_params=params(),
    )(*args)


ROWS = 256


def untail(tail, keep):
    sources = tail.shape[0] // MAIN
    to = lax.broadcasted_iota(jnp.int32, (sources * TAIL, tail.shape[0]), 0)
    of = lax.broadcasted_iota(jnp.int32, (sources * TAIL, tail.shape[0]), 1)
    width = tail.shape[1]
    for q in range(QUART):
        pick = of == to // TAIL * MAIN + q * TAIL + to % TAIL
        piece = dot(jnp.where(pick, 1.0, 0.0).astype(BF), tail)
        keep(slice(q * width, (q + 1) * width), piece.astype(BF))


def hidden_kernel(rows_ref, tail_ref, down_ref, out_ref, scaled_ref):
    step = pl.program_id(0)
    last = pl.num_programs(0) - 1

    @pl.when(step < last)
    def _():
        out_ref[...] = dot(rows_ref[...], down_ref[...], 1, 1)

    @pl.when(step == last)
    def _():
        def keep(cols, piece):
            scaled_ref[:, cols] = piece

        untail(tail_ref[...], keep)
        out_ref[...] = dot(scaled_ref[...], down_ref[...], 1, 1)


def hidden_grad(cot, down):
    rows = cot.shape[0]
    units, width = down.shape
    blocks = rows // ROWS
    tails = rows // MAIN * TAIL
    return pl.pallas_call(
        hidden_kernel,
        grid=(blocks + 1,),
        in_specs=[
            pl.BlockSpec((ROWS, width), lambda i: (jnp.minimum(i, blocks - 1), 0)),
            pl.BlockSpec((rows, width // QUART), lambda i: (0, QUART)),
            whole(down),
        ],
        out_specs=[
            pl.BlockSpec((ROWS, units), lambda i: (i, 0)),
            pl.BlockSpec((tails, width), lambda i: (0, 0)),
        ],
        out_shape=[
            jax.ShapeDtypeStruct((rows + tails, units), F32),
            jax.ShapeDtypeStruct((tails, width), BF),
        ],
        compiler_params=params(),
    )(cot, cot, down)


def grads_kernel(
    x_ref, tail_ref, back_ref, gate_ref, up_ref, scaled_ref, scaled_tail_ref,
    grad_gate_ref, grad_up_ref, grad_down_ref, x_s, hidden_s, pre_s,
):
    step = pl.program_id(0)
    total, _ = x_s.shape
    units = gate_ref.shape[1]
    blocks = total // ROWS
    part = pl.ds(pl.multiple_of(step * ROWS, ROWS), ROWS)

    @pl.when(step < blocks - 1)
    def _():
        x_s[part, :] = x_ref[...]

    @pl.when(step == blocks - 1)
    def _():
        def keep(cols, piece):
            x_s[total - ROWS :, cols] = piece

        untail(tail_ref[...], keep)

    @pl.when(step < blocks)
    def _():
        x = x_s[part, :]
        piece = 256
        for c in range(units // piece):
            cols = slice(c * piece, (c + 1) * piece)
            gate = dot(x, gate_ref[:, cols])
            up = dot(x, up_ref[:, cols])
            back = back_ref[:, cols]
            sig = jax.nn.sigmoid(gate)
            active = gate * sig
            hidden_s[cols, part] = jnp.transpose(active * up).astype(BF)
            slope = sig * (1.0 + gate * (1.0 - sig))
            pre_s[part, cols] = (back * up * slope).astype(BF)
            pre_s[part, units + c * piece : units + (c + 1) * piece] = (back * active).astype(BF)

    @pl.when(step >= blocks)
    def _():
        block = grad_gate_ref.shape[0]
        x = x_s[:, pl.ds(pl.multiple_of((step - blocks) * block, block), block)]
        both = dot(x, pre_s[...], 0, 0)
        grad_gate_ref[...] = both[:, :units].astype(BF)
        grad_up_ref[...] = both[:, units:].astype(BF)
        main = scaled_ref.shape[0]
        down = dot(hidden_s[:, :main], scaled_ref[...])
        down = down + dot(hidden_s[:, main:], scaled_tail_ref[...])
        grad_down_ref[...] = down.astype(BF)


def expert_grads(moe, cot, scaled_tail, back, gate, up):
    main = moe.shape[0]
    width, units = gate.shape
    total = back.shape[0]
    blocks = total // ROWS
    block = 512
    at_rows = lambda i: (jnp.minimum(i, blocks - 2), 0)
    at_cols = lambda i: (0, jnp.maximum(i - blocks, 0))
    at_out = lambda i: (jnp.maximum(i - blocks, 0), 0)
    return pl.pallas_call(
        grads_kernel,
        grid=(blocks + width // block,),
        in_specs=[
            pl.BlockSpec((ROWS, width), at_rows),
            pl.BlockSpec((main, width // QUART), lambda i: (0, QUART)),
            pl.BlockSpec((ROWS, units), lambda i: (jnp.minimum(i, blocks - 1), 0)),
            whole(gate),
            whole(up),
            pl.BlockSpec((main, block), at_cols),
            pl.BlockSpec((total - main, block), at_cols),
        ],
        out_specs=[
            pl.BlockSpec((block, units), at_out),
            pl.BlockSpec((block, units), at_out),
            pl.BlockSpec((units, block), at_cols),
        ],
        out_shape=[
            jax.ShapeDtypeStruct((width, units), BF),
            jax.ShapeDtypeStruct((width, units), BF),
            jax.ShapeDtypeStruct((units, width), BF),
        ],
        scratch_shapes=[
            pltpu.VMEM((total, width), BF),
            pltpu.VMEM((units, total), BF),
            pltpu.VMEM((total, 2 * units), BF),
        ],
        compiler_params=params(),
    )(moe, moe, back, gate, up, cot, scaled_tail)


def shift(array, axis, by):
    size = lax.axis_size(axis)
    return lax.ppermute(array, axis, [(i, (i + by) % size) for i in range(size)])


def around(first, second, axis):
    left_first = shift(first, axis, 1)
    right_second = shift(second, axis, -1)
    left_second = shift(second, axis, 1)
    right_first = shift(first, axis, -1)
    far_first = shift(left_first, axis, 1)
    far_second = shift(right_second, axis, -1)
    return [first, left_first, right_first, far_first], [second, left_second, right_second, far_second]


def spread_weight(weight):
    quarter = weight.shape[1] // 4
    parts = [weight[:, n * quarter : (n + 1) * quarter] for n in range(4)]
    pieces = []
    for n, (near, far) in enumerate((("z", "x"), ("x", "z"))):
        halves = around(parts[2 * n], parts[2 * n + 1], near)
        first, second = (jnp.concatenate(half, axis=0) for half in halves)
        for half in around(first, second, far):
            pieces += half
    return tuple(pieces)


def exchange(array, axes):
    return lax.all_to_all(array, axes, split_axis=0, concat_axis=0, tiled=True)


def on_device(
    queries, key_heads, value_heads, out_gain, out_weight, residual, norm_gain,
    routes, route_weights, cotangent, w_gate, w_up, w_down,
):
    n_ctx = lax.axis_size("ctx")
    width = residual.shape[1]
    at = lax.axis_index("ctx").astype(jnp.int32).reshape(1)
    n_x, n_z = lax.axis_size("x"), lax.axis_size("z")
    near = jnp.array(NEAR, jnp.int32)
    at_x = (lax.axis_index("x") + near) % n_x
    at_z = (lax.axis_index("z") + near) % n_z
    order = (at_x[:, None] * n_z + at_z[None, :]).reshape(-1)
    place = jnp.concatenate([lax.axis_index("core").reshape(1), order]).astype(jnp.int32)

    pieces = spread_weight(out_weight)
    states = span_states(key_heads, value_heads, n_ctx)
    states = exchange(states, "ctx")
    attention = attend(at, queries, key_heads, value_heads, states, out_gain[None])
    by_chip = exchange(attention, CHIP)
    routes_t = routes.T
    cot = pack_cot(routes_t, route_weights.T, cotangent)
    cot, by_chip, pieces = lax.optimization_barrier((cot, by_chip, pieces))
    cot = exchange(cot.reshape(EXPERTS, MAIN, -1), ALL)

    mine, squares, theirs = project(place, by_chip, pieces, width)
    got = lax.ppermute(theirs, "core", [(0, 1), (1, 0)])
    hidden_out, moe = norm_pack(mine, squares, got, residual, norm_gain[None], routes_t)
    moe = exchange(moe.reshape(EXPERTS, MAIN, -1), ALL)

    moe = moe.reshape(EXPERTS * MAIN, -1)
    cot = cot.reshape(EXPERTS * MAIN, -1)
    back, scaled_tail = hidden_grad(cot, w_down[0])
    grads = expert_grads(moe, cot, scaled_tail, back, w_gate[0], w_up[0])
    return (hidden_out,) + tuple(g[None] for g in grads)


def solution(mesh):
    n_ctx, n_head = mesh.devices.shape
    side = 4
    fine = Mesh(mesh.devices.reshape(n_ctx, side, n_head // (2 * side), 2), ALL)
    head = CHIP + ("core",)
    in_specs = (
        P("ctx", head), P("ctx", head), P("ctx", head), P(head), P(head, None),
        P(ALL, None), P(), P(ALL, None), P(ALL, None), P(ALL, None),
        P(ALL, None, None), P(ALL, None, None), P(ALL, None, None),
    )
    out_specs = (P(ALL, None), P(ALL, None, None), P(ALL, None, None), P(ALL, None, None))

    return jax.shard_map(
        on_device, mesh=fine, in_specs=in_specs, out_specs=out_specs, check_vma=False
    )
```

```python
import jax
import jax.numpy as jnp
from jax import lax
from jax.experimental import pallas as pl
from jax.experimental.pallas import tpu as pltpu
from jax.sharding import Mesh, PartitionSpec as P


HD = 128
HEADS = 32
EXPERTS = 128
TOPK = 8
MAIN = 8
TAIL = 2
QUART = 4
EPS = 1e-06
BF = jnp.bfloat16
F32 = jnp.float32
CHIP = ("x", "z")
ALL = ("ctx",) + CHIP + ("core",)
NEAR = (0, -1, 1, 2)


def phi(values):
    wide = values.astype(F32)
    return jnp.where(wide > 0, wide + 1.0, jnp.exp(jnp.minimum(wide, 0.0))).astype(BF)


def dot(a, b, ca=1, cb=0):
    return lax.dot_general(a, b, (((ca,), (cb,)), ((), ())), preferred_element_type=F32)


def params(**kw):
    return pltpu.CompilerParams(vmem_limit_bytes=56 * 1024 * 1024, **kw)


def state_kernel(k_ref, v_ref, o_ref, acc):
    i = pl.program_id(0)

    @pl.when(i == 0)
    def _():
        acc[...] = jnp.zeros_like(acc)

    kf = phi(k_ref[...])
    v = v_ref[...]
    acc[...] += dot(kf, jnp.concatenate([v, jnp.ones_like(v)], axis=1), 0, 0)

    @pl.when(i == pl.num_programs(0) - 1)
    def _():
        for c in range(o_ref.shape[0]):
            o_ref[c] = acc[...].astype(BF)


def span_states(keys, values, n_ctx):
    length = keys.shape[0]
    block = min(1024, length)
    return pl.pallas_call(
        state_kernel,
        grid=(length // block,),
        in_specs=[pl.BlockSpec((block, HD), lambda i: (i, 0))] * 2,
        out_specs=pl.BlockSpec((n_ctx, HD, 2 * HD), lambda i: (0, 0, 0)),
        out_shape=jax.ShapeDtypeStruct((n_ctx, HD, 2 * HD), BF),
        scratch_shapes=[pltpu.VMEM((HD, 2 * HD), F32)],
        compiler_params=params(),
    )(keys, values)


CHUNK = 256
EXTRA = 16


def attend_kernel(at_ref, q_ref, k_ref, v_ref, s_ref, g_ref, o_ref, state):
    @pl.when(pl.program_id(0) == 0)
    def _():
        total = jnp.zeros(state.shape, F32)
        for c in range(s_ref.shape[0]):
            total = total + jnp.where(c < at_ref[0], s_ref[c].astype(F32), 0.0)
        state[...] = total

    rows = lax.broadcasted_iota(jnp.int32, (CHUNK, CHUNK), 0)
    cols = lax.broadcasted_iota(jnp.int32, (CHUNK, CHUNK), 1)
    run = state[...]
    cores, rows_out, _ = o_ref.shape
    own = CHUNK // cores
    for c in range(cores):
        o_ref[c, rows_out - EXTRA :, :] = jnp.broadcast_to(g_ref[...], (EXTRA, HD))
    for n in range(q_ref.shape[0] // CHUNK):
        part = pl.ds(n * CHUNK, CHUNK)
        qf = phi(q_ref[part, :])
        kf = phi(k_ref[part, :])
        v = v_ref[part, :]
        v1 = jnp.concatenate([v, jnp.ones_like(v)], axis=1)
        scores = jnp.where(rows >= cols, dot(qf, kf, 1, 1), 0.0).astype(BF)
        both = dot(scores, v1) + dot(qf, run.astype(BF))
        result = (both[:, :HD] / both[:, HD:]).astype(BF)
        for c in range(cores):
            o_ref[c, n * own : (n + 1) * own, :] = result[c * own : (c + 1) * own]
        run = run + dot(kf, v1, 0, 0)
    state[...] = run


def attend(at, queries, keys, values, states, gain, groups, cores):
    length = queries.shape[0]
    block = length // groups
    rows = block // cores + EXTRA
    tok = pl.BlockSpec((block, HD), lambda i, at: (i, 0))
    return pl.pallas_call(
        attend_kernel,
        grid_spec=pltpu.PrefetchScalarGridSpec(
            num_scalar_prefetch=1,
            grid=(groups,),
            in_specs=[tok, tok, tok, whole(states), whole(gain)],
            out_specs=pl.BlockSpec((cores, rows, HD), lambda i, at: (i, 0, 0)),
            scratch_shapes=[pltpu.VMEM((HD, 2 * HD), F32)],
        ),
        out_shape=jax.ShapeDtypeStruct((groups * cores, rows, HD), BF),
        compiler_params=params(),
    )(at, queries, keys, values, states, gain)


def ranks(routes_t, expand):
    tokens = routes_t.shape[1]
    experts = lax.broadcasted_iota(jnp.int32, (EXPERTS, tokens), 0)
    named = jnp.zeros((EXPERTS, tokens), F32)
    for k in range(TOPK):
        named = named + jnp.where(routes_t[k : k + 1, :] == experts, 1.0, 0.0)
    earlier = lax.broadcasted_iota(jnp.int32, (tokens, tokens), 0)
    later = lax.broadcasted_iota(jnp.int32, (tokens, tokens), 1)
    before = jnp.where(earlier < later, 1.0, 0.0).astype(BF)
    rank = jnp.where(named > 0.0, dot(named.astype(BF), before), -1.0)
    return dot(expand, rank.astype(BF))


def expander():
    row = lax.broadcasted_iota(jnp.int32, (EXPERTS * MAIN, EXPERTS), 0) // MAIN
    col = lax.broadcasted_iota(jnp.int32, (EXPERTS * MAIN, EXPERTS), 1)
    return jnp.where(row == col, 1.0, 0.0).astype(BF)


def picks(rank8):
    row = lax.broadcasted_iota(jnp.int32, rank8.shape, 0)
    main = rank8 == (row % MAIN).astype(F32)
    tail = rank8 == (MAIN + row % TAIL).astype(F32)
    return main, tail, (row % MAIN) // TAIL


def tail_rows(tail, quarter, table):
    width = table.shape[1] // QUART
    total = None
    for q in range(QUART):
        pick = jnp.where(tail & (quarter == q), 1.0, 0.0).astype(BF)
        piece = dot(pick, table[:, q * width : (q + 1) * width])
        total = piece if total is None else total + piece
    return total


BLOCKS = 4


def pack_cot_kernel(routes_ref, weights_ref, cot_ref, out_ref, rank_s, weight_s):
    step = pl.program_id(0)

    @pl.when(step == 0)
    def _():
        expand = expander()
        routes_t = routes_ref[...]
        rank_s[...] = ranks(routes_t, expand)
        experts = lax.broadcasted_iota(jnp.int32, (EXPERTS, routes_t.shape[1]), 0)
        weight = jnp.zeros(experts.shape, F32)
        for k in range(TOPK):
            weight = weight + jnp.where(
                routes_t[k : k + 1, :] == experts, weights_ref[k : k + 1, :], 0.0
            )
        total = jnp.zeros(rank_s.shape, F32)
        for _ in range(3):
            piece = weight.astype(BF)
            total = total + dot(expand, piece)
            weight = weight - piece.astype(F32)
        weight_s[...] = total

    size = EXPERTS * MAIN // BLOCKS
    part = pl.ds(step * size, size)
    weight8 = weight_s[part, :]
    main, tail, quarter = picks(rank_s[part, :])
    table = cot_ref[...]
    scale = jnp.sum(jnp.where(main, weight8, 0.0), axis=1, keepdims=True)
    width = table.shape[1]
    out_ref[:, :width] = (dot(jnp.where(main, 1.0, 0.0).astype(BF), table) * scale).astype(BF)
    scale = jnp.sum(jnp.where(tail, weight8, 0.0), axis=1, keepdims=True)
    out_ref[:, width:] = (tail_rows(tail, quarter, table) * scale).astype(BF)


def packed(width):
    rows = EXPERTS * MAIN
    wide = width + width // QUART
    spec = pl.BlockSpec((rows // BLOCKS, wide), lambda i: (i, 0))
    return spec, jax.ShapeDtypeStruct((rows, wide), BF)


def whole(array):
    return pl.BlockSpec(array.shape, lambda *_: (0,) * array.ndim)


def pack_cot(routes_t, weights_t, cotangent):
    tokens, width = cotangent.shape
    spec, shape = packed(width)
    return pl.pallas_call(
        pack_cot_kernel,
        grid=(BLOCKS,),
        in_specs=[whole(routes_t), whole(weights_t), whole(cotangent)],
        out_specs=spec,
        out_shape=shape,
        scratch_shapes=[pltpu.VMEM((EXPERTS * MAIN, tokens), F32)] * 2,
        compiler_params=params(),
    )(routes_t, weights_t, cotangent)


def project_kernel(place_ref, x_ref, *refs):
    pieces, (mine_ref, ss_ref, *out_refs), keep = refs[:8], refs[8:-1], refs[-1]
    tokens, total = mine_ref.shape
    for d in range(4):
        at = pl.multiple_of(place_ref[d] * tokens, tokens)
        rows = slice(d * tokens, (d + 1) * tokens)
        square = jnp.zeros((tokens, HD), F32)
        for s in range(8):
            source = place_ref[4 + s]
            wide = x_ref[source, pl.ds(at, tokens), :].astype(F32)
            gain = x_ref[source, pl.ds(4 * tokens, 8), :].astype(F32)[:1]
            square = square + wide * wide
            keep[rows, s * HD : (s + 1) * HD] = (wide * gain).astype(BF)
        summed = jnp.broadcast_to(jnp.sum(square, axis=1, keepdims=True), (tokens, HD))
        if d == 0:
            ss_ref[...] = summed
        else:
            high = summed.astype(BF)
            out_refs[d - 1][:, total : total + HD] = high
            out_refs[d - 1][:, total + HD :] = (summed - high.astype(F32)).astype(BF)

    side = 512
    for n in range(total // side):
        cols = slice(n * side, (n + 1) * side)
        both = jnp.zeros((4 * tokens, side), F32)
        for s in range(8):
            both = both + dot(keep[:, s * HD : (s + 1) * HD], pieces[s][:, cols])
        mine_ref[:, cols] = both[:tokens]
        for d in range(1, 4):
            out_refs[d - 1][:, cols] = both[d * tokens : (d + 1) * tokens].astype(BF)


def project(place, x, pieces):
    tokens = (x.shape[1] - EXTRA) // 4
    width = pieces[0].shape[1]
    args = (x,) + tuple(pieces)
    shapes = [(width, F32), (HD, F32)] + [(width + 2 * HD, BF)] * 3
    return pl.pallas_call(
        project_kernel,
        grid_spec=pltpu.PrefetchScalarGridSpec(
            num_scalar_prefetch=1,
            grid=(1,),
            in_specs=[whole(a) for a in args],
            out_specs=[pl.BlockSpec((tokens, n), lambda i, c: (0, 0)) for n, _ in shapes],
            scratch_shapes=[pltpu.VMEM((4 * tokens, 8 * HD), BF)],
        ),
        out_shape=[jax.ShapeDtypeStruct((tokens, n), kind) for n, kind in shapes],
        compiler_params=params(),
    )(place, *args)


def norm_pack_kernel(
    mine_ref, ss_ref, got_a, got_b, got_c, residual_ref, gain_ref, routes_ref,
    hidden_ref, out_ref, rank_s, table_s,
):
    step = pl.program_id(0)

    @pl.when(step == 0)
    def _():
        width = mine_ref.shape[1]
        squares = ss_ref[...]
        projected = mine_ref[...]
        for got in (got_a, got_b, got_c):
            squares = squares + got[:, width : width + HD].astype(F32)
            squares = squares + got[:, width + HD :].astype(F32)
            projected = projected + got[:, :width].astype(F32)
        inverse = lax.rsqrt(squares[:, :1] / (HEADS * HD) + EPS)
        projected = projected * inverse
        hidden = (residual_ref[...].astype(F32) + projected).astype(BF)
        hidden_ref[...] = hidden
        wide = hidden.astype(F32)
        scale = lax.rsqrt(jnp.mean(wide * wide, axis=1, keepdims=True) + EPS)
        table_s[...] = (wide * scale * gain_ref[...].astype(F32)).astype(BF)
        rank_s[...] = ranks(routes_ref[...], expander())

    size = EXPERTS * MAIN // BLOCKS
    main, tail, quarter = picks(rank_s[pl.ds(step * size, size), :])
    table = table_s[...]
    width = table.shape[1]
    out_ref[:, :width] = dot(jnp.where(main, 1.0, 0.0).astype(BF), table).astype(BF)
    out_ref[:, width:] = tail_rows(tail, quarter, table).astype(BF)


def norm_pack(mine, squares, arrived, residual, gain, routes_t):
    tokens, width = residual.shape
    spec, shape = packed(width)
    args = (mine, squares) + tuple(arrived) + (residual, gain, routes_t)
    return pl.pallas_call(
        norm_pack_kernel,
        grid=(BLOCKS,),
        in_specs=[whole(a) for a in args],
        out_specs=[pl.BlockSpec((tokens, width), lambda i: (0, 0)), spec],
        out_shape=[jax.ShapeDtypeStruct((tokens, width), BF), shape],
        scratch_shapes=[
            pltpu.VMEM((EXPERTS * MAIN, tokens), F32),
            pltpu.VMEM((tokens, width), BF),
        ],
        compiler_params=params(),
    )(*args)


ROWS = 256


def untail(tail, keep):
    sources = tail.shape[0] // MAIN
    to = lax.broadcasted_iota(jnp.int32, (sources * TAIL, tail.shape[0]), 0)
    of = lax.broadcasted_iota(jnp.int32, (sources * TAIL, tail.shape[0]), 1)
    width = tail.shape[1]
    for q in range(QUART):
        pick = of == to // TAIL * MAIN + q * TAIL + to % TAIL
        piece = dot(jnp.where(pick, 1.0, 0.0).astype(BF), tail)
        keep(slice(q * width, (q + 1) * width), piece.astype(BF))


def hidden_kernel(rows_ref, tail_ref, down_ref, out_ref, scaled_ref):
    step = pl.program_id(0)
    last = pl.num_programs(0) - 1

    @pl.when(step < last)
    def _():
        out_ref[...] = dot(rows_ref[...], down_ref[...], 1, 1)

    @pl.when(step == last)
    def _():
        def keep(cols, piece):
            scaled_ref[:, cols] = piece

        untail(tail_ref[...], keep)
        out_ref[...] = dot(scaled_ref[...], down_ref[...], 1, 1)


def hidden_grad(cot, down):
    rows = cot.shape[0]
    units, width = down.shape
    blocks = rows // ROWS
    tails = rows // MAIN * TAIL
    return pl.pallas_call(
        hidden_kernel,
        grid=(blocks + 1,),
        in_specs=[
            pl.BlockSpec((ROWS, width), lambda i: (jnp.minimum(i, blocks - 1), 0)),
            pl.BlockSpec((rows, width // QUART), lambda i: (0, QUART)),
            whole(down),
        ],
        out_specs=[
            pl.BlockSpec((ROWS, units), lambda i: (i, 0)),
            pl.BlockSpec((tails, width), lambda i: (0, 0)),
        ],
        out_shape=[
            jax.ShapeDtypeStruct((rows + tails, units), F32),
            jax.ShapeDtypeStruct((tails, width), BF),
        ],
        compiler_params=params(),
    )(cot, cot, down)


def grads_kernel(
    x_ref, tail_ref, back_ref, gate_ref, up_ref, scaled_ref, scaled_tail_ref,
    grad_gate_ref, grad_up_ref, grad_down_ref, x_s, hidden_s, pre_s,
):
    step = pl.program_id(0)
    total, _ = x_s.shape
    units = gate_ref.shape[1]
    blocks = total // ROWS
    part = pl.ds(pl.multiple_of(step * ROWS, ROWS), ROWS)

    @pl.when(step < blocks - 1)
    def _():
        x_s[part, :] = x_ref[...]

    @pl.when(step == blocks - 1)
    def _():
        def keep(cols, piece):
            x_s[total - ROWS :, cols] = piece

        untail(tail_ref[...], keep)

    @pl.when(step < blocks)
    def _():
        x = x_s[part, :]
        piece = 256
        for c in range(units // piece):
            cols = slice(c * piece, (c + 1) * piece)
            gate = dot(x, gate_ref[:, cols])
            up = dot(x, up_ref[:, cols])
            back = back_ref[:, cols]
            sig = jax.nn.sigmoid(gate)
            active = gate * sig
            hidden_s[cols, part] = jnp.transpose(active * up).astype(BF)
            slope = sig * (1.0 + gate * (1.0 - sig))
            pre_s[part, cols] = (back * up * slope).astype(BF)
            pre_s[part, units + c * piece : units + (c + 1) * piece] = (back * active).astype(BF)

    @pl.when(step >= blocks)
    def _():
        block = grad_gate_ref.shape[0]
        x = x_s[:, pl.ds(pl.multiple_of((step - blocks) * block, block), block)]
        both = dot(x, pre_s[...], 0, 0)
        grad_gate_ref[...] = both[:, :units].astype(BF)
        grad_up_ref[...] = both[:, units:].astype(BF)
        main = scaled_ref.shape[0]
        down = dot(hidden_s[:, :main], scaled_ref[...])
        down = down + dot(hidden_s[:, main:], scaled_tail_ref[...])
        grad_down_ref[...] = down.astype(BF)


def expert_grads(moe, cot, scaled_tail, back, gate, up):
    main = moe.shape[0]
    width, units = gate.shape
    total = back.shape[0]
    blocks = total // ROWS
    block = 512
    at_rows = lambda i: (jnp.minimum(i, blocks - 2), 0)
    at_cols = lambda i: (0, jnp.maximum(i - blocks, 0))
    at_out = lambda i: (jnp.maximum(i - blocks, 0), 0)
    return pl.pallas_call(
        grads_kernel,
        grid=(blocks + width // block,),
        in_specs=[
            pl.BlockSpec((ROWS, width), at_rows),
            pl.BlockSpec((main, width // QUART), lambda i: (0, QUART)),
            pl.BlockSpec((ROWS, units), lambda i: (jnp.minimum(i, blocks - 1), 0)),
            whole(gate),
            whole(up),
            pl.BlockSpec((main, block), at_cols),
            pl.BlockSpec((total - main, block), at_cols),
        ],
        out_specs=[
            pl.BlockSpec((block, units), at_out),
            pl.BlockSpec((block, units), at_out),
            pl.BlockSpec((units, block), at_cols),
        ],
        out_shape=[
            jax.ShapeDtypeStruct((width, units), BF),
            jax.ShapeDtypeStruct((width, units), BF),
            jax.ShapeDtypeStruct((units, width), BF),
        ],
        scratch_shapes=[
            pltpu.VMEM((total, width), BF),
            pltpu.VMEM((units, total), BF),
            pltpu.VMEM((total, 2 * units), BF),
        ],
        compiler_params=params(),
    )(moe, moe, back, gate, up, cot, scaled_tail)


def shift(array, axis, by):
    size = lax.axis_size(axis)
    return lax.ppermute(array, axis, [(i, (i + by) % size) for i in range(size)])


def exchange(array, axes):
    return lax.all_to_all(array, axes, split_axis=0, concat_axis=0, tiled=True)


def on_device(
    queries, key_heads, value_heads, out_gain, out_weight, residual, norm_gain,
    routes, route_weights, cotangent, w_gate, w_up, w_down,
):
    n_ctx = lax.axis_size("ctx")
    at = lax.axis_index("ctx").astype(jnp.int32).reshape(1)
    n_x, n_z = lax.axis_size("x"), lax.axis_size("z")
    n_core = lax.axis_size("core")
    near = jnp.array(NEAR, jnp.int32)
    at_x = (lax.axis_index("x") + near) % n_x
    at_z = (lax.axis_index("z") + near) % n_z
    core = lax.axis_index("core")
    sources = at_x[None, :] * n_core + jnp.stack([core, 1 - core])[:, None]
    place = jnp.concatenate([at_z, sources.reshape(-1)]).astype(jnp.int32)

    pieces = [out_weight] + [shift(out_weight, "x", -d) for d in NEAR[1:]]
    pieces += [shift(piece, "core", 1) for piece in pieces]
    states = span_states(key_heads, value_heads, n_ctx)
    states = exchange(states, "ctx")
    attention = attend(
        at, queries, key_heads, value_heads, states, out_gain[None], n_x, n_core
    )
    heads = exchange(attention, ("x", "core"))
    routes_t = routes.T
    cot = pack_cot(routes_t, route_weights.T, cotangent)
    cot, heads = lax.optimization_barrier((cot, heads))
    cot = exchange(cot.reshape(EXPERTS, MAIN, -1), ALL)

    mine, squares, *partial = project(place, heads, pieces)
    arrived = [shift(part, "z", d) for part, d in zip(partial, NEAR[1:])]
    hidden_out, moe = norm_pack(
        mine, squares, arrived, residual, norm_gain[None], routes_t
    )
    moe = exchange(moe.reshape(EXPERTS, MAIN, -1), ALL)

    moe = moe.reshape(EXPERTS * MAIN, -1)
    cot = cot.reshape(EXPERTS * MAIN, -1)
    back, scaled_tail = hidden_grad(cot, w_down[0])
    grads = expert_grads(moe, cot, scaled_tail, back, w_gate[0], w_up[0])
    return (hidden_out,) + tuple(g[None] for g in grads)


def solution(mesh):
    n_ctx, n_head = mesh.devices.shape
    side = 4
    fine = Mesh(mesh.devices.reshape(n_ctx, side, n_head // (2 * side), 2), ALL)
    head = CHIP + ("core",)
    in_specs = (
        P("ctx", head), P("ctx", head), P("ctx", head), P(head), P(head, None),
        P(ALL, None), P(), P(ALL, None), P(ALL, None), P(ALL, None),
        P(ALL, None, None), P(ALL, None, None), P(ALL, None, None),
    )
    out_specs = (P(ALL, None), P(ALL, None, None), P(ALL, None, None), P(ALL, None, None))

    return jax.shard_map(
        on_device, mesh=fine, in_specs=in_specs, out_specs=out_specs, check_vma=False
    )
```

```python
import jax
import jax.numpy as jnp
from jax import lax
from jax.experimental import pallas as pl
from jax.experimental.pallas import tpu as pltpu
from jax.sharding import Mesh, PartitionSpec as P


HD = 128
HEADS = 32
EXPERTS = 128
TOPK = 8
MAIN = 8
TAIL = 2
QUART = 4
EPS = 1e-06
BF = jnp.bfloat16
F32 = jnp.float32
CHIP = ("x", "z")
ALL = ("ctx",) + CHIP + ("core",)
NEAR = (0, -1, 1, 2)


def phi(values):
    wide = values.astype(F32)
    return jnp.where(wide > 0, wide + 1.0, jnp.exp(jnp.minimum(wide, 0.0))).astype(BF)


def dot(a, b, ca=1, cb=0):
    return lax.dot_general(a, b, (((ca,), (cb,)), ((), ())), preferred_element_type=F32)


def params(**kw):
    return pltpu.CompilerParams(vmem_limit_bytes=56 * 1024 * 1024, **kw)


def state_kernel(k_ref, v_ref, o_ref, acc):
    i = pl.program_id(0)

    @pl.when(i == 0)
    def _():
        acc[...] = jnp.zeros_like(acc)

    kf = phi(k_ref[...])
    v = v_ref[...]
    acc[...] += dot(kf, jnp.concatenate([v, jnp.ones_like(v)], axis=1), 0, 0)

    @pl.when(i == pl.num_programs(0) - 1)
    def _():
        for c in range(o_ref.shape[0]):
            o_ref[c] = acc[...].astype(BF)


def span_states(keys, values, n_ctx):
    length = keys.shape[0]
    block = min(1024, length)
    return pl.pallas_call(
        state_kernel,
        grid=(length // block,),
        in_specs=[pl.BlockSpec((block, HD), lambda i: (i, 0))] * 2,
        out_specs=pl.BlockSpec((n_ctx, HD, 2 * HD), lambda i: (0, 0, 0)),
        out_shape=jax.ShapeDtypeStruct((n_ctx, HD, 2 * HD), BF),
        scratch_shapes=[pltpu.VMEM((HD, 2 * HD), F32)],
        compiler_params=params(),
    )(keys, values)


CHUNK = 256
EXTRA = 16


def attend_kernel(at_ref, q_ref, k_ref, v_ref, s_ref, g_ref, o_ref, state):
    @pl.when(pl.program_id(0) == 0)
    def _():
        total = jnp.zeros(state.shape, F32)
        for c in range(s_ref.shape[0]):
            total = total + jnp.where(c < at_ref[0], s_ref[c].astype(F32), 0.0)
        state[...] = total

    rows = lax.broadcasted_iota(jnp.int32, (CHUNK, CHUNK), 0)
    cols = lax.broadcasted_iota(jnp.int32, (CHUNK, CHUNK), 1)
    run = state[...]
    cores, rows_out, _ = o_ref.shape
    own = CHUNK // cores
    for c in range(cores):
        o_ref[c, rows_out - EXTRA :, :] = jnp.broadcast_to(g_ref[...], (EXTRA, HD))
    for n in range(q_ref.shape[0] // CHUNK):
        part = pl.ds(n * CHUNK, CHUNK)
        qf = phi(q_ref[part, :])
        kf = phi(k_ref[part, :])
        v = v_ref[part, :]
        v1 = jnp.concatenate([v, jnp.ones_like(v)], axis=1)
        scores = jnp.where(rows >= cols, dot(qf, kf, 1, 1), 0.0).astype(BF)
        both = dot(scores, v1) + dot(qf, run.astype(BF))
        result = (both[:, :HD] / both[:, HD:]).astype(BF)
        for c in range(cores):
            o_ref[c, n * own : (n + 1) * own, :] = result[c * own : (c + 1) * own]
        run = run + dot(kf, v1, 0, 0)
    state[...] = run


def attend(at, queries, keys, values, states, gain, groups, cores):
    length = queries.shape[0]
    block = length // groups
    rows = block // cores + EXTRA
    tok = pl.BlockSpec((block, HD), lambda i, at: (i, 0))
    return pl.pallas_call(
        attend_kernel,
        grid_spec=pltpu.PrefetchScalarGridSpec(
            num_scalar_prefetch=1,
            grid=(groups,),
            in_specs=[tok, tok, tok, whole(states), whole(gain)],
            out_specs=pl.BlockSpec((cores, rows, HD), lambda i, at: (i, 0, 0)),
            scratch_shapes=[pltpu.VMEM((HD, 2 * HD), F32)],
        ),
        out_shape=jax.ShapeDtypeStruct((groups * cores, rows, HD), BF),
        compiler_params=params(),
    )(at, queries, keys, values, states, gain)


def ranks(routes_t, expand):
    tokens = routes_t.shape[1]
    experts = lax.broadcasted_iota(jnp.int32, (EXPERTS, tokens), 0)
    named = jnp.zeros((EXPERTS, tokens), F32)
    for k in range(TOPK):
        named = named + jnp.where(routes_t[k : k + 1, :] == experts, 1.0, 0.0)
    earlier = lax.broadcasted_iota(jnp.int32, (tokens, tokens), 0)
    later = lax.broadcasted_iota(jnp.int32, (tokens, tokens), 1)
    before = jnp.where(earlier < later, 1.0, 0.0).astype(BF)
    rank = jnp.where(named > 0.0, dot(named.astype(BF), before), -1.0)
    return dot(expand, rank.astype(BF))


def expander():
    row = lax.broadcasted_iota(jnp.int32, (EXPERTS * MAIN, EXPERTS), 0) // MAIN
    col = lax.broadcasted_iota(jnp.int32, (EXPERTS * MAIN, EXPERTS), 1)
    return jnp.where(row == col, 1.0, 0.0).astype(BF)


def picks(rank8):
    row = lax.broadcasted_iota(jnp.int32, rank8.shape, 0)
    main = rank8 == (row % MAIN).astype(F32)
    tail = rank8 == (MAIN + row % TAIL).astype(F32)
    return main, tail, (row % MAIN) // TAIL


def tail_rows(tail, quarter, table):
    width = table.shape[1] // QUART
    total = None
    for q in range(QUART):
        pick = jnp.where(tail & (quarter == q), 1.0, 0.0).astype(BF)
        piece = dot(pick, table[:, q * width : (q + 1) * width])
        total = piece if total is None else total + piece
    return total


BLOCKS = 4


def pack_cot_kernel(routes_ref, weights_ref, cot_ref, first_ref, rest_ref, rank_s, weight_s):
    step = pl.program_id(0)

    @pl.when(step == 0)
    def _():
        expand = expander()
        routes_t = routes_ref[...]
        rank_s[...] = ranks(routes_t, expand)
        experts = lax.broadcasted_iota(jnp.int32, (EXPERTS, routes_t.shape[1]), 0)
        weight = jnp.zeros(experts.shape, F32)
        for k in range(TOPK):
            weight = weight + jnp.where(
                routes_t[k : k + 1, :] == experts, weights_ref[k : k + 1, :], 0.0
            )
        total = jnp.zeros(rank_s.shape, F32)
        for _ in range(3):
            piece = weight.astype(BF)
            total = total + dot(expand, piece)
            weight = weight - piece.astype(F32)
        weight_s[...] = total

    size = EXPERTS * MAIN // BLOCKS
    part = pl.ds(step * size, size)
    weight8 = weight_s[part, :]
    main, tail, quarter = picks(rank_s[part, :])
    table = cot_ref[...]
    scale = jnp.sum(jnp.where(main, weight8, 0.0), axis=1, keepdims=True)
    half = first_ref.shape[1]
    rows = (dot(jnp.where(main, 1.0, 0.0).astype(BF), table) * scale).astype(BF)
    first_ref[...] = rows[:, :half]
    rest_ref[:, :half] = rows[:, half:]
    scale = jnp.sum(jnp.where(tail, weight8, 0.0), axis=1, keepdims=True)
    rest_ref[:, half:] = (tail_rows(tail, quarter, table) * scale).astype(BF)


def packed(main, tail):
    rows = EXPERTS * MAIN
    wide = main + tail
    spec = pl.BlockSpec((rows // BLOCKS, wide), lambda i: (i, 0))
    return spec, jax.ShapeDtypeStruct((rows, wide), BF)


def whole(array):
    return pl.BlockSpec(array.shape, lambda *_: (0,) * array.ndim)


def pack_cot(routes_t, weights_t, cotangent):
    tokens, width = cotangent.shape
    first, rest = packed(width // 2, 0), packed(width // 2, width // QUART)
    return pl.pallas_call(
        pack_cot_kernel,
        grid=(BLOCKS,),
        in_specs=[whole(routes_t), whole(weights_t), whole(cotangent)],
        out_specs=[first[0], rest[0]],
        out_shape=[first[1], rest[1]],
        scratch_shapes=[pltpu.VMEM((EXPERTS * MAIN, tokens), F32)] * 2,
        compiler_params=params(),
    )(routes_t, weights_t, cotangent)


def project_kernel(place_ref, x_ref, *refs):
    pieces, (mine_ref, ss_ref, *out_refs), keep = refs[:8], refs[8:-1], refs[-1]
    tokens, total = mine_ref.shape
    for d in range(4):
        at = pl.multiple_of(place_ref[d] * tokens, tokens)
        rows = slice(d * tokens, (d + 1) * tokens)
        square = jnp.zeros((tokens, HD), F32)
        for s in range(8):
            source = place_ref[4 + s]
            wide = x_ref[source, pl.ds(at, tokens), :].astype(F32)
            gain = x_ref[source, pl.ds(4 * tokens, 8), :].astype(F32)[:1]
            square = square + wide * wide
            keep[rows, s * HD : (s + 1) * HD] = (wide * gain).astype(BF)
        summed = jnp.broadcast_to(jnp.sum(square, axis=1, keepdims=True), (tokens, HD))
        if d == 0:
            ss_ref[...] = summed
        else:
            high = summed.astype(BF)
            out_refs[d - 1][:, total : total + HD] = high
            out_refs[d - 1][:, total + HD :] = (summed - high.astype(F32)).astype(BF)

    side = 512
    for n in range(total // side):
        cols = slice(n * side, (n + 1) * side)
        both = jnp.zeros((4 * tokens, side), F32)
        for s in range(8):
            both = both + dot(keep[:, s * HD : (s + 1) * HD], pieces[s][:, cols])
        mine_ref[:, cols] = both[:tokens]
        for d in range(1, 4):
            out_refs[d - 1][:, cols] = both[d * tokens : (d + 1) * tokens].astype(BF)


def project(place, x, pieces):
    tokens = (x.shape[1] - EXTRA) // 4
    width = pieces[0].shape[1]
    args = (x,) + tuple(pieces)
    shapes = [(width, F32), (HD, F32)] + [(width + 2 * HD, BF)] * 3
    return pl.pallas_call(
        project_kernel,
        grid_spec=pltpu.PrefetchScalarGridSpec(
            num_scalar_prefetch=1,
            grid=(1,),
            in_specs=[whole(a) for a in args],
            out_specs=[pl.BlockSpec((tokens, n), lambda i, c: (0, 0)) for n, _ in shapes],
            scratch_shapes=[pltpu.VMEM((4 * tokens, 8 * HD), BF)],
        ),
        out_shape=[jax.ShapeDtypeStruct((tokens, n), kind) for n, kind in shapes],
        compiler_params=params(),
    )(place, *args)


def norm_pack_kernel(
    mine_ref, ss_ref, got_a, got_b, got_c, residual_ref, gain_ref, routes_ref,
    hidden_ref, out_ref, rank_s, table_s,
):
    step = pl.program_id(0)

    @pl.when(step == 0)
    def _():
        width = mine_ref.shape[1]
        squares = ss_ref[...]
        projected = mine_ref[...]
        for got in (got_a, got_b, got_c):
            squares = squares + got[:, width : width + HD].astype(F32)
            squares = squares + got[:, width + HD :].astype(F32)
            projected = projected + got[:, :width].astype(F32)
        inverse = lax.rsqrt(squares[:, :1] / (HEADS * HD) + EPS)
        projected = projected * inverse
        hidden = (residual_ref[...].astype(F32) + projected).astype(BF)
        hidden_ref[...] = hidden
        wide = hidden.astype(F32)
        scale = lax.rsqrt(jnp.mean(wide * wide, axis=1, keepdims=True) + EPS)
        table_s[...] = (wide * scale * gain_ref[...].astype(F32)).astype(BF)
        rank_s[...] = ranks(routes_ref[...], expander())

    size = EXPERTS * MAIN // BLOCKS
    main, tail, quarter = picks(rank_s[pl.ds(step * size, size), :])
    table = table_s[...]
    width = table.shape[1]
    out_ref[:, :width] = dot(jnp.where(main, 1.0, 0.0).astype(BF), table).astype(BF)
    out_ref[:, width:] = tail_rows(tail, quarter, table).astype(BF)


def norm_pack(mine, squares, arrived, residual, gain, routes_t):
    tokens, width = residual.shape
    spec, shape = packed(width, width // QUART)
    args = (mine, squares) + tuple(arrived) + (residual, gain, routes_t)
    return pl.pallas_call(
        norm_pack_kernel,
        grid=(BLOCKS,),
        in_specs=[whole(a) for a in args],
        out_specs=[pl.BlockSpec((tokens, width), lambda i: (0, 0)), spec],
        out_shape=[jax.ShapeDtypeStruct((tokens, width), BF), shape],
        scratch_shapes=[
            pltpu.VMEM((EXPERTS * MAIN, tokens), F32),
            pltpu.VMEM((tokens, width), BF),
        ],
        compiler_params=params(),
    )(*args)


ROWS = 256


def untail(tail, keep):
    sources = tail.shape[0] // MAIN
    to = lax.broadcasted_iota(jnp.int32, (sources * TAIL, tail.shape[0]), 0)
    of = lax.broadcasted_iota(jnp.int32, (sources * TAIL, tail.shape[0]), 1)
    width = tail.shape[1]
    for q in range(QUART):
        pick = of == to // TAIL * MAIN + q * TAIL + to % TAIL
        piece = dot(jnp.where(pick, 1.0, 0.0).astype(BF), tail)
        keep(slice(q * width, (q + 1) * width), piece.astype(BF))


def hidden_kernel(first_ref, second_ref, tail_ref, down_ref, out_ref, scaled_ref):
    step = pl.program_id(0)
    last = pl.num_programs(0) - 1

    @pl.when(step < last)
    def _():
        half = first_ref.shape[1]
        total = dot(first_ref[...], down_ref[:, :half], 1, 1)
        out_ref[...] = total + dot(second_ref[...], down_ref[:, half:], 1, 1)

    @pl.when(step == last)
    def _():
        def keep(cols, piece):
            scaled_ref[:, cols] = piece

        untail(tail_ref[...], keep)
        out_ref[...] = dot(scaled_ref[...], down_ref[...], 1, 1)


def hidden_grad(first, rest, down):
    rows, half = first.shape
    units, width = down.shape
    blocks = rows // ROWS
    tails = rows // MAIN * TAIL
    part = pl.BlockSpec((ROWS, half), lambda i: (jnp.minimum(i, blocks - 1), 0))
    return pl.pallas_call(
        hidden_kernel,
        grid=(blocks + 1,),
        in_specs=[
            part,
            part,
            pl.BlockSpec((rows, width // QUART), lambda i: (0, QUART // 2)),
            whole(down),
        ],
        out_specs=[
            pl.BlockSpec((ROWS, units), lambda i: (i, 0)),
            pl.BlockSpec((tails, width), lambda i: (0, 0)),
        ],
        out_shape=[
            jax.ShapeDtypeStruct((rows + tails, units), F32),
            jax.ShapeDtypeStruct((tails, width), BF),
        ],
        compiler_params=params(),
    )(first, rest, rest, down)


def grads_kernel(
    x_ref, tail_ref, back_ref, gate_ref, up_ref, first_ref, second_ref, scaled_tail_ref,
    grad_gate_ref, grad_up_ref, grad_down_ref, x_s, hidden_s, pre_s,
):
    step = pl.program_id(0)
    total, _ = x_s.shape
    units = gate_ref.shape[1]
    blocks = total // ROWS
    part = pl.ds(pl.multiple_of(step * ROWS, ROWS), ROWS)

    @pl.when(step < blocks - 1)
    def _():
        x_s[part, :] = x_ref[...]

    @pl.when(step == blocks - 1)
    def _():
        def keep(cols, piece):
            x_s[total - ROWS :, cols] = piece

        untail(tail_ref[...], keep)

    @pl.when(step < blocks)
    def _():
        x = x_s[part, :]
        piece = 256
        for c in range(units // piece):
            cols = slice(c * piece, (c + 1) * piece)
            gate = dot(x, gate_ref[:, cols])
            up = dot(x, up_ref[:, cols])
            back = back_ref[:, cols]
            sig = jax.nn.sigmoid(gate)
            active = gate * sig
            hidden_s[cols, part] = jnp.transpose(active * up).astype(BF)
            slope = sig * (1.0 + gate * (1.0 - sig))
            pre_s[part, cols] = (back * up * slope).astype(BF)
            pre_s[part, units + c * piece : units + (c + 1) * piece] = (back * active).astype(BF)

    @pl.when(step >= blocks)
    def _():
        block = grad_gate_ref.shape[0]
        x = x_s[:, pl.ds(pl.multiple_of((step - blocks) * block, block), block)]
        both = dot(x, pre_s[...], 0, 0)
        grad_gate_ref[...] = both[:, :units].astype(BF)
        grad_up_ref[...] = both[:, units:].astype(BF)
        main = first_ref.shape[0]
        rest = dot(hidden_s[:, main:], scaled_tail_ref[...])
        middle = blocks + (pl.num_programs(0) - blocks) // 2

        @pl.when(step < middle)
        def _():
            grad_down_ref[...] = (dot(hidden_s[:, :main], first_ref[...]) + rest).astype(BF)

        @pl.when(step >= middle)
        def _():
            grad_down_ref[...] = (dot(hidden_s[:, :main], second_ref[...]) + rest).astype(BF)


def expert_grads(moe, first, rest, scaled_tail, back, gate, up):
    main = moe.shape[0]
    width, units = gate.shape
    total = back.shape[0]
    blocks = total // ROWS
    block = 512
    halves = width // 2 // block
    at_rows = lambda i: (jnp.minimum(i, blocks - 2), 0)
    at_cols = lambda i: (0, jnp.maximum(i - blocks, 0))
    at_out = lambda i: (jnp.maximum(i - blocks, 0), 0)
    return pl.pallas_call(
        grads_kernel,
        grid=(blocks + width // block,),
        in_specs=[
            pl.BlockSpec((ROWS, width), at_rows),
            pl.BlockSpec((main, width // QUART), lambda i: (0, QUART)),
            pl.BlockSpec((ROWS, units), lambda i: (jnp.minimum(i, blocks - 1), 0)),
            whole(gate),
            whole(up),
            pl.BlockSpec((main, block), lambda i: (0, jnp.clip(i - blocks, 0, halves - 1))),
            pl.BlockSpec((main, block), lambda i: (0, jnp.maximum(i - blocks - halves, 0))),
            pl.BlockSpec((total - main, block), at_cols),
        ],
        out_specs=[
            pl.BlockSpec((block, units), at_out),
            pl.BlockSpec((block, units), at_out),
            pl.BlockSpec((units, block), at_cols),
        ],
        out_shape=[
            jax.ShapeDtypeStruct((width, units), BF),
            jax.ShapeDtypeStruct((width, units), BF),
            jax.ShapeDtypeStruct((units, width), BF),
        ],
        scratch_shapes=[
            pltpu.VMEM((total, width), BF),
            pltpu.VMEM((units, total), BF),
            pltpu.VMEM((total, 2 * units), BF),
        ],
        compiler_params=params(),
    )(moe, moe, back, gate, up, first, rest, scaled_tail)


def shift(array, axis, by):
    size = lax.axis_size(axis)
    return lax.ppermute(array, axis, [(i, (i + by) % size) for i in range(size)])


def exchange(array, axes):
    return lax.all_to_all(array, axes, split_axis=0, concat_axis=0, tiled=True)


def on_device(
    queries, key_heads, value_heads, out_gain, out_weight, residual, norm_gain,
    routes, route_weights, cotangent, w_gate, w_up, w_down,
):
    n_ctx = lax.axis_size("ctx")
    at = lax.axis_index("ctx").astype(jnp.int32).reshape(1)
    n_x, n_z = lax.axis_size("x"), lax.axis_size("z")
    n_core = lax.axis_size("core")
    near = jnp.array(NEAR, jnp.int32)
    at_x = (lax.axis_index("x") + near) % n_x
    at_z = (lax.axis_index("z") + near) % n_z
    core = lax.axis_index("core")
    sources = at_x[None, :] * n_core + jnp.stack([core, 1 - core])[:, None]
    place = jnp.concatenate([at_z, sources.reshape(-1)]).astype(jnp.int32)

    pieces = [out_weight] + [shift(out_weight, "x", -d) for d in NEAR[1:]]
    pieces += [shift(piece, "core", 1) for piece in pieces]
    states = span_states(key_heads, value_heads, n_ctx)
    states = exchange(states, "ctx")
    attention = attend(
        at, queries, key_heads, value_heads, states, out_gain[None], n_x, n_core
    )
    heads = exchange(attention, ("x", "core"))
    routes_t = routes.T
    first, rest = pack_cot(routes_t, route_weights.T, cotangent)
    first, heads = lax.optimization_barrier((first, heads))
    first = exchange(first.reshape(EXPERTS, MAIN, -1), ALL)

    mine, squares, *partial = project(place, heads, pieces)
    rest, first, _ = lax.optimization_barrier((rest, first, partial))
    arrived = [shift(part, "z", d) for part, d in zip(partial, NEAR[1:])]
    rest = exchange(rest.reshape(EXPERTS, MAIN, -1), ALL)
    hidden_out, moe = norm_pack(
        mine, squares, arrived, residual, norm_gain[None], routes_t
    )
    moe = exchange(moe.reshape(EXPERTS, MAIN, -1), ALL)

    moe = moe.reshape(EXPERTS * MAIN, -1)
    first = first.reshape(EXPERTS * MAIN, -1)
    rest = rest.reshape(EXPERTS * MAIN, -1)
    back, scaled_tail = hidden_grad(first, rest, w_down[0])
    grads = expert_grads(moe, first, rest, scaled_tail, back, w_gate[0], w_up[0])
    return (hidden_out,) + tuple(g[None] for g in grads)


def solution(mesh):
    n_ctx, n_head = mesh.devices.shape
    side = 4
    fine = Mesh(mesh.devices.reshape(n_ctx, side, n_head // (2 * side), 2), ALL)
    head = CHIP + ("core",)
    in_specs = (
        P("ctx", head), P("ctx", head), P("ctx", head), P(head), P(head, None),
        P(ALL, None), P(), P(ALL, None), P(ALL, None), P(ALL, None),
        P(ALL, None, None), P(ALL, None, None), P(ALL, None, None),
    )
    out_specs = (P(ALL, None), P(ALL, None, None), P(ALL, None, None), P(ALL, None, None))

    return jax.shard_map(
        on_device, mesh=fine, in_specs=in_specs, out_specs=out_specs, check_vma=False
    )
```

```python
import jax
import jax.numpy as jnp
from jax import lax
from jax.experimental import pallas as pl
from jax.experimental.pallas import tpu as pltpu
from jax.sharding import Mesh, PartitionSpec as P


HD = 128
HEADS = 32
EXPERTS = 128
TOPK = 8
MAIN = 8
TAIL = 2
QUART = 4
EPS = 1e-06
BF = jnp.bfloat16
F32 = jnp.float32
CHIP = ("x", "z")
ALL = ("ctx",) + CHIP + ("core",)
NEAR = (0, -1, 1, 2)


def phi(values):
    wide = values.astype(F32)
    return jnp.where(wide > 0, wide + 1.0, jnp.exp(jnp.minimum(wide, 0.0))).astype(BF)


def dot(a, b, ca=1, cb=0):
    return lax.dot_general(a, b, (((ca,), (cb,)), ((), ())), preferred_element_type=F32)


def params(limit=28):
    return pltpu.CompilerParams(vmem_limit_bytes=limit * 1024 * 1024)


def state_kernel(k_ref, v_ref, o_ref, acc):
    i = pl.program_id(0)

    @pl.when(i == 0)
    def _():
        acc[...] = jnp.zeros_like(acc)

    kf = phi(k_ref[...])
    v = v_ref[...]
    acc[...] += dot(kf, jnp.concatenate([v, jnp.ones_like(v)], axis=1), 0, 0)

    @pl.when(i == pl.num_programs(0) - 1)
    def _():
        for c in range(o_ref.shape[0]):
            o_ref[c] = acc[...].astype(BF)


def span_states(keys, values, n_ctx):
    length = keys.shape[0]
    block = min(1024, length)
    return pl.pallas_call(
        state_kernel,
        grid=(length // block,),
        in_specs=[pl.BlockSpec((block, HD), lambda i: (i, 0))] * 2,
        out_specs=pl.BlockSpec((n_ctx, HD, 2 * HD), lambda i: (0, 0, 0)),
        out_shape=jax.ShapeDtypeStruct((n_ctx, HD, 2 * HD), BF),
        scratch_shapes=[pltpu.VMEM((HD, 2 * HD), F32)],
        compiler_params=params(),
    )(keys, values)


CHUNK = 256
EXTRA = 16


def attend_kernel(at_ref, q_ref, k_ref, v_ref, s_ref, g_ref, o_ref, state):
    @pl.when(pl.program_id(0) == 0)
    def _():
        total = jnp.zeros(state.shape, F32)
        for c in range(s_ref.shape[0]):
            total = total + jnp.where(c < at_ref[0], s_ref[c].astype(F32), 0.0)
        state[...] = total

    rows = lax.broadcasted_iota(jnp.int32, (CHUNK, CHUNK), 0)
    cols = lax.broadcasted_iota(jnp.int32, (CHUNK, CHUNK), 1)
    run = state[...]
    cores, rows_out, _ = o_ref.shape
    own = CHUNK // cores
    for c in range(cores):
        o_ref[c, rows_out - EXTRA :, :] = jnp.broadcast_to(g_ref[...], (EXTRA, HD))
    for n in range(q_ref.shape[0] // CHUNK):
        part = pl.ds(n * CHUNK, CHUNK)
        qf = phi(q_ref[part, :])
        kf = phi(k_ref[part, :])
        v = v_ref[part, :]
        v1 = jnp.concatenate([v, jnp.ones_like(v)], axis=1)
        scores = jnp.where(rows >= cols, dot(qf, kf, 1, 1), 0.0).astype(BF)
        both = dot(scores, v1) + dot(qf, run.astype(BF))
        result = (both[:, :HD] / both[:, HD:]).astype(BF)
        for c in range(cores):
            o_ref[c, n * own : (n + 1) * own, :] = result[c * own : (c + 1) * own]
        run = run + dot(kf, v1, 0, 0)
    state[...] = run


def attend(at, queries, keys, values, states, gain, groups, cores):
    length = queries.shape[0]
    block = length // groups
    rows = block // cores + EXTRA
    tok = pl.BlockSpec((block, HD), lambda i, at: (i, 0))
    return pl.pallas_call(
        attend_kernel,
        grid_spec=pltpu.PrefetchScalarGridSpec(
            num_scalar_prefetch=1,
            grid=(groups,),
            in_specs=[tok, tok, tok, whole(states), whole(gain)],
            out_specs=pl.BlockSpec((cores, rows, HD), lambda i, at: (i, 0, 0)),
            scratch_shapes=[pltpu.VMEM((HD, 2 * HD), F32)],
        ),
        out_shape=jax.ShapeDtypeStruct((groups * cores, rows, HD), BF),
        compiler_params=params(),
    )(at, queries, keys, values, states, gain)


def ranks(routes_t, expand):
    tokens = routes_t.shape[1]
    experts = lax.broadcasted_iota(jnp.int32, (EXPERTS, tokens), 0)
    named = jnp.zeros((EXPERTS, tokens), F32)
    for k in range(TOPK):
        named = named + jnp.where(routes_t[k : k + 1, :] == experts, 1.0, 0.0)
    earlier = lax.broadcasted_iota(jnp.int32, (tokens, tokens), 0)
    later = lax.broadcasted_iota(jnp.int32, (tokens, tokens), 1)
    before = jnp.where(earlier < later, 1.0, 0.0).astype(BF)
    rank = jnp.where(named > 0.0, dot(named.astype(BF), before), -1.0)
    return dot(expand, rank.astype(BF))


def expander():
    row = lax.broadcasted_iota(jnp.int32, (EXPERTS * MAIN, EXPERTS), 0) // MAIN
    col = lax.broadcasted_iota(jnp.int32, (EXPERTS * MAIN, EXPERTS), 1)
    return jnp.where(row == col, 1.0, 0.0).astype(BF)


def picks(rank8):
    row = lax.broadcasted_iota(jnp.int32, rank8.shape, 0)
    main = rank8 == (row % MAIN).astype(F32)
    tail = rank8 == (MAIN + row % TAIL).astype(F32)
    return main, tail, (row % MAIN) // TAIL


def tail_rows(tail, quarter, table):
    width = table.shape[1] // QUART
    total = None
    for q in range(QUART):
        pick = jnp.where(tail & (quarter == q), 1.0, 0.0).astype(BF)
        piece = dot(pick, table[:, q * width : (q + 1) * width])
        total = piece if total is None else total + piece
    return total


BLOCKS = 4


def pack_cot_kernel(routes_ref, weights_ref, cot_ref, out_ref, rank_s, weight_s):
    step = pl.program_id(0)

    @pl.when(step == 0)
    def _():
        expand = expander()
        routes_t = routes_ref[...]
        rank_s[...] = ranks(routes_t, expand)
        experts = lax.broadcasted_iota(jnp.int32, (EXPERTS, routes_t.shape[1]), 0)
        weight = jnp.zeros(experts.shape, F32)
        for k in range(TOPK):
            weight = weight + jnp.where(
                routes_t[k : k + 1, :] == experts, weights_ref[k : k + 1, :], 0.0
            )
        total = jnp.zeros(rank_s.shape, F32)
        for _ in range(3):
            piece = weight.astype(BF)
            total = total + dot(expand, piece)
            weight = weight - piece.astype(F32)
        weight_s[...] = total

    size = EXPERTS * MAIN // BLOCKS
    part = pl.ds(step * size, size)
    weight8 = weight_s[part, :]
    main, tail, quarter = picks(rank_s[part, :])
    table = cot_ref[...]
    scale = jnp.sum(jnp.where(main, weight8, 0.0), axis=1, keepdims=True)
    width = table.shape[1]
    out_ref[:, :width] = (dot(jnp.where(main, 1.0, 0.0).astype(BF), table) * scale).astype(BF)
    scale = jnp.sum(jnp.where(tail, weight8, 0.0), axis=1, keepdims=True)
    out_ref[:, width:] = (tail_rows(tail, quarter, table) * scale).astype(BF)


def packed(width):
    rows = EXPERTS * MAIN
    wide = width + width // QUART
    spec = pl.BlockSpec((rows // BLOCKS, wide), lambda i: (i, 0))
    return spec, jax.ShapeDtypeStruct((rows, wide), BF)


def whole(array):
    return pl.BlockSpec(array.shape, lambda *_: (0,) * array.ndim)


def pack_cot(routes_t, weights_t, cotangent):
    tokens, width = cotangent.shape
    spec, shape = packed(width)
    return pl.pallas_call(
        pack_cot_kernel,
        grid=(BLOCKS,),
        in_specs=[whole(routes_t), whole(weights_t), whole(cotangent)],
        out_specs=spec,
        out_shape=shape,
        scratch_shapes=[pltpu.VMEM((EXPERTS * MAIN, tokens), F32)] * 2,
        compiler_params=params(),
    )(routes_t, weights_t, cotangent)


def project_kernel(place_ref, x_ref, *refs):
    pieces, (mine_ref, ss_ref, *out_refs), keep = refs[:8], refs[8:-1], refs[-1]
    tokens, total = mine_ref.shape
    for d in range(4):
        at = pl.multiple_of(place_ref[d] * tokens, tokens)
        rows = slice(d * tokens, (d + 1) * tokens)
        square = jnp.zeros((tokens, HD), F32)
        for s in range(8):
            source = place_ref[4 + s]
            wide = x_ref[source, pl.ds(at, tokens), :].astype(F32)
            gain = x_ref[source, pl.ds(4 * tokens, 8), :].astype(F32)[:1]
            square = square + wide * wide
            keep[rows, s * HD : (s + 1) * HD] = (wide * gain).astype(BF)
        summed = jnp.broadcast_to(jnp.sum(square, axis=1, keepdims=True), (tokens, HD))
        if d == 0:
            ss_ref[...] = summed
        else:
            high = summed.astype(BF)
            out_refs[d - 1][:, total : total + HD] = high
            out_refs[d - 1][:, total + HD :] = (summed - high.astype(F32)).astype(BF)

    side = 512
    for n in range(total // side):
        cols = slice(n * side, (n + 1) * side)
        both = jnp.zeros((4 * tokens, side), F32)
        for s in range(8):
            both = both + dot(keep[:, s * HD : (s + 1) * HD], pieces[s][:, cols])
        mine_ref[:, cols] = both[:tokens]
        for d in range(1, 4):
            out_refs[d - 1][:, cols] = both[d * tokens : (d + 1) * tokens].astype(BF)


def project(place, x, pieces):
    tokens = (x.shape[1] - EXTRA) // 4
    width = pieces[0].shape[1]
    args = (x,) + tuple(pieces)
    shapes = [(width, F32), (HD, F32)] + [(width + 2 * HD, BF)] * 3
    return pl.pallas_call(
        project_kernel,
        grid_spec=pltpu.PrefetchScalarGridSpec(
            num_scalar_prefetch=1,
            grid=(1,),
            in_specs=[whole(a) for a in args],
            out_specs=[pl.BlockSpec((tokens, n), lambda i, c: (0, 0)) for n, _ in shapes],
            scratch_shapes=[pltpu.VMEM((4 * tokens, 8 * HD), BF)],
        ),
        out_shape=[jax.ShapeDtypeStruct((tokens, n), kind) for n, kind in shapes],
        compiler_params=params(),
    )(place, *args)


def norm_pack_kernel(
    mine_ref, ss_ref, got_a, got_b, got_c, residual_ref, gain_ref, routes_ref,
    hidden_ref, out_ref, rank_s, table_s,
):
    step = pl.program_id(0)

    @pl.when(step == 0)
    def _():
        width = mine_ref.shape[1]
        squares = ss_ref[...]
        projected = mine_ref[...]
        for got in (got_a, got_b, got_c):
            squares = squares + got[:, width : width + HD].astype(F32)
            squares = squares + got[:, width + HD :].astype(F32)
            projected = projected + got[:, :width].astype(F32)
        inverse = lax.rsqrt(squares[:, :1] / (HEADS * HD) + EPS)
        projected = projected * inverse
        hidden = (residual_ref[...].astype(F32) + projected).astype(BF)
        hidden_ref[...] = hidden
        wide = hidden.astype(F32)
        scale = lax.rsqrt(jnp.mean(wide * wide, axis=1, keepdims=True) + EPS)
        table_s[...] = (wide * scale * gain_ref[...].astype(F32)).astype(BF)
        rank_s[...] = ranks(routes_ref[...], expander())

    size = EXPERTS * MAIN // BLOCKS
    main, tail, quarter = picks(rank_s[pl.ds(step * size, size), :])
    table = table_s[...]
    width = table.shape[1]
    out_ref[:, :width] = dot(jnp.where(main, 1.0, 0.0).astype(BF), table).astype(BF)
    out_ref[:, width:] = tail_rows(tail, quarter, table).astype(BF)


def norm_pack(mine, squares, arrived, residual, gain, routes_t):
    tokens, width = residual.shape
    spec, shape = packed(width)
    args = (mine, squares) + tuple(arrived) + (residual, gain, routes_t)
    return pl.pallas_call(
        norm_pack_kernel,
        grid=(BLOCKS,),
        in_specs=[whole(a) for a in args],
        out_specs=[pl.BlockSpec((tokens, width), lambda i: (0, 0)), spec],
        out_shape=[jax.ShapeDtypeStruct((tokens, width), BF), shape],
        scratch_shapes=[
            pltpu.VMEM((EXPERTS * MAIN, tokens), F32),
            pltpu.VMEM((tokens, width), BF),
        ],
        compiler_params=params(),
    )(*args)


ROWS = 256


def untail(tail, keep):
    sources = tail.shape[0] // MAIN
    to = lax.broadcasted_iota(jnp.int32, (sources * TAIL, tail.shape[0]), 0)
    of = lax.broadcasted_iota(jnp.int32, (sources * TAIL, tail.shape[0]), 1)
    width = tail.shape[1]
    for q in range(QUART):
        pick = of == to // TAIL * MAIN + q * TAIL + to % TAIL
        piece = dot(jnp.where(pick, 1.0, 0.0).astype(BF), tail)
        keep(slice(q * width, (q + 1) * width), piece.astype(BF))


def hidden_kernel(rows_ref, tail_ref, down_ref, out_ref, scaled_ref):
    step = pl.program_id(0)
    last = pl.num_programs(0) - 1

    @pl.when(step < last)
    def _():
        out_ref[...] = dot(rows_ref[...], down_ref[...], 1, 1)

    @pl.when(step == last)
    def _():
        def keep(cols, piece):
            scaled_ref[:, cols] = piece

        untail(tail_ref[...], keep)
        out_ref[...] = dot(scaled_ref[...], down_ref[...], 1, 1)


def hidden_grad(cot, down):
    rows = cot.shape[0]
    units, width = down.shape
    blocks = rows // ROWS
    tails = rows // MAIN * TAIL
    return pl.pallas_call(
        hidden_kernel,
        grid=(blocks + 1,),
        in_specs=[
            pl.BlockSpec((ROWS, width), lambda i: (jnp.minimum(i, blocks - 1), 0)),
            pl.BlockSpec((rows, width // QUART), lambda i: (0, QUART)),
            whole(down),
        ],
        out_specs=[
            pl.BlockSpec((ROWS, units), lambda i: (i, 0)),
            pl.BlockSpec((tails, width), lambda i: (0, 0)),
        ],
        out_shape=[
            jax.ShapeDtypeStruct((rows + tails, units), F32),
            jax.ShapeDtypeStruct((tails, width), BF),
        ],
        compiler_params=params(),
    )(cot, cot, down)


def grads_kernel(
    x_ref, tail_ref, back_ref, gate_ref, up_ref, scaled_ref, scaled_tail_ref,
    grad_gate_ref, grad_up_ref, grad_down_ref, x_s, hidden_s, pre_s,
):
    step = pl.program_id(0)
    total, _ = x_s.shape
    units = gate_ref.shape[1]
    blocks = total // ROWS
    part = pl.ds(pl.multiple_of(step * ROWS, ROWS), ROWS)

    @pl.when(step < blocks - 1)
    def _():
        x_s[part, :] = x_ref[...]

    @pl.when(step == blocks - 1)
    def _():
        def keep(cols, piece):
            x_s[total - ROWS :, cols] = piece

        untail(tail_ref[...], keep)

    @pl.when(step < blocks)
    def _():
        x = x_s[part, :]
        piece = 256
        for c in range(units // piece):
            cols = slice(c * piece, (c + 1) * piece)
            gate = dot(x, gate_ref[:, cols])
            up = dot(x, up_ref[:, cols])
            back = back_ref[:, cols]
            sig = jax.nn.sigmoid(gate)
            active = gate * sig
            hidden_s[cols, part] = jnp.transpose(active * up).astype(BF)
            slope = sig * (1.0 + gate * (1.0 - sig))
            pre_s[part, cols] = (back * up * slope).astype(BF)
            pre_s[part, units + c * piece : units + (c + 1) * piece] = (back * active).astype(BF)

    @pl.when(step >= blocks)
    def _():
        block = grad_gate_ref.shape[0]
        x = x_s[:, pl.ds(pl.multiple_of((step - blocks) * block, block), block)]
        both = dot(x, pre_s[...], 0, 0)
        grad_gate_ref[...] = both[:, :units].astype(BF)
        grad_up_ref[...] = both[:, units:].astype(BF)
        main = scaled_ref.shape[0]
        down = dot(hidden_s[:, :main], scaled_ref[...])
        down = down + dot(hidden_s[:, main:], scaled_tail_ref[...])
        grad_down_ref[...] = down.astype(BF)


def held(array):
    return pltpu.with_memory_space_constraint(array, pltpu.VMEM)


def expert_grads(moe, cot, scaled_tail, back, gate, up):
    main = moe.shape[0]
    width, units = gate.shape
    total = back.shape[0]
    blocks = total // ROWS
    block = 512
    at_rows = lambda i: (jnp.minimum(i, blocks - 2), 0)
    at_cols = lambda i: (0, jnp.maximum(i - blocks, 0))
    at_out = lambda i: (jnp.maximum(i - blocks, 0), 0)
    return pl.pallas_call(
        grads_kernel,
        grid=(blocks + width // block,),
        in_specs=[
            pl.BlockSpec((ROWS, width), at_rows),
            pl.BlockSpec((main, width // QUART), lambda i: (0, QUART)),
            pl.BlockSpec((ROWS, units), lambda i: (jnp.minimum(i, blocks - 1), 0)),
            pl.BlockSpec(memory_space=pltpu.VMEM),
            pl.BlockSpec(memory_space=pltpu.VMEM),
            pl.BlockSpec((main, block), at_cols),
            pl.BlockSpec((total - main, block), at_cols),
        ],
        out_specs=[
            pl.BlockSpec((block, units), at_out),
            pl.BlockSpec((block, units), at_out),
            pl.BlockSpec((units, block), at_cols),
        ],
        out_shape=[
            jax.ShapeDtypeStruct((width, units), BF),
            jax.ShapeDtypeStruct((width, units), BF),
            jax.ShapeDtypeStruct((units, width), BF),
        ],
        scratch_shapes=[
            pltpu.VMEM((total, width), BF),
            pltpu.VMEM((units, total), BF),
            pltpu.VMEM((total, 2 * units), BF),
        ],
        compiler_params=params(44),
    )(moe, moe, back, held(gate), held(up), cot, scaled_tail)


def shift(array, axis, by):
    size = lax.axis_size(axis)
    return lax.ppermute(array, axis, [(i, (i + by) % size) for i in range(size)])


def exchange(array, axes):
    return lax.all_to_all(array, axes, split_axis=0, concat_axis=0, tiled=True)


def on_device(
    queries, key_heads, value_heads, out_gain, out_weight, residual, norm_gain,
    routes, route_weights, cotangent, w_gate, w_up, w_down,
):
    n_ctx = lax.axis_size("ctx")
    width = residual.shape[1]
    at = lax.axis_index("ctx").astype(jnp.int32).reshape(1)
    n_x, n_z = lax.axis_size("x"), lax.axis_size("z")
    n_core = lax.axis_size("core")
    near = jnp.array(NEAR, jnp.int32)
    at_x = (lax.axis_index("x") + near) % n_x
    at_z = (lax.axis_index("z") + near) % n_z
    core = lax.axis_index("core")
    sources = at_x[None, :] * n_core + jnp.stack([core, 1 - core])[:, None]
    place = jnp.concatenate([at_z, sources.reshape(-1)]).astype(jnp.int32)

    half = width // 2
    left, right = shift(out_weight, "x", 1), shift(out_weight, "x", -1)
    far = [shift(left[:, :half], "x", 1), shift(right[:, half:], "x", -1)]
    pieces = [out_weight, left, right, jnp.concatenate(far, axis=1)]
    pieces += [shift(piece, "core", 1) for piece in pieces]
    states = span_states(key_heads, value_heads, n_ctx)
    states = exchange(states, "ctx")
    attention = attend(
        at, queries, key_heads, value_heads, states, out_gain[None], n_x, n_core
    )
    heads = exchange(attention, ("x", "core"))
    routes_t = routes.T
    cot = pack_cot(routes_t, route_weights.T, cotangent)
    cot, heads = lax.optimization_barrier((cot, heads))
    cot = exchange(cot.reshape(EXPERTS, MAIN, -1), ALL)

    mine, squares, *partial = project(place, heads, pieces)
    arrived = [shift(part, "z", d) for part, d in zip(partial, NEAR[1:])]
    hidden_out, moe = norm_pack(
        mine, squares, arrived, residual, norm_gain[None], routes_t
    )
    moe = exchange(moe.reshape(EXPERTS, MAIN, -1), ALL)

    moe = moe.reshape(EXPERTS * MAIN, -1)
    cot = cot.reshape(EXPERTS * MAIN, -1)
    back, scaled_tail = hidden_grad(cot, w_down[0])
    grads = expert_grads(moe, cot, scaled_tail, back, w_gate[0], w_up[0])
    return (hidden_out,) + tuple(g[None] for g in grads)


def solution(mesh):
    n_ctx, n_head = mesh.devices.shape
    side = 4
    fine = Mesh(mesh.devices.reshape(n_ctx, side, n_head // (2 * side), 2), ALL)
    head = CHIP + ("core",)
    in_specs = (
        P("ctx", head), P("ctx", head), P("ctx", head), P(head), P(head, None),
        P(ALL, None), P(), P(ALL, None), P(ALL, None), P(ALL, None),
        P(ALL, None, None), P(ALL, None, None), P(ALL, None, None),
    )
    out_specs = (P(ALL, None), P(ALL, None, None), P(ALL, None, None), P(ALL, None, None))

    return jax.shard_map(
        on_device, mesh=fine, in_specs=in_specs, out_specs=out_specs, check_vma=False
    )
```

```python
import jax
import jax.numpy as jnp
from jax import lax
from jax.experimental import pallas as pl
from jax.experimental.pallas import tpu as pltpu
from jax.sharding import Mesh, PartitionSpec as P


HD = 128
HEADS = 32
EXPERTS = 128
TOPK = 8
MAIN = 8
TAIL = 2
QUART = 4
EPS = 1e-06
BF = jnp.bfloat16
F32 = jnp.float32
CHIP = ("x", "z")
ALL = ("ctx",) + CHIP + ("core",)
NEAR = (0, -1, 1, 2)


def phi(values):
    wide = values.astype(F32)
    return jnp.where(wide > 0, wide + 1.0, jnp.exp(jnp.minimum(wide, 0.0))).astype(BF)


def dot(a, b, ca=1, cb=0):
    return lax.dot_general(a, b, (((ca,), (cb,)), ((), ())), preferred_element_type=F32)


def params(limit=28):
    return pltpu.CompilerParams(vmem_limit_bytes=limit * 1024 * 1024)


def state_kernel(k_ref, v_ref, o_ref, acc):
    i = pl.program_id(0)

    @pl.when(i == 0)
    def _():
        acc[...] = jnp.zeros_like(acc)

    kf = phi(k_ref[...])
    v = v_ref[...]
    acc[...] += dot(kf, jnp.concatenate([v, jnp.ones_like(v)], axis=1), 0, 0)

    @pl.when(i == pl.num_programs(0) - 1)
    def _():
        for c in range(o_ref.shape[0]):
            o_ref[c] = acc[...].astype(BF)


def span_states(keys, values, n_ctx):
    length = keys.shape[0]
    block = min(1024, length)
    return pl.pallas_call(
        state_kernel,
        grid=(length // block,),
        in_specs=[pl.BlockSpec((block, HD), lambda i: (i, 0))] * 2,
        out_specs=pl.BlockSpec((n_ctx, HD, 2 * HD), lambda i: (0, 0, 0)),
        out_shape=jax.ShapeDtypeStruct((n_ctx, HD, 2 * HD), BF),
        scratch_shapes=[pltpu.VMEM((HD, 2 * HD), F32)],
        compiler_params=params(56),
    )(keys, values)


CHUNK = 256
EXTRA = 16


def attend_kernel(at_ref, q_ref, k_ref, v_ref, s_ref, g_ref, o_ref, state):
    @pl.when(pl.program_id(0) == 0)
    def _():
        total = jnp.zeros(state.shape, F32)
        for c in range(s_ref.shape[0]):
            total = total + jnp.where(c < at_ref[0], s_ref[c].astype(F32), 0.0)
        state[...] = total

    rows = lax.broadcasted_iota(jnp.int32, (CHUNK, CHUNK), 0)
    cols = lax.broadcasted_iota(jnp.int32, (CHUNK, CHUNK), 1)
    run = state[...]
    cores, rows_out, _ = o_ref.shape
    own = CHUNK // cores
    for c in range(cores):
        o_ref[c, rows_out - EXTRA :, :] = jnp.broadcast_to(g_ref[...], (EXTRA, HD))
    for n in range(q_ref.shape[0] // CHUNK):
        part = pl.ds(n * CHUNK, CHUNK)
        qf = phi(q_ref[part, :])
        kf = phi(k_ref[part, :])
        v = v_ref[part, :]
        v1 = jnp.concatenate([v, jnp.ones_like(v)], axis=1)
        scores = jnp.where(rows >= cols, dot(qf, kf, 1, 1), 0.0).astype(BF)
        both = dot(scores, v1) + dot(qf, run.astype(BF))
        result = (both[:, :HD] / both[:, HD:]).astype(BF)
        for c in range(cores):
            o_ref[c, n * own : (n + 1) * own, :] = result[c * own : (c + 1) * own]
        run = run + dot(kf, v1, 0, 0)
    state[...] = run


def attend(at, queries, keys, values, states, gain, groups, cores):
    length = queries.shape[0]
    block = length // groups
    rows = block // cores + EXTRA
    tok = pl.BlockSpec((block, HD), lambda i, at: (i, 0))
    return pl.pallas_call(
        attend_kernel,
        grid_spec=pltpu.PrefetchScalarGridSpec(
            num_scalar_prefetch=1,
            grid=(groups,),
            in_specs=[tok, tok, tok, whole(states), whole(gain)],
            out_specs=pl.BlockSpec((cores, rows, HD), lambda i, at: (i, 0, 0)),
            scratch_shapes=[pltpu.VMEM((HD, 2 * HD), F32)],
        ),
        out_shape=jax.ShapeDtypeStruct((groups * cores, rows, HD), BF),
        compiler_params=params(),
    )(at, queries, keys, values, states, gain)


def ranks(routes_t, expand):
    tokens = routes_t.shape[1]
    experts = lax.broadcasted_iota(jnp.int32, (EXPERTS, tokens), 0)
    named = jnp.zeros((EXPERTS, tokens), F32)
    for k in range(TOPK):
        named = named + jnp.where(routes_t[k : k + 1, :] == experts, 1.0, 0.0)
    earlier = lax.broadcasted_iota(jnp.int32, (tokens, tokens), 0)
    later = lax.broadcasted_iota(jnp.int32, (tokens, tokens), 1)
    before = jnp.where(earlier < later, 1.0, 0.0).astype(BF)
    rank = jnp.where(named > 0.0, dot(named.astype(BF), before), -1.0)
    return dot(expand, rank.astype(BF))


def expander():
    row = lax.broadcasted_iota(jnp.int32, (EXPERTS * MAIN, EXPERTS), 0) // MAIN
    col = lax.broadcasted_iota(jnp.int32, (EXPERTS * MAIN, EXPERTS), 1)
    return jnp.where(row == col, 1.0, 0.0).astype(BF)


def picks(rank8):
    row = lax.broadcasted_iota(jnp.int32, rank8.shape, 0)
    main = rank8 == (row % MAIN).astype(F32)
    tail = rank8 == (MAIN + row % TAIL).astype(F32)
    return main, tail, (row % MAIN) // TAIL


def tail_rows(tail, quarter, table):
    width = table.shape[1] // QUART
    total = None
    for q in range(QUART):
        pick = jnp.where(tail & (quarter == q), 1.0, 0.0).astype(BF)
        piece = dot(pick, table[:, q * width : (q + 1) * width])
        total = piece if total is None else total + piece
    return total


BLOCKS = 4


def pack_cot_kernel(routes_ref, weights_ref, cot_ref, out_ref, rank_s, weight_s):
    step = pl.program_id(0)

    @pl.when(step == 0)
    def _():
        expand = expander()
        routes_t = routes_ref[...]
        rank_s[...] = ranks(routes_t, expand)
        experts = lax.broadcasted_iota(jnp.int32, (EXPERTS, routes_t.shape[1]), 0)
        weight = jnp.zeros(experts.shape, F32)
        for k in range(TOPK):
            weight = weight + jnp.where(
                routes_t[k : k + 1, :] == experts, weights_ref[k : k + 1, :], 0.0
            )
        total = jnp.zeros(rank_s.shape, F32)
        for _ in range(3):
            piece = weight.astype(BF)
            total = total + dot(expand, piece)
            weight = weight - piece.astype(F32)
        weight_s[...] = total

    size = EXPERTS * MAIN // BLOCKS
    part = pl.ds(step * size, size)
    weight8 = weight_s[part, :]
    main, tail, quarter = picks(rank_s[part, :])
    table = cot_ref[...]
    scale = jnp.sum(jnp.where(main, weight8, 0.0), axis=1, keepdims=True)
    width = table.shape[1]
    out_ref[:, :width] = (dot(jnp.where(main, 1.0, 0.0).astype(BF), table) * scale).astype(BF)
    scale = jnp.sum(jnp.where(tail, weight8, 0.0), axis=1, keepdims=True)
    out_ref[:, width:] = (tail_rows(tail, quarter, table) * scale).astype(BF)


def packed(width):
    rows = EXPERTS * MAIN
    wide = width + width // QUART
    spec = pl.BlockSpec((rows // BLOCKS, wide), lambda i: (i, 0))
    return spec, pltpu.HBM((rows, wide), BF)


def whole(array):
    return pl.BlockSpec(array.shape, lambda *_: (0,) * array.ndim)


def pack_cot(routes_t, weights_t, cotangent):
    tokens, width = cotangent.shape
    spec, shape = packed(width)
    return pl.pallas_call(
        pack_cot_kernel,
        grid=(BLOCKS,),
        in_specs=[whole(routes_t), whole(weights_t), whole(cotangent)],
        out_specs=spec,
        out_shape=shape,
        scratch_shapes=[pltpu.VMEM((EXPERTS * MAIN, tokens), F32)] * 2,
        compiler_params=params(),
    )(routes_t, weights_t, cotangent)


def project_kernel(place_ref, x_ref, *refs):
    pieces, (mine_ref, ss_ref, *out_refs), keep = refs[:8], refs[8:-1], refs[-1]
    tokens, total = mine_ref.shape
    for d in range(4):
        at = pl.multiple_of(place_ref[d] * tokens, tokens)
        rows = slice(d * tokens, (d + 1) * tokens)
        square = jnp.zeros((tokens, HD), F32)
        for s in range(8):
            source = place_ref[4 + s]
            wide = x_ref[source, pl.ds(at, tokens), :].astype(F32)
            gain = x_ref[source, pl.ds(4 * tokens, 8), :].astype(F32)[:1]
            square = square + wide * wide
            keep[rows, s * HD : (s + 1) * HD] = (wide * gain).astype(BF)
        summed = jnp.broadcast_to(jnp.sum(square, axis=1, keepdims=True), (tokens, HD))
        if d == 0:
            ss_ref[...] = summed
        else:
            high = summed.astype(BF)
            out_refs[d - 1][:, total : total + HD] = high
            out_refs[d - 1][:, total + HD :] = (summed - high.astype(F32)).astype(BF)

    side = 512
    for n in range(total // side):
        cols = slice(n * side, (n + 1) * side)
        both = jnp.zeros((4 * tokens, side), F32)
        for s in range(8):
            both = both + dot(keep[:, s * HD : (s + 1) * HD], pieces[s][:, cols])
        mine_ref[:, cols] = both[:tokens]
        for d in range(1, 4):
            out_refs[d - 1][:, cols] = both[d * tokens : (d + 1) * tokens].astype(BF)


def project(place, x, pieces):
    tokens = (x.shape[1] - EXTRA) // 4
    width = pieces[0].shape[1]
    args = (x,) + tuple(pieces)
    shapes = [(width, F32), (HD, F32)] + [(width + 2 * HD, BF)] * 3
    return pl.pallas_call(
        project_kernel,
        grid_spec=pltpu.PrefetchScalarGridSpec(
            num_scalar_prefetch=1,
            grid=(1,),
            in_specs=[whole(a) for a in args],
            out_specs=[pl.BlockSpec((tokens, n), lambda i, c: (0, 0)) for n, _ in shapes],
            scratch_shapes=[pltpu.VMEM((4 * tokens, 8 * HD), BF)],
        ),
        out_shape=[jax.ShapeDtypeStruct((tokens, n), kind) for n, kind in shapes],
        compiler_params=params(),
    )(place, *args)


def norm_pack_kernel(
    mine_ref, ss_ref, got_a, got_b, got_c, residual_ref, gain_ref, routes_ref,
    hidden_ref, out_ref, rank_s, table_s,
):
    step = pl.program_id(0)

    @pl.when(step == 0)
    def _():
        width = mine_ref.shape[1]
        squares = ss_ref[...]
        projected = mine_ref[...]
        for got in (got_a, got_b, got_c):
            squares = squares + got[:, width : width + HD].astype(F32)
            squares = squares + got[:, width + HD :].astype(F32)
            projected = projected + got[:, :width].astype(F32)
        inverse = lax.rsqrt(squares[:, :1] / (HEADS * HD) + EPS)
        projected = projected * inverse
        hidden = (residual_ref[...].astype(F32) + projected).astype(BF)
        hidden_ref[...] = hidden
        wide = hidden.astype(F32)
        scale = lax.rsqrt(jnp.mean(wide * wide, axis=1, keepdims=True) + EPS)
        table_s[...] = (wide * scale * gain_ref[...].astype(F32)).astype(BF)
        rank_s[...] = ranks(routes_ref[...], expander())

    size = EXPERTS * MAIN // BLOCKS
    main, tail, quarter = picks(rank_s[pl.ds(step * size, size), :])
    table = table_s[...]
    width = table.shape[1]
    out_ref[:, :width] = dot(jnp.where(main, 1.0, 0.0).astype(BF), table).astype(BF)
    out_ref[:, width:] = tail_rows(tail, quarter, table).astype(BF)


def norm_pack(mine, squares, arrived, residual, gain, routes_t):
    tokens, width = residual.shape
    spec, shape = packed(width)
    args = (mine, squares) + tuple(arrived) + (residual, gain, routes_t)
    return pl.pallas_call(
        norm_pack_kernel,
        grid=(BLOCKS,),
        in_specs=[whole(a) for a in args],
        out_specs=[pl.BlockSpec((tokens, width), lambda i: (0, 0)), spec],
        out_shape=[jax.ShapeDtypeStruct((tokens, width), BF), shape],
        scratch_shapes=[
            pltpu.VMEM((EXPERTS * MAIN, tokens), F32),
            pltpu.VMEM((tokens, width), BF),
        ],
        compiler_params=params(),
    )(*args)


ROWS = 256


def untail(tail, keep):
    sources = tail.shape[0] // MAIN
    to = lax.broadcasted_iota(jnp.int32, (sources * TAIL, tail.shape[0]), 0)
    of = lax.broadcasted_iota(jnp.int32, (sources * TAIL, tail.shape[0]), 1)
    width = tail.shape[1]
    for q in range(QUART):
        pick = of == to // TAIL * MAIN + q * TAIL + to % TAIL
        piece = dot(jnp.where(pick, 1.0, 0.0).astype(BF), tail)
        keep(slice(q * width, (q + 1) * width), piece.astype(BF))


def hidden_kernel(rows_ref, tail_ref, down_ref, out_ref, scaled_ref):
    step = pl.program_id(0)
    last = pl.num_programs(0) - 1

    @pl.when(step < last)
    def _():
        out_ref[...] = dot(rows_ref[...], down_ref[...], 1, 1)

    @pl.when(step == last)
    def _():
        def keep(cols, piece):
            scaled_ref[:, cols] = piece

        untail(tail_ref[...], keep)
        out_ref[...] = dot(scaled_ref[...], down_ref[...], 1, 1)


def hidden_grad(cot, down):
    rows = cot.shape[0]
    units, width = down.shape
    blocks = rows // ROWS
    tails = rows // MAIN * TAIL
    return pl.pallas_call(
        hidden_kernel,
        grid=(blocks + 1,),
        in_specs=[
            pl.BlockSpec((ROWS, width), lambda i: (jnp.minimum(i, blocks - 1), 0)),
            pl.BlockSpec((rows, width // QUART), lambda i: (0, QUART)),
            whole(down),
        ],
        out_specs=[
            pl.BlockSpec((ROWS, units), lambda i: (i, 0)),
            pl.BlockSpec((tails, width), lambda i: (0, 0)),
        ],
        out_shape=[
            pltpu.HBM((rows + tails, units), F32),
            pltpu.HBM((tails, width), BF),
        ],
        compiler_params=params(),
    )(cot, cot, down)


def grads_kernel(
    x_ref, tail_ref, back_ref, gate_ref, up_ref, scaled_ref, scaled_tail_ref,
    grad_gate_ref, grad_up_ref, grad_down_ref, x_s, hidden_s, pre_s,
):
    step = pl.program_id(0)
    total, _ = x_s.shape
    units = gate_ref.shape[1]
    blocks = total // ROWS
    part = pl.ds(pl.multiple_of(step * ROWS, ROWS), ROWS)

    @pl.when(step < blocks - 1)
    def _():
        x_s[part, :] = x_ref[...]

    @pl.when(step == blocks - 1)
    def _():
        def keep(cols, piece):
            x_s[total - ROWS :, cols] = piece

        untail(tail_ref[...], keep)

    @pl.when(step < blocks)
    def _():
        x = x_s[part, :]
        piece = 256
        for c in range(units // piece):
            cols = slice(c * piece, (c + 1) * piece)
            gate = dot(x, gate_ref[:, cols])
            up = dot(x, up_ref[:, cols])
            back = back_ref[:, cols]
            sig = jax.nn.sigmoid(gate)
            active = gate * sig
            hidden_s[cols, part] = jnp.transpose(active * up).astype(BF)
            slope = sig * (1.0 + gate * (1.0 - sig))
            pre_s[part, cols] = (back * up * slope).astype(BF)
            pre_s[part, units + c * piece : units + (c + 1) * piece] = (back * active).astype(BF)

    @pl.when(step >= blocks)
    def _():
        block = grad_gate_ref.shape[0]
        x = x_s[:, pl.ds(pl.multiple_of((step - blocks) * block, block), block)]
        both = dot(x, pre_s[...], 0, 0)
        grad_gate_ref[...] = both[:, :units].astype(BF)
        grad_up_ref[...] = both[:, units:].astype(BF)
        main = scaled_ref.shape[0]
        down = dot(hidden_s[:, :main], scaled_ref[...])
        down = down + dot(hidden_s[:, main:], scaled_tail_ref[...])
        grad_down_ref[...] = down.astype(BF)


def held(array, space=pltpu.VMEM):
    return pltpu.with_memory_space_constraint(array, space)


def expert_grads(moe, cot, scaled_tail, back, gate, up):
    main = moe.shape[0]
    width, units = gate.shape
    total = back.shape[0]
    blocks = total // ROWS
    block = 512
    at_rows = lambda i: (jnp.minimum(i, blocks - 2), 0)
    at_cols = lambda i: (0, jnp.maximum(i - blocks, 0))
    at_out = lambda i: (jnp.maximum(i - blocks, 0), 0)
    return pl.pallas_call(
        grads_kernel,
        grid=(blocks + width // block,),
        in_specs=[
            pl.BlockSpec((ROWS, width), at_rows),
            pl.BlockSpec((main, width // QUART), lambda i: (0, QUART)),
            pl.BlockSpec((ROWS, units), lambda i: (jnp.minimum(i, blocks - 1), 0)),
            pl.BlockSpec(memory_space=pltpu.VMEM),
            whole(up),
            pl.BlockSpec((main, block), at_cols),
            pl.BlockSpec((total - main, block), at_cols),
        ],
        out_specs=[
            pl.BlockSpec((block, units), at_out),
            pl.BlockSpec((block, units), at_out),
            pl.BlockSpec((units, block), at_cols),
        ],
        out_shape=[
            jax.ShapeDtypeStruct((width, units), BF),
            jax.ShapeDtypeStruct((width, units), BF),
            jax.ShapeDtypeStruct((units, width), BF),
        ],
        scratch_shapes=[
            pltpu.VMEM((total, width), BF),
            pltpu.VMEM((units, total), BF),
            pltpu.VMEM((total, 2 * units), BF),
        ],
        compiler_params=params(44),
    )(moe, moe, held(back, pltpu.HBM), gate, up, cot, held(scaled_tail, pltpu.HBM))


def shift(array, axis, by):
    size = lax.axis_size(axis)
    return lax.ppermute(array, axis, [(i, (i + by) % size) for i in range(size)])


def exchange(array, axes):
    return lax.all_to_all(array, axes, split_axis=0, concat_axis=0, tiled=True)


def on_device(
    queries, key_heads, value_heads, out_gain, out_weight, residual, norm_gain,
    routes, route_weights, cotangent, w_gate, w_up, w_down,
):
    n_ctx = lax.axis_size("ctx")
    width = residual.shape[1]
    at = lax.axis_index("ctx").astype(jnp.int32).reshape(1)
    n_x, n_z = lax.axis_size("x"), lax.axis_size("z")
    n_core = lax.axis_size("core")
    near = jnp.array(NEAR, jnp.int32)
    at_x = (lax.axis_index("x") + near) % n_x
    at_z = (lax.axis_index("z") + near) % n_z
    core = lax.axis_index("core")
    sources = at_x[None, :] * n_core + jnp.stack([core, 1 - core])[:, None]
    place = jnp.concatenate([at_z, sources.reshape(-1)]).astype(jnp.int32)

    half = width // 2
    left, right = shift(out_weight, "x", 1), shift(out_weight, "x", -1)
    far = [shift(left[:, :half], "x", 1), shift(right[:, half:], "x", -1)]
    pieces = [out_weight, left, right, jnp.concatenate(far, axis=1)]
    pieces += [shift(piece, "core", 1) for piece in pieces]
    states = span_states(key_heads, value_heads, n_ctx)
    states = exchange(states, "ctx")
    attention = attend(
        at, queries, key_heads, value_heads, states, out_gain[None], n_x, n_core
    )
    heads = exchange(attention, ("x", "core"))
    routes_t = routes.T
    cot = pack_cot(routes_t, route_weights.T, cotangent)
    cot, heads = lax.optimization_barrier((cot, heads))
    cot = exchange(cot.reshape(EXPERTS, MAIN, -1), ALL)

    mine, squares, *partial = project(place, heads, pieces)
    arrived = [shift(part, "z", d) for part, d in zip(partial, NEAR[1:])]
    hidden_out, moe = norm_pack(
        mine, squares, arrived, residual, norm_gain[None], routes_t
    )
    moe = exchange(moe.reshape(EXPERTS, MAIN, -1), ALL)

    moe = moe.reshape(EXPERTS * MAIN, -1)
    cot = cot.reshape(EXPERTS * MAIN, -1)
    gate, up = held(w_gate[0]), held(w_up[0], pltpu.HBM)
    back, scaled_tail = hidden_grad(cot, w_down[0])
    grads = expert_grads(moe, cot, scaled_tail, back, gate, up)
    return (hidden_out,) + tuple(g[None] for g in grads)


def solution(mesh):
    n_ctx, n_head = mesh.devices.shape
    side = 4
    fine = Mesh(mesh.devices.reshape(n_ctx, side, n_head // (2 * side), 2), ALL)
    head = CHIP + ("core",)
    in_specs = (
        P("ctx", head), P("ctx", head), P("ctx", head), P(head), P(head, None),
        P(ALL, None), P(), P(ALL, None), P(ALL, None), P(ALL, None),
        P(ALL, None, None), P(ALL, None, None), P(ALL, None, None),
    )
    out_specs = (P(ALL, None), P(ALL, None, None), P(ALL, None, None), P(ALL, None, None))

    return jax.shard_map(
        on_device, mesh=fine, in_specs=in_specs, out_specs=out_specs, check_vma=False
    )
```

```python
import jax
import jax.numpy as jnp
from jax import lax
from jax.experimental import pallas as pl
from jax.experimental.pallas import tpu as pltpu
from jax.sharding import Mesh, PartitionSpec as P


HD = 128
HEADS = 32
EXPERTS = 128
TOPK = 8
MAIN = 8
TAIL = 2
QUART = 4
EPS = 1e-06
BF = jnp.bfloat16
F32 = jnp.float32
CHIP = ("x", "z")
ALL = ("ctx",) + CHIP + ("core",)
NEAR = (0, -1, 1, 2)


def phi(values):
    wide = values.astype(F32)
    return jnp.where(wide > 0, wide + 1.0, jnp.exp(jnp.minimum(wide, 0.0))).astype(BF)


def dot(a, b, ca=1, cb=0):
    return lax.dot_general(a, b, (((ca,), (cb,)), ((), ())), preferred_element_type=F32)


def params(limit=28):
    return pltpu.CompilerParams(vmem_limit_bytes=limit * 1024 * 1024)


def state_kernel(k_ref, v_ref, o_ref, acc):
    i = pl.program_id(0)

    @pl.when(i == 0)
    def _():
        acc[...] = jnp.zeros_like(acc)

    kf = phi(k_ref[...])
    v = v_ref[...]
    acc[...] += dot(kf, jnp.concatenate([v, jnp.ones_like(v)], axis=1), 0, 0)

    @pl.when(i == pl.num_programs(0) - 1)
    def _():
        for c in range(o_ref.shape[0]):
            o_ref[c] = acc[...].astype(BF)


def span_states(keys, values, n_ctx):
    length = keys.shape[0]
    block = min(1024, length)
    return pl.pallas_call(
        state_kernel,
        grid=(length // block,),
        in_specs=[pl.BlockSpec((block, HD), lambda i: (i, 0))] * 2,
        out_specs=pl.BlockSpec((n_ctx, HD, 2 * HD), lambda i: (0, 0, 0)),
        out_shape=jax.ShapeDtypeStruct((n_ctx, HD, 2 * HD), BF),
        scratch_shapes=[pltpu.VMEM((HD, 2 * HD), F32)],
        compiler_params=params(56),
    )(keys, values)


CHUNK = 256
EXTRA = 16


def attend_kernel(at_ref, q_ref, k_ref, v_ref, s_ref, g_ref, o_ref, state):
    @pl.when(pl.program_id(0) == 0)
    def _():
        total = jnp.zeros(state.shape, F32)
        for c in range(s_ref.shape[0]):
            total = total + jnp.where(c < at_ref[0], s_ref[c].astype(F32), 0.0)
        state[...] = total

    rows = lax.broadcasted_iota(jnp.int32, (CHUNK, CHUNK), 0)
    cols = lax.broadcasted_iota(jnp.int32, (CHUNK, CHUNK), 1)
    run = state[...]
    cores, rows_out, _ = o_ref.shape
    own = CHUNK // cores
    for c in range(cores):
        o_ref[c, rows_out - EXTRA :, :] = jnp.broadcast_to(g_ref[...], (EXTRA, HD))
    for n in range(q_ref.shape[0] // CHUNK):
        part = pl.ds(n * CHUNK, CHUNK)
        qf = phi(q_ref[part, :])
        kf = phi(k_ref[part, :])
        v = v_ref[part, :]
        v1 = jnp.concatenate([v, jnp.ones_like(v)], axis=1)
        scores = jnp.where(rows >= cols, dot(qf, kf, 1, 1), 0.0).astype(BF)
        both = dot(scores, v1) + dot(qf, run.astype(BF))
        result = (both[:, :HD] / both[:, HD:]).astype(BF)
        for c in range(cores):
            o_ref[c, n * own : (n + 1) * own, :] = result[c * own : (c + 1) * own]
        run = run + dot(kf, v1, 0, 0)
    state[...] = run


def attend(at, queries, keys, values, states, gain, groups, cores):
    length = queries.shape[0]
    block = length // groups
    rows = block // cores + EXTRA
    tok = pl.BlockSpec((block, HD), lambda i, at: (i, 0))
    return pl.pallas_call(
        attend_kernel,
        grid_spec=pltpu.PrefetchScalarGridSpec(
            num_scalar_prefetch=1,
            grid=(groups,),
            in_specs=[tok, tok, tok, whole(states), whole(gain)],
            out_specs=pl.BlockSpec((cores, rows, HD), lambda i, at: (i, 0, 0)),
            scratch_shapes=[pltpu.VMEM((HD, 2 * HD), F32)],
        ),
        out_shape=jax.ShapeDtypeStruct((groups * cores, rows, HD), BF),
        compiler_params=params(),
    )(at, queries, keys, values, states, gain)


def ranks(routes_t, expand):
    tokens = routes_t.shape[1]
    experts = lax.broadcasted_iota(jnp.int32, (EXPERTS, tokens), 0)
    named = jnp.zeros((EXPERTS, tokens), F32)
    for k in range(TOPK):
        named = named + jnp.where(routes_t[k : k + 1, :] == experts, 1.0, 0.0)
    earlier = lax.broadcasted_iota(jnp.int32, (tokens, tokens), 0)
    later = lax.broadcasted_iota(jnp.int32, (tokens, tokens), 1)
    before = jnp.where(earlier < later, 1.0, 0.0).astype(BF)
    rank = jnp.where(named > 0.0, dot(named.astype(BF), before), -1.0)
    return dot(expand, rank.astype(BF))


def expander():
    row = lax.broadcasted_iota(jnp.int32, (EXPERTS * MAIN, EXPERTS), 0) // MAIN
    col = lax.broadcasted_iota(jnp.int32, (EXPERTS * MAIN, EXPERTS), 1)
    return jnp.where(row == col, 1.0, 0.0).astype(BF)


def picks(rank8):
    row = lax.broadcasted_iota(jnp.int32, rank8.shape, 0)
    main = rank8 == (row % MAIN).astype(F32)
    tail = rank8 == (MAIN + row % TAIL).astype(F32)
    return main, tail, (row % MAIN) // TAIL


def tail_rows(tail, quarter, table):
    width = table.shape[1] // QUART
    total = None
    for q in range(QUART):
        pick = jnp.where(tail & (quarter == q), 1.0, 0.0).astype(BF)
        piece = dot(pick, table[:, q * width : (q + 1) * width])
        total = piece if total is None else total + piece
    return total


BLOCKS = 4


def pack_cot_kernel(routes_ref, weights_ref, cot_ref, out_ref, rank_s, weight_s):
    step = pl.program_id(0)

    @pl.when(step == 0)
    def _():
        expand = expander()
        routes_t = routes_ref[...]
        rank_s[...] = ranks(routes_t, expand)
        experts = lax.broadcasted_iota(jnp.int32, (EXPERTS, routes_t.shape[1]), 0)
        weight = jnp.zeros(experts.shape, F32)
        for k in range(TOPK):
            weight = weight + jnp.where(
                routes_t[k : k + 1, :] == experts, weights_ref[k : k + 1, :], 0.0
            )
        total = jnp.zeros(rank_s.shape, F32)
        for _ in range(3):
            piece = weight.astype(BF)
            total = total + dot(expand, piece)
            weight = weight - piece.astype(F32)
        weight_s[...] = total

    size = EXPERTS * MAIN // BLOCKS
    part = pl.ds(step * size, size)
    weight8 = weight_s[part, :]
    main, tail, quarter = picks(rank_s[part, :])
    table = cot_ref[...]
    scale = jnp.sum(jnp.where(main, weight8, 0.0), axis=1, keepdims=True)
    width = table.shape[1]
    out_ref[:, :width] = (dot(jnp.where(main, 1.0, 0.0).astype(BF), table) * scale).astype(BF)
    scale = jnp.sum(jnp.where(tail, weight8, 0.0), axis=1, keepdims=True)
    out_ref[:, width:] = (tail_rows(tail, quarter, table) * scale).astype(BF)


def packed(width):
    rows = EXPERTS * MAIN
    wide = width + width // QUART
    spec = pl.BlockSpec((rows // BLOCKS, wide), lambda i: (i, 0))
    return spec, pltpu.HBM((rows, wide), BF)


def whole(array):
    return pl.BlockSpec(array.shape, lambda *_: (0,) * array.ndim)


def pack_cot(routes_t, weights_t, cotangent):
    tokens, width = cotangent.shape
    spec, shape = packed(width)
    return pl.pallas_call(
        pack_cot_kernel,
        grid=(BLOCKS,),
        in_specs=[whole(routes_t), whole(weights_t), whole(cotangent)],
        out_specs=spec,
        out_shape=shape,
        scratch_shapes=[pltpu.VMEM((EXPERTS * MAIN, tokens), F32)] * 2,
        compiler_params=params(),
    )(routes_t, weights_t, cotangent)


def project_kernel(place_ref, x_ref, *refs):
    pieces, (mine_ref, ss_ref, *out_refs), keep = refs[:8], refs[8:-1], refs[-1]
    tokens, total = mine_ref.shape
    for d in range(4):
        at = pl.multiple_of(place_ref[d] * tokens, tokens)
        rows = slice(d * tokens, (d + 1) * tokens)
        square = jnp.zeros((tokens, HD), F32)
        for s in range(8):
            source = place_ref[4 + s]
            wide = x_ref[source, pl.ds(at, tokens), :].astype(F32)
            gain = x_ref[source, pl.ds(4 * tokens, 8), :].astype(F32)[:1]
            square = square + wide * wide
            keep[rows, s * HD : (s + 1) * HD] = (wide * gain).astype(BF)
        summed = jnp.broadcast_to(jnp.sum(square, axis=1, keepdims=True), (tokens, HD))
        if d == 0:
            ss_ref[...] = summed
        else:
            high = summed.astype(BF).astype(F32)
            lane = lax.broadcasted_iota(jnp.int32, high.shape, 1)
            both = jnp.where(lane < HD // 2, high, summed - high)
            out_refs[d - 1][:, total:] = both.astype(BF)

    side = 512
    for n in range(total // side):
        cols = slice(n * side, (n + 1) * side)
        both = jnp.zeros((4 * tokens, side), F32)
        for s in range(8):
            both = both + dot(keep[:, s * HD : (s + 1) * HD], pieces[s][:, cols])
        mine_ref[:, cols] = both[:tokens]
        for d in range(1, 4):
            out_refs[d - 1][:, cols] = both[d * tokens : (d + 1) * tokens].astype(BF)


def project(place, x, pieces):
    tokens = (x.shape[1] - EXTRA) // 4
    width = pieces[0].shape[1]
    args = (x,) + tuple(pieces)
    shapes = [(width, F32), (HD, F32)] + [(width + HD, BF)] * 3
    return pl.pallas_call(
        project_kernel,
        grid_spec=pltpu.PrefetchScalarGridSpec(
            num_scalar_prefetch=1,
            grid=(1,),
            in_specs=[whole(a) for a in args],
            out_specs=[pl.BlockSpec((tokens, n), lambda i, c: (0, 0)) for n, _ in shapes],
            scratch_shapes=[pltpu.VMEM((4 * tokens, 8 * HD), BF)],
        ),
        out_shape=[jax.ShapeDtypeStruct((tokens, n), kind) for n, kind in shapes],
        compiler_params=params(),
    )(place, *args)


def norm_pack_kernel(
    mine_ref, ss_ref, got_a, got_b, got_c, residual_ref, gain_ref, routes_ref,
    hidden_ref, out_ref, rank_s, table_s,
):
    step = pl.program_id(0)

    @pl.when(step == 0)
    def _():
        width = mine_ref.shape[1]
        squares = ss_ref[:, :1]
        projected = mine_ref[...]
        for got in (got_a, got_b, got_c):
            sent = got[:, width:].astype(F32)
            squares = squares + sent[:, :1] + sent[:, HD // 2 : HD // 2 + 1]
            projected = projected + got[:, :width].astype(F32)
        inverse = lax.rsqrt(squares / (HEADS * HD) + EPS)
        projected = projected * inverse
        hidden = (residual_ref[...].astype(F32) + projected).astype(BF)
        hidden_ref[...] = hidden
        wide = hidden.astype(F32)
        scale = lax.rsqrt(jnp.mean(wide * wide, axis=1, keepdims=True) + EPS)
        table_s[...] = (wide * scale * gain_ref[...].astype(F32)).astype(BF)
        rank_s[...] = ranks(routes_ref[...], expander())

    size = EXPERTS * MAIN // BLOCKS
    main, tail, quarter = picks(rank_s[pl.ds(step * size, size), :])
    table = table_s[...]
    width = table.shape[1]
    out_ref[:, :width] = dot(jnp.where(main, 1.0, 0.0).astype(BF), table).astype(BF)
    out_ref[:, width:] = tail_rows(tail, quarter, table).astype(BF)


def norm_pack(mine, squares, arrived, residual, gain, routes_t):
    tokens, width = residual.shape
    spec, shape = packed(width)
    args = (mine, squares) + tuple(arrived) + (residual, gain, routes_t)
    return pl.pallas_call(
        norm_pack_kernel,
        grid=(BLOCKS,),
        in_specs=[whole(a) for a in args],
        out_specs=[pl.BlockSpec((tokens, width), lambda i: (0, 0)), spec],
        out_shape=[jax.ShapeDtypeStruct((tokens, width), BF), shape],
        scratch_shapes=[
            pltpu.VMEM((EXPERTS * MAIN, tokens), F32),
            pltpu.VMEM((tokens, width), BF),
        ],
        compiler_params=params(),
    )(*args)


ROWS = 256


def untail(tail, keep):
    sources = tail.shape[0] // MAIN
    to = lax.broadcasted_iota(jnp.int32, (sources * TAIL, tail.shape[0]), 0)
    of = lax.broadcasted_iota(jnp.int32, (sources * TAIL, tail.shape[0]), 1)
    width = tail.shape[1]
    for q in range(QUART):
        pick = of == to // TAIL * MAIN + q * TAIL + to % TAIL
        piece = dot(jnp.where(pick, 1.0, 0.0).astype(BF), tail)
        keep(slice(q * width, (q + 1) * width), piece.astype(BF))


def hidden_kernel(rows_ref, tail_ref, down_ref, out_ref, scaled_ref):
    step = pl.program_id(0)
    last = pl.num_programs(0) - 1

    @pl.when(step < last)
    def _():
        out_ref[...] = dot(rows_ref[...], down_ref[...], 1, 1)

    @pl.when(step == last)
    def _():
        def keep(cols, piece):
            scaled_ref[:, cols] = piece

        untail(tail_ref[...], keep)
        out_ref[...] = dot(scaled_ref[...], down_ref[...], 1, 1)


def hidden_grad(cot, down):
    rows = cot.shape[0]
    units, width = down.shape
    blocks = rows // ROWS
    tails = rows // MAIN * TAIL
    return pl.pallas_call(
        hidden_kernel,
        grid=(blocks + 1,),
        in_specs=[
            pl.BlockSpec((ROWS, width), lambda i: (jnp.minimum(i, blocks - 1), 0)),
            pl.BlockSpec((rows, width // QUART), lambda i: (0, QUART)),
            whole(down),
        ],
        out_specs=[
            pl.BlockSpec((ROWS, units), lambda i: (i, 0)),
            pl.BlockSpec((tails, width), lambda i: (0, 0)),
        ],
        out_shape=[
            pltpu.HBM((rows + tails, units), F32),
            pltpu.HBM((tails, width), BF),
        ],
        compiler_params=params(),
    )(cot, cot, down)


def grads_kernel(
    x_ref, tail_ref, back_ref, gate_ref, up_ref, scaled_ref, scaled_tail_ref,
    grad_gate_ref, grad_up_ref, grad_down_ref, x_s, hidden_s, pre_s,
):
    step = pl.program_id(0)
    total, _ = x_s.shape
    units = gate_ref.shape[1]
    blocks = total // ROWS
    part = pl.ds(pl.multiple_of(step * ROWS, ROWS), ROWS)

    @pl.when(step < blocks - 1)
    def _():
        x_s[part, :] = x_ref[...]

    @pl.when(step == blocks - 1)
    def _():
        def keep(cols, piece):
            x_s[total - ROWS :, cols] = piece

        untail(tail_ref[...], keep)

    @pl.when(step < blocks)
    def _():
        x = x_s[part, :]
        piece = 256
        for c in range(units // piece):
            cols = slice(c * piece, (c + 1) * piece)
            gate = dot(x, gate_ref[:, cols])
            up = dot(x, up_ref[:, cols])
            back = back_ref[:, cols]
            sig = jax.nn.sigmoid(gate)
            active = gate * sig
            hidden_s[cols, part] = jnp.transpose(active * up).astype(BF)
            slope = sig * (1.0 + gate * (1.0 - sig))
            pre_s[part, cols] = (back * up * slope).astype(BF)
            pre_s[part, units + c * piece : units + (c + 1) * piece] = (back * active).astype(BF)

    @pl.when(step >= blocks)
    def _():
        block = grad_gate_ref.shape[0]
        x = x_s[:, pl.ds(pl.multiple_of((step - blocks) * block, block), block)]
        both = dot(x, pre_s[...], 0, 0)
        grad_gate_ref[...] = both[:, :units].astype(BF)
        grad_up_ref[...] = both[:, units:].astype(BF)
        main = scaled_ref.shape[0]
        down = dot(hidden_s[:, :main], scaled_ref[...])
        down = down + dot(hidden_s[:, main:], scaled_tail_ref[...])
        grad_down_ref[...] = down.astype(BF)


def held(array, space=pltpu.VMEM):
    return pltpu.with_memory_space_constraint(array, space)


def expert_grads(moe, cot, scaled_tail, back, gate, up):
    main = moe.shape[0]
    width, units = gate.shape
    total = back.shape[0]
    blocks = total // ROWS
    block = 512
    at_rows = lambda i: (jnp.minimum(i, blocks - 2), 0)
    at_cols = lambda i: (0, jnp.maximum(i - blocks, 0))
    at_out = lambda i: (jnp.maximum(i - blocks, 0), 0)
    return pl.pallas_call(
        grads_kernel,
        grid=(blocks + width // block,),
        in_specs=[
            pl.BlockSpec((ROWS, width), at_rows),
            pl.BlockSpec((main, width // QUART), lambda i: (0, QUART)),
            pl.BlockSpec((ROWS, units), lambda i: (jnp.minimum(i, blocks - 1), 0)),
            pl.BlockSpec(memory_space=pltpu.VMEM),
            whole(up),
            pl.BlockSpec((main, block), at_cols),
            pl.BlockSpec((total - main, block), at_cols),
        ],
        out_specs=[
            pl.BlockSpec((block, units), at_out),
            pl.BlockSpec((block, units), at_out),
            pl.BlockSpec((units, block), at_cols),
        ],
        out_shape=[
            jax.ShapeDtypeStruct((width, units), BF),
            jax.ShapeDtypeStruct((width, units), BF),
            jax.ShapeDtypeStruct((units, width), BF),
        ],
        scratch_shapes=[
            pltpu.VMEM((total, width), BF),
            pltpu.VMEM((units, total), BF),
            pltpu.VMEM((total, 2 * units), BF),
        ],
        compiler_params=params(44),
    )(moe, moe, held(back, pltpu.HBM), gate, up, cot, held(scaled_tail, pltpu.HBM))


def shift(array, axis, by):
    size = lax.axis_size(axis)
    return lax.ppermute(array, axis, [(i, (i + by) % size) for i in range(size)])


def exchange(array, axes):
    return lax.all_to_all(array, axes, split_axis=0, concat_axis=0, tiled=True)


def on_device(
    queries, key_heads, value_heads, out_gain, out_weight, residual, norm_gain,
    routes, route_weights, cotangent, w_gate, w_up, w_down,
):
    n_ctx = lax.axis_size("ctx")
    width = residual.shape[1]
    at = lax.axis_index("ctx").astype(jnp.int32).reshape(1)
    n_x, n_z = lax.axis_size("x"), lax.axis_size("z")
    n_core = lax.axis_size("core")
    near = jnp.array(NEAR, jnp.int32)
    at_x = (lax.axis_index("x") + near) % n_x
    at_z = (lax.axis_index("z") + near) % n_z
    core = lax.axis_index("core")
    sources = at_x[None, :] * n_core + jnp.stack([core, 1 - core])[:, None]
    place = jnp.concatenate([at_z, sources.reshape(-1)]).astype(jnp.int32)

    half = width // 2
    left, right = shift(out_weight, "x", 1), shift(out_weight, "x", -1)
    far = [shift(left[:, :half], "x", 1), shift(right[:, half:], "x", -1)]
    pieces = [out_weight, left, right, jnp.concatenate(far, axis=1)]
    pieces += [shift(piece, "core", 1) for piece in pieces]
    states = span_states(key_heads, value_heads, n_ctx)
    states = exchange(states, "ctx")
    attention = attend(
        at, queries, key_heads, value_heads, states, out_gain[None], n_x, n_core
    )
    heads = exchange(attention, ("x", "core"))
    routes_t = routes.T
    cot = pack_cot(routes_t, route_weights.T, cotangent)
    cot, heads = lax.optimization_barrier((cot, heads))
    cot = exchange(cot.reshape(EXPERTS, MAIN, -1), ALL)

    mine, squares, *partial = project(place, heads, pieces)
    arrived = [shift(part, "z", d) for part, d in zip(partial, NEAR[1:])]
    hidden_out, moe = norm_pack(
        mine, squares, arrived, residual, norm_gain[None], routes_t
    )
    moe = exchange(moe.reshape(EXPERTS, MAIN, -1), ALL)

    moe = moe.reshape(EXPERTS * MAIN, -1)
    cot = cot.reshape(EXPERTS * MAIN, -1)
    gate, up = held(w_gate[0]), held(w_up[0], pltpu.HBM)
    back, scaled_tail = hidden_grad(cot, w_down[0])
    grads = expert_grads(moe, cot, scaled_tail, back, gate, up)
    return (hidden_out,) + tuple(g[None] for g in grads)


def solution(mesh):
    n_ctx, n_head = mesh.devices.shape
    side = 4
    fine = Mesh(mesh.devices.reshape(n_ctx, side, n_head // (2 * side), 2), ALL)
    head = CHIP + ("core",)
    in_specs = (
        P("ctx", head), P("ctx", head), P("ctx", head), P(head), P(head, None),
        P(ALL, None), P(), P(ALL, None), P(ALL, None), P(ALL, None),
        P(ALL, None, None), P(ALL, None, None), P(ALL, None, None),
    )
    out_specs = (P(ALL, None), P(ALL, None, None), P(ALL, None, None), P(ALL, None, None))

    return jax.shard_map(
        on_device, mesh=fine, in_specs=in_specs, out_specs=out_specs, check_vma=False
    )
```
